32 devices in a mesh: ctx: 8 (over z, x), tp: 4 (over y, core).
Axes of the slice: x: 2, y: 2, z: 4, core: 2. Of those that a mesh axis runs over, the one named last changes fastest.
Arguments:
- residual: bfloat16 [1024, 4096], P('ctx', 'tp')
- mixer_input: bfloat16 [1024, 4096], P('ctx', 'tp')
- gate_input: bfloat16 [1024, 4096], P('ctx', 'tp'), may hold values from -6 to 6
- state_proj: bfloat16 [1024, 32], P('ctx'), may hold values from -6 to 6
- step_raw: float32 [1024, 64], P('ctx', 'tp'), may hold values from -5 to 5
- conv_weight: float32 [4, 4096], P(None, 'tp'), may hold values from -3 to 3
- conv_state_weight: float32 [4, 32], replicated, may hold values from -3 to 3
- step_bias: float32 [64], P('tp'), may hold values from -3.5 to 0.5
- decay_log: float32 [64], P('tp')
- skip_gain: float32 [64], P('tp'), may hold values from 0.5 to 1.5
- mixer_gain: float32 [4096], P('tp'), may hold values from 0.5 to 1.5
- out_weight: bfloat16 [4096, 4096], P('tp', 'ctx'), may hold values from -0.09375 to 0.09375
- feed_gain: float32 [4096], P('tp'), may hold values from 0.5 to 1.5
- expert_gate: bfloat16 [8, 4096, 7168], P('ctx', 'tp'), may hold values from -0.09375 to 0.09375
- expert_up: bfloat16 [8, 4096, 7168], P('ctx', 'tp'), may hold values from -0.09375 to 0.09375
- expert_down: bfloat16 [8, 7168, 4096], P('ctx', None, 'tp'), may hold values from -0.0625 to 0.0625
- expert_ids: int32 [1024, 2], P('ctx'), may hold values from 0 to 7, all different within a row; in each aligned block of 128 rows (0 to 127, 128 to 255, ...) at most 36 rows name the same one
- expert_weights: float32 [1024, 2], P('ctx'), may hold values from 0.1 to 0.9
Outputs:
- block_out: bfloat16 [1024, 4096], P('ctx', 'tp')
The draws below stay inside these ranges and needn't reach their ends.
Inputs may be any that keep to these rules, and one draw needn't show every extreme that they name: `expert_ids`: in each aligned block of 128 rows no expert is named more than 36 times, and some block reaches 36; the two experts of a row differ.
All inputs are finite; a program needn't handle non-finite values.
Results may differ from the reference program's by a relative error of at most 0.014.
Values may be sent and summed in bfloat16 or wider, within the bound.
A program may use at most 128 MiB of HBM per device.

```python
import math
import jax
import jax.numpy as jnp
import numpy as np
from jax import lax

D = 4096
E = 4096
HEADDIM = 64
NSTATE = 16
CONV = 4
EXPERTS = 8
TOPK = 2
FF = 7168
TOK_DEV = 128
HEADS = 64
CAP = 36
GROUP = 1
FFG = 7168
TOKENS = 1024
N_CTX = 8
N_TP = 4


def rising_field(key, rows, columns):
    first, second, third = jax.random.split(key, 3)
    base = jax.random.normal(first, (rows, columns), jnp.float32)
    ramp = jnp.exp(math.log(10.0) * jnp.arange(columns, dtype=jnp.float32) / columns)
    rough = jax.random.uniform(second, (columns,), jnp.float32, 0.6, 1.4)
    row_scale = jnp.exp(jax.random.uniform(third, (rows, 1), jnp.float32, -0.7, 0.7))
    return base * (ramp * rough / 4.0)[None, :] * row_scale


def draw_residual(key, part):
    return rising_field(jax.random.fold_in(key, 3), TOKENS, D).astype(jnp.bfloat16)


def draw_mixer_input(key, part):
    return rising_field(jax.random.fold_in(key, 5), TOKENS, E).astype(jnp.bfloat16)


def head_plan(key):
    base = jax.random.fold_in(key, 17)
    first, second, third = jax.random.split(base, 3)
    share = 0.5
    slow = jax.random.uniform(first, (HEADS,), jnp.float32) < share
    offset = jax.random.uniform(second, (HEADS,), jnp.float32, -1.0, 1.0)
    spread = jax.random.uniform(third, (HEADS,), jnp.float32, 0.0, 1.0)
    return (slow, offset, spread)


def draw_step_bias(key, part):
    slow, offset, spread = head_plan(key)
    return jnp.where(slow, -3.0 + 0.5 * offset, 0.5 * offset).astype(jnp.float32)


def draw_decay_log(key, part):
    slow, offset, spread = head_plan(key)
    fast_rate = math.log(1.0 / 50.0) + spread * math.log(50.0 / 30.0) - math.log(0.8)
    slow_rate = math.log(0.3) + spread * math.log(5.0) - math.log(0.07) - jnp.log(jnp.float32(TOKENS))
    return jnp.where(slow, slow_rate, fast_rate).astype(jnp.float32)


def block_levels(own_key, dims, cuts, least, largest):
    gain, own = 1.0, jax.random.fold_in(own_key, 6)
    for dim, shards_of in cuts:
        heights = jnp.exp(jax.random.uniform(jax.random.fold_in(own, dim), (shards_of,), jnp.float32, least / len(cuts), largest / len(cuts)))
        gain = gain * jnp.repeat(heights, dims[dim] // shards_of).reshape([-1 if axis == dim else 1 for axis in range(len(dims))])
    return gain


def shared_out(stream_key, own, number, rows, count, top, bound, slope):
    sequence = jax.random.permutation(stream_key, count)
    packed, usual = portions_of(count, rows * top, bound, slope, True), portions_of(count, rows * top, bound, slope, False)
    places = jnp.arange(count)

    def named(lengths, offset_by):
        used = int((lengths > 0).sum())
        fixed = max(1, used // 4)
        passed = fixed + (places - fixed + offset_by * (used - fixed)) % max(1, count - fixed)
        return jnp.zeros((count,), jnp.int32).at[sequence[jnp.where(places < fixed, places, passed)]].set(jnp.asarray(lengths, jnp.int32))

    lengths = jnp.where(number % 4 == 0, named(packed, number // 4), named(usual, number - number // 4 - 1))
    mixed = jax.random.permutation(jax.random.fold_in(own, 3), count)
    giver, sink = mixed[0:count // 2 * 2:2], mixed[1:count // 2 * 2:2]
    room = jnp.minimum(lengths[giver] - 1, bound - lengths[sink]) // 2
    room = jnp.where((giver == sequence[0]) | (sink == sequence[0]) | (lengths[sink] == 0), 0, jnp.maximum(room, 0))
    passed = jax.random.randint(jax.random.fold_in(own, 4), (count // 2,), 0, 1 << 20) % (room + 1)
    lengths = lengths.at[giver].add(-passed).at[sink].add(passed)
    labels = jnp.searchsorted(jnp.cumsum(lengths), jnp.arange(rows * top), side="right").astype(jnp.int32)
    grid = labels.reshape(top, rows).T
    grid = grid[jax.random.permutation(jax.random.fold_in(own, 1), rows)]
    offset_by = jax.random.randint(jax.random.fold_in(own, 2), (rows, 1), 0, top)
    return jnp.take_along_axis(grid, (jnp.arange(top)[None, :] + offset_by) % top, axis=1)


def portions_of(amount, total, bound, lean, full):
    portions = [(1 << 20) // math.isqrt(grade ** lean) + 1 for grade in range(1, amount + 1)]
    largest = bound if full else min(bound, max(-(-total // amount), total * portions[0] // sum(portions)))
    least = 1 if total - largest >= amount - 1 else 0
    given, rest = [largest] + [least] * (amount - 1), total - largest - least * (amount - 1)
    while rest > 0:
        free = [i for i in range(1, amount) if given[i] < largest] or [i for i in range(1, amount) if given[i] < bound]
        whole, budget = sum([portions[i] for i in free]), rest
        for i in free:
            more = min(bound - given[i], max(1, budget * portions[i] // whole), rest)
            given[i] = given[i] + more
            rest = rest - more
    return np.array(given)


def noise(rng, shape, scale, bound, cuts=(), kind=jnp.bfloat16):
    drawn = jax.random.normal(rng, shape, jnp.float32) * scale
    if len(cuts) > 0:
        drawn = block_levels(rng, shape, cuts, -0.22, 0.18) * drawn
    return jnp.clip(drawn, min=-bound, max=bound).astype(kind)


def setup_inputs(seed: int = 0) -> dict:
    splits = jax.random.split(jax.random.key(seed), 19)
    residual = draw_residual(jax.random.fold_in(splits[18], 71), 0)
    mixer_input = draw_mixer_input(jax.random.fold_in(splits[18], 71), 0)
    gate_input = noise(splits[2], (TOKENS, E), 1.0, 6.0, ((0, 8), (1, 4)))
    state_proj = noise(splits[3], (TOKENS, 2 * NSTATE), 1.0, 6.0, ((0, 8),))
    step_raw = noise(splits[4], (TOKENS, HEADS), 1.0, 5.0, ((0, 8), (1, 4)), jnp.float32)
    conv_weight = noise(splits[5], (CONV, E), CONV ** -0.5, 3.0, ((1, 4),), jnp.float32)
    conv_state_weight = noise(splits[6], (CONV, 2 * NSTATE), CONV ** -0.5, 3.0, (), jnp.float32)
    step_bias = draw_step_bias(jax.random.fold_in(splits[18], 71), 0)
    decay_log = draw_decay_log(jax.random.fold_in(splits[18], 71), 0)
    skip_gain = jnp.clip(0.5 + 1.0 * jax.random.uniform(splits[9], (HEADS,), jnp.float32) ** block_levels(splits[9], (HEADS,), ((0, 4),), -0.2, 0.2), 0.5, 1.5)
    mixer_gain = jnp.clip(1.0 + 0.1 * jax.random.normal(splits[10], (E,), jnp.float32), 0.5, 1.5)
    out_weight = noise(splits[11], (E, D), E ** -0.5, 0.09375, ((0, 4), (1, 8)))
    feed_gain = jnp.clip(1.0 + 0.1 * jax.random.normal(splits[12], (D,), jnp.float32), 0.5, 1.5)
    expert_gate = noise(splits[13], (EXPERTS * GROUP, D, FFG), D ** -0.5, 0.09375, ((0, 8), (1, 4)))
    expert_up = noise(splits[14], (EXPERTS * GROUP, D, FFG), D ** -0.5, 0.09375, ((0, 8), (1, 4)))
    expert_down = noise(splits[15], (EXPERTS * GROUP, FFG, D), FF ** -0.5, 0.0625, ((0, 8), (2, 4)))
    expert_ids_keys = jax.random.split(jax.random.fold_in(splits[16], 1), TOKENS // TOK_DEV)
    expert_ids_turns = jax.random.permutation(jax.random.fold_in(splits[16], 3), TOKENS // TOK_DEV)
    expert_ids = jax.vmap(lambda own, number: shared_out(jax.random.fold_in(splits[16], 2), own, number, TOK_DEV, EXPERTS, TOPK, CAP, 2))(expert_ids_keys, expert_ids_turns).reshape((TOKENS, TOPK))
    expert_weights = jnp.clip(0.1 + 0.79999997 * jax.random.uniform(splits[17], (TOKENS, TOPK), jnp.float32) ** block_levels(splits[17], (TOKENS, TOPK), ((0, 8),), -0.2, 0.2), 0.1, 0.9)
    return dict(residual=residual, mixer_input=mixer_input, gate_input=gate_input, state_proj=state_proj, step_raw=step_raw, conv_weight=conv_weight, conv_state_weight=conv_state_weight, step_bias=step_bias, decay_log=decay_log, skip_gain=skip_gain, mixer_gain=mixer_gain, out_weight=out_weight, feed_gain=feed_gain, expert_gate=expert_gate, expert_up=expert_up, expert_down=expert_down, expert_ids=expert_ids, expert_weights=expert_weights)


EPSILON = 1e-05

def causal_filter(previous, current, kernel):
    joined = jnp.concatenate([previous, current], axis=0)
    length = current.shape[0]
    total = jnp.zeros(current.shape, jnp.float32)
    for offset in range(kernel.shape[0]):
        total = total + kernel[offset][None, :] * joined[offset:offset + length]
    return jax.nn.silu(total)

def local_terms(values, writer, reader, step_size, log_decay):
    length = values.shape[0]
    cumulative = jnp.cumsum(log_decay, axis=0)
    scores = jnp.dot(reader, writer.T, precision=lax.Precision.HIGHEST)
    order = jnp.arange(length)
    causal = (order[:, None] >= order[None, :])[:, :, None]
    spans = cumulative[:, None, :] - cumulative[None, :, :]
    factor = jnp.where(causal, jnp.exp(jnp.where(causal, spans, 0.0)), 0.0)
    factor = factor * step_size[None, :, :] * scores[:, :, None]
    inside = jnp.einsum('tsh,shp->thp', factor, values, precision=lax.Precision.HIGHEST)
    tail = cumulative[length - 1]
    ending = jnp.exp(tail[None, :] - cumulative) * step_size
    fresh = jnp.einsum('th,thp,tn->hpn', ending, values, writer, precision=lax.Precision.HIGHEST)
    return (inside, cumulative, fresh, tail)

def expert_rows(rows, gate_block, up_block, down_block):
    count = rows.shape[0]
    split_rows = rows.reshape(count, N_TP, D // N_TP).astype(jnp.float32)
    gate_split = gate_block.reshape(GROUP, N_TP, D // N_TP, FFG).astype(jnp.float32)
    up_split = up_block.reshape(GROUP, N_TP, D // N_TP, FFG).astype(jnp.float32)
    gate_terms = jnp.einsum('rtd,gtdf->tgrf', split_rows, gate_split, precision=lax.Precision.HIGHEST)
    up_terms = jnp.einsum('rtd,gtdf->tgrf', split_rows, up_split, precision=lax.Precision.HIGHEST)
    gate_sum = lax.optimization_barrier(jnp.sum(lax.optimization_barrier(gate_terms.astype(jnp.bfloat16)).astype(jnp.float32), axis=0))
    up_sum = lax.optimization_barrier(jnp.sum(lax.optimization_barrier(up_terms.astype(jnp.bfloat16)).astype(jnp.float32), axis=0))
    activated = (jax.nn.silu(gate_sum) * up_sum).astype(jnp.bfloat16)
    activated_wide = lax.optimization_barrier(activated).astype(jnp.float32)
    pieces = jnp.einsum('grf,gfd->grd', activated_wide, down_block.astype(jnp.float32), precision=lax.Precision.HIGHEST)
    return lax.optimization_barrier(jnp.sum(lax.optimization_barrier(pieces.astype(jnp.bfloat16)).astype(jnp.float32), axis=0))

def reference(residual, mixer_input, gate_input, state_proj, step_raw, conv_weight, conv_state_weight, step_bias, decay_log, skip_gain, mixer_gain, out_weight, feed_gain, expert_gate, expert_up, expert_down, expert_ids, expert_weights):
    joined = jnp.concatenate([mixer_input, state_proj], axis=1).astype(jnp.float32)
    kernel = jnp.concatenate([conv_weight, conv_state_weight], axis=1)
    previous = jnp.zeros((CONV - 1, joined.shape[1]), jnp.float32)
    filtered = causal_filter(previous, joined, kernel)
    values = filtered[:, :E].reshape(N_CTX, TOK_DEV, HEADS, HEADDIM)
    writer = filtered[:, E:E + NSTATE].reshape(N_CTX, TOK_DEV, NSTATE)
    reader = filtered[:, E + NSTATE:].reshape(N_CTX, TOK_DEV, NSTATE)
    step_flat = jax.nn.softplus(step_raw + step_bias[None, :])
    log_decay = (-step_flat * jnp.exp(decay_log)[None, :]).reshape(N_CTX, TOK_DEV, HEADS)
    step_size = step_flat.reshape(N_CTX, TOK_DEV, HEADS)

    def advance(state, block):
        values_block, writer_block, reader_block, size_block, decay_block = block
        inside, cumulative, fresh, tail = local_terms(values_block, writer_block, reader_block, size_block, decay_block)
        carried = jnp.einsum('tn,hpn->thp', reader_block, state, precision=lax.Precision.HIGHEST) * jnp.exp(cumulative)[:, :, None]
        mixed_block = inside + carried + skip_gain[None, :, None] * values_block
        return (jnp.exp(tail)[:, None, None] * state + fresh, mixed_block)
    start = jnp.zeros((HEADS, HEADDIM, NSTATE), jnp.float32)
    final_state, mixed = lax.scan(advance, start, (values, writer, reader, step_size, log_decay))
    gated = mixed.reshape(TOKENS, E) * jax.nn.silu(gate_input.astype(jnp.float32))
    scale = lax.rsqrt(lax.optimization_barrier(jnp.mean(gated * gated, axis=1)) + EPSILON)
    normed = (gated * scale[:, None] * mixer_gain[None, :]).astype(jnp.bfloat16)
    mixer_out = jnp.dot(normed, out_weight, preferred_element_type=jnp.float32)
    hidden_state = (residual.astype(jnp.float32) + mixer_out).astype(jnp.bfloat16)
    state_float = lax.optimization_barrier(hidden_state).astype(jnp.float32)
    norm_scale = lax.rsqrt(lax.optimization_barrier(jnp.mean(state_float * state_float, axis=1)) + EPSILON)
    expert_input = (state_float * norm_scale[:, None] * feed_gain[None, :]).astype(jnp.bfloat16)
    blocks = expert_ids.reshape(N_CTX, TOK_DEV * TOPK).astype(jnp.int32)
    matches = (blocks[:, :, None] == jnp.arange(EXPERTS, dtype=jnp.int32)[None, None, :]).astype(jnp.int32)
    slots = lax.optimization_barrier(jnp.sum((jnp.cumsum(matches, axis=1) - matches) * matches, axis=2)).astype(jnp.int32)
    targets = (blocks * CAP + slots).astype(jnp.int32)
    rows = jnp.repeat(expert_input.reshape(N_CTX, TOK_DEV, D), TOPK, axis=1)
    owners = jnp.arange(N_CTX, dtype=jnp.int32)[:, None]
    buffer = jnp.zeros((N_CTX, EXPERTS * CAP, D), jnp.bfloat16).at[owners, targets].set(rows)
    gate_all = expert_gate.reshape(EXPERTS, GROUP, D, FFG)
    up_all = expert_up.reshape(EXPERTS, GROUP, D, FFG)
    down_all = expert_down.reshape(EXPERTS, GROUP, FFG, D)

    def one_expert(index):
        picked = lax.dynamic_slice_in_dim(buffer, (index * CAP).astype(jnp.int32), CAP, 1).reshape(N_CTX * CAP, D)
        return expert_rows(picked, gate_all[index], up_all[index], down_all[index]).reshape(N_CTX, CAP, D)
    outputs = lax.map(one_expert, jnp.arange(EXPERTS, dtype=jnp.int32))
    chosen = outputs[blocks, owners, slots].reshape(TOKENS, TOPK, D)
    routed = lax.optimization_barrier(jnp.sum(expert_weights[:, :, None] * chosen, axis=1))
    return (state_float + routed).astype(jnp.bfloat16)
```

```python
import functools

import jax
import jax.numpy as jnp
from jax import lax
from jax.experimental import pallas as pl
from jax.experimental.pallas import tpu as pltpu
from jax.sharding import PartitionSpec as P


EXPERTS = 8
CAP = 36


EPSILON = 1e-05


def passed_along(value, axis, steps):
    count = lax.axis_size(axis)
    first, last = (max(0, -steps), min(count, count - steps))
    return lax.ppermute(value, axis, [(source, source + steps) for source in range(first, last)])


def swapped(value, distance):
    return lax.ppermute(value, "tp", [(p, p ^ distance) for p in range(lax.axis_size("tp"))])


def rotated(value, steps):
    count = lax.axis_size("ctx")
    return lax.ppermute(value, "ctx", [(c, (c + steps) % count) for c in range(count)])


def tensor_total(value):
    return (value + swapped(value, 1)) + (swapped(value, 2) + swapped(value, 3))


def entering(decay, fresh, axis):
    peers, position = (lax.axis_size(axis), lax.axis_index(axis))
    packed = jnp.concatenate([fresh, decay[None, :]], axis=0).astype(jnp.bfloat16)
    if peers == EXPERTS:
        total, carry = (jnp.zeros_like(fresh), jnp.ones_like(decay)[None, :])
        for distance in range(1, peers):
            part = passed_along(packed, axis, distance).astype(jnp.float32)
            total = total + carry * part[:-1]
            carry = carry * part[-1:]
        return total
    everything = lax.all_gather(packed, axis).astype(jnp.float32)

    def step(k, before):
        part = everything[k]
        return jnp.where(k < position, part[-1:] * before + part[:-1], before)

    return lax.fori_loop(0, peers, step, jnp.zeros_like(fresh))


def causal_filter(previous, current, kernel):
    joined = jnp.concatenate([previous, current], axis=0)
    length = current.shape[0]
    total = jnp.zeros(current.shape, jnp.float32)
    for offset in range(kernel.shape[0]):
        total = total + kernel[offset][None, :] * joined[offset : offset + length]
    return jax.nn.silu(total)


def local_terms(values, writer, reader, step_size, log_decay):
    length = values.shape[0]
    cumulative = jnp.cumsum(log_decay, axis=0)
    scores = jnp.dot(reader, writer.T, precision=lax.Precision.HIGHEST)
    order = jnp.arange(length)
    causal = (order[:, None] >= order[None, :])[:, :, None]
    spans = cumulative[:, None, :] - cumulative[None, :, :]
    factor = jnp.where(causal, jnp.exp(jnp.where(causal, spans, 0.0)), 0.0)
    factor = factor * step_size[None, :, :] * scores[:, :, None]
    inside = jnp.einsum("tsh,shp->thp", factor, values, precision=lax.Precision.HIGHEST)
    tail = cumulative[length - 1]
    ending = jnp.exp(tail[None, :] - cumulative) * step_size
    weighted = (ending[:, :, None] * values).reshape(length, -1)
    fresh = jnp.dot(writer.T, weighted, precision=lax.Precision.HIGHEST)
    return (inside, cumulative, fresh, tail)


SUB = 16
CHUNK = 256
MESH = pl.DeviceIdType.MESH


def remote(source, target, send, receive, device):
    return pltpu.make_async_remote_copy(
        src_ref=source,
        dst_ref=target,
        send_sem=send,
        recv_sem=receive,
        device_id=device,
        device_id_type=MESH,
    )


def unfold(count, extra, fold, part):
    j = lax.broadcasted_iota(jnp.int32, (count * extra, count * SUB), 0)
    i = lax.broadcasted_iota(jnp.int32, (count * extra, count * SUB), 1)
    return (i == j * fold + part).astype(jnp.bfloat16)


def refold(count, extra, fold, part):
    j = lax.broadcasted_iota(jnp.int32, (count * SUB, count * extra), 1)
    i = lax.broadcasted_iota(jnp.int32, (count * SUB, count * extra), 0)
    return (i == j * fold + part).astype(jnp.bfloat16)


def expert_kernel(
    peers,
    expert_input,
    picker,
    hidden,
    weights_high,
    weights_low,
    gate,
    up,
    down,
    out,
    gate_tiles,
    up_tiles,
    down_tiles,
    packed,
    packed_extra,
    rows,
    rows_extra,
    answers,
    answers_extra,
    first,
    first_in,
    far,
    far_in,
    near_in,
    active,
    active_beside,
    active_across,
    active_diagonal,
    total,
    tile_sem,
    home_send,
    home_receive,
    pair_send,
    pair_receive,
):
    ctx, tp = lax.axis_index("ctx"), lax.axis_index("tp")
    beside = tp + 1 - 2 * (tp % 2)
    across = (tp + 2) % 4
    diagonal = 3 - tp
    width = rows.shape[1]
    chunks = first.shape[1]
    hidden_width = chunks * CHUNK
    main = packed.shape[0] // peers
    extra = (rows.shape[0] - peers * main) // peers
    fold = SUB // extra
    piece = width // fold

    places = ((diagonal, across, beside, tp), (diagonal, across, beside, tp), (tp, beside, across, diagonal))

    def tile(kind, place, j):
        span = pl.ds(pl.multiple_of(places[kind][place] * hidden_width + j * CHUNK, CHUNK), CHUNK)
        source = (gate, up, down)[kind]
        source = source.at[0, span, :] if kind == 2 else source.at[0, :, span]
        target = (gate_tiles, up_tiles, down_tiles)[kind].at[place, j]
        return pltpu.make_async_copy(source, target, tile_sem.at[4 * kind + place, j])

    def start_group(chosen):
        def body(j, carry):
            for kind, place in chosen:
                tile(kind, place, j).start()
            return carry

        lax.fori_loop(0, chunks, body, 0)

    start_group([(kind, place) for place in (0, 1) for kind in (0, 1)])
    start_group([(kind, place) for place in (2, 3) for kind in (0, 1)])
    start_group([(2, place) for place in range(4)])

    barrier = pltpu.get_barrier_semaphore()
    for distance in range(1, peers):
        pl.semaphore_signal(
            barrier, inc=1, device_id={"ctx": (ctx + distance) % peers}, device_id_type=MESH
        )
    for other in (beside, across, diagonal):
        pl.semaphore_signal(barrier, inc=1, device_id={"tp": other}, device_id_type=MESH)

    picked = jnp.dot(picker[...], expert_input[...], preferred_element_type=jnp.float32)
    packed[...] = picked[: peers * main].astype(jnp.bfloat16)
    tail = picked[peers * main :].astype(jnp.bfloat16)
    folded = jnp.zeros((peers * SUB, piece), jnp.float32)
    for part in range(fold):
        folded = folded + jnp.dot(
            refold(peers, extra, fold, part),
            tail[:, part * piece : (part + 1) * piece],
            preferred_element_type=jnp.float32,
        )
    packed_extra[...] = folded.astype(jnp.bfloat16)
    pl.semaphore_wait(barrier, peers - 1 + 3)

    def travel(sources, targets, sign, base):
        copies = []
        for kind, (source, target) in enumerate(zip(sources, targets)):
            size = (main, SUB)[kind]
            for distance in range(1, peers):
                block = pl.ds(distance * size, size)
                copies.append(
                    remote(
                        source.at[block],
                        target.at[block],
                        home_send.at[base + kind, distance],
                        home_receive.at[base + kind, distance],
                        {"ctx": (ctx + sign * distance + peers) % peers},
                    )
                )
        return copies

    outward = travel((packed, packed_extra), (rows, rows_extra), 1, 0)
    for copy in outward:
        copy.start()
    rows[:main] = packed[:main]
    rows_extra[:SUB] = packed_extra[:SUB]
    for copy in outward:
        copy.wait_recv()
    landed = rows_extra[...]
    for part in range(fold):
        rows[peers * main :, part * piece : (part + 1) * piece] = jnp.dot(
            unfold(peers, extra, fold, part), landed, preferred_element_type=jnp.float32
        ).astype(jnp.bfloat16)

    def pair(kind, j, source, target, other):
        return remote(source, target, pair_send.at[kind, j], pair_receive.at[kind, j], {"tp": other})

    both = (gate_tiles, up_tiles)

    def product(which, place, j):
        tile(which, place, j).wait()
        return jnp.dot(rows[...], both[which][place, j], preferred_element_type=jnp.float32)

    def first_copy(which, j):
        return pair(which, j, first.at[which, j], first_in.at[which, j], beside)

    def far_copy(which, j):
        return pair(2 + which, j, far.at[which, j], far_in.at[which, j], across)

    def near_copy(which, j):
        return pair(4 + which, j, first.at[which, j], near_in.at[which, j], beside)

    def beside_copy(j):
        return pair(6, j, active.at[j], active_beside.at[j], beside)

    def across_copy(j):
        return pair(7, j, active.at[j], active_across.at[j], across)

    def diagonal_copy(j):
        return pair(8, j, active_across.at[j], active_diagonal.at[j], beside)

    def far_step(j, carry):
        for which in range(2):
            first[which, j] = product(which, 0, j).astype(jnp.bfloat16)
            first_copy(which, j).start()
        for which in range(2):
            mine = product(which, 1, j)
            first_copy(which, j).wait_recv()
            far[which, j] = (mine + first_in[which, j].astype(jnp.float32)).astype(jnp.bfloat16)
            far_copy(which, j).start()
        return carry

    lax.fori_loop(0, chunks, far_step, 0)

    def near_step(j, carry):
        for which in range(2):
            mine = product(which, 2, j).astype(jnp.bfloat16)
            first_copy(which, j).wait_send()
            first[which, j] = mine
            near_copy(which, j).start()
        return carry

    lax.fori_loop(0, chunks, near_step, 0)
    total[...] = jnp.zeros_like(total)

    def lowered(source, place, j):
        tile(2, place, j).wait()
        total[...] += jnp.dot(source[j], down_tiles[place, j], preferred_element_type=jnp.float32)

    def own_step(j, carry):
        sums = []
        for which in range(2):
            mine = product(which, 3, j).astype(jnp.bfloat16).astype(jnp.float32)
            near_copy(which, j).wait_recv()
            mine = mine + near_in[which, j].astype(jnp.float32)
            far_copy(which, j).wait_recv()
            sums.append(mine + far_in[which, j].astype(jnp.float32))
        active[j] = (jax.nn.silu(sums[0]) * sums[1]).astype(jnp.bfloat16)
        across_copy(j).start()
        beside_copy(j).start()
        lowered(active, 0, j)
        beside_copy(j).wait_recv()
        lowered(active_beside, 1, j)
        return carry

    lax.fori_loop(0, chunks, own_step, 0)

    def last_step(j, carry):
        across_copy(j).wait_recv()
        diagonal_copy(j).start()
        lowered(active_across, 2, j)
        diagonal_copy(j).wait_recv()
        lowered(active_diagonal, 3, j)
        return carry

    lax.fori_loop(0, chunks, last_step, 0)

    for copy in outward:
        copy.wait_send()
    packed[...] = total[: peers * main].astype(jnp.bfloat16)
    tail = total[peers * main :].astype(jnp.bfloat16)
    folded = jnp.zeros((peers * SUB, piece), jnp.float32)
    for part in range(fold):
        folded = folded + jnp.dot(
            refold(peers, extra, fold, part),
            tail[:, part * piece : (part + 1) * piece],
            preferred_element_type=jnp.float32,
        )
    packed_extra[...] = folded.astype(jnp.bfloat16)
    homeward = travel((packed, packed_extra), (answers, answers_extra), -1, 2)
    for copy in homeward:
        copy.start()
    answers[:main] = packed[:main]
    answers_extra[:SUB] = packed_extra[:SUB]

    def drain(j, carry):
        for which in range(2):
            far_copy(which, j).wait_send()
            near_copy(which, j).wait_send()
        beside_copy(j).wait_send()
        across_copy(j).wait_send()
        diagonal_copy(j).wait_send()
        return carry

    lax.fori_loop(0, chunks, drain, 0)
    for copy in homeward:
        copy.wait_recv()
    landed = answers_extra[...]
    for part in range(fold):
        answers[peers * main :, part * piece : (part + 1) * piece] = jnp.dot(
            unfold(peers, extra, fold, part), landed, preferred_element_type=jnp.float32
        ).astype(jnp.bfloat16)
    routed = jnp.dot(weights_high[...], answers[...], preferred_element_type=jnp.float32)
    routed = routed + jnp.dot(weights_low[...], answers[...], preferred_element_type=jnp.float32)
    out[...] = (hidden[...].astype(jnp.float32) + routed).astype(jnp.bfloat16)
    for copy in homeward:
        copy.wait_send()


def experts_direct(expert_input, hidden, expert_ids, expert_weights, gate, up, down):
    peers = lax.axis_size("ctx")
    ctx = lax.axis_index("ctx")
    tokens, width = expert_input.shape
    hidden_width = gate.shape[2] // 4
    chunks = hidden_width // CHUNK
    main = CAP // SUB * SUB
    extra = CAP - main
    count = peers * CAP
    flat = expert_ids.reshape(-1)
    matches = (flat[:, None] == jnp.arange(EXPERTS)[None, :]).astype(jnp.int32)
    slots = jnp.sum((jnp.cumsum(matches, axis=0) - matches) * matches, axis=1)
    places = (flat - ctx) % EXPERTS
    targets = jnp.where(
        slots < main, places * main + slots, peers * main + places * extra + slots - main
    ).reshape(tokens, -1)
    chosen = targets[:, :, None] == jnp.arange(count)[None, None, :]
    weights = jnp.sum(jnp.where(chosen, expert_weights[:, :, None], 0.0), axis=1)
    weights_high = weights.astype(jnp.bfloat16)
    weights_low = (weights - weights_high.astype(jnp.float32)).astype(jnp.bfloat16)
    picker = jnp.any(
        targets[None, :, :] == jnp.arange(count)[:, None, None], axis=2
    ).astype(jnp.bfloat16)
    vmem = pl.BlockSpec(memory_space=pltpu.VMEM)
    anywhere = pl.BlockSpec(memory_space=pl.ANY)
    block = (chunks, count, CHUNK)
    low = jnp.bfloat16
    return pl.pallas_call(
        functools.partial(expert_kernel, peers),
        out_shape=jax.ShapeDtypeStruct((tokens, width), low),
        in_specs=[vmem] * 5 + [anywhere] * 3,
        out_specs=vmem,
        scratch_shapes=[
            pltpu.VMEM((4, chunks, width, CHUNK), low),
            pltpu.VMEM((4, chunks, width, CHUNK), low),
            pltpu.VMEM((4, chunks, CHUNK, width), low),
            pltpu.VMEM((peers * main, width), low),
            pltpu.VMEM((peers * SUB, width * extra // SUB), low),
            pltpu.VMEM((count, width), low),
            pltpu.VMEM((peers * SUB, width * extra // SUB), low),
            pltpu.VMEM((count, width), low),
            pltpu.VMEM((peers * SUB, width * extra // SUB), low),
            pltpu.VMEM((2,) + block, low),
            pltpu.VMEM((2,) + block, low),
            pltpu.VMEM((2,) + block, low),
            pltpu.VMEM((2,) + block, low),
            pltpu.VMEM((2,) + block, low),
            pltpu.VMEM(block, low),
            pltpu.VMEM(block, low),
            pltpu.VMEM(block, low),
            pltpu.VMEM(block, low),
            pltpu.VMEM((count, width), jnp.float32),
            pltpu.SemaphoreType.DMA((12, chunks)),
            pltpu.SemaphoreType.DMA((4, peers)),
            pltpu.SemaphoreType.DMA((4, peers)),
            pltpu.SemaphoreType.DMA((9, chunks)),
            pltpu.SemaphoreType.DMA((9, chunks)),
        ],
        compiler_params=pltpu.CompilerParams(
            collective_id=0, has_side_effects=True, vmem_limit_bytes=66_000_000
        ),
        name="experts",
    )(expert_input, picker, hidden, weights_high, weights_low, gate, up, down)


def body(
    residual,
    mixer_input,
    gate_input,
    state_proj,
    step_raw,
    conv_weight,
    conv_state_weight,
    step_bias,
    decay_log,
    skip_gain,
    mixer_gain,
    out_weight,
    feed_gain,
    expert_gate,
    expert_up,
    expert_down,
    expert_ids,
    expert_weights,
):
    tensor_count = lax.axis_size("tp")
    context_count = lax.axis_size("ctx")
    tokens = mixer_input.shape[0]
    channels = mixer_input.shape[1]
    states = state_proj.shape[1] // 2
    heads_local = step_raw.shape[1]
    head_size = channels // heads_local
    taps = conv_weight.shape[0]
    joined = jnp.concatenate([mixer_input, state_proj], axis=1)
    previous = passed_along(joined[tokens - (taps - 1) :], "ctx", 1)
    kernel = jnp.concatenate([conv_weight, conv_state_weight], axis=1)
    filtered = causal_filter(previous.astype(jnp.float32), joined.astype(jnp.float32), kernel)
    values = filtered[:, :channels].reshape(tokens, heads_local, head_size)
    writer = filtered[:, channels : channels + states]
    reader = filtered[:, channels + states :]
    step_size = jax.nn.softplus(step_raw + step_bias[None, :])
    log_decay = -step_size * jnp.exp(decay_log)[None, :]
    inside, cumulative, fresh, tail = local_terms(values, writer, reader, step_size, log_decay)

    incoming = entering(jnp.repeat(jnp.exp(tail), head_size), fresh, "ctx")
    carried = (
        jnp.dot(reader, incoming, precision=lax.Precision.HIGHEST).reshape(values.shape)
        * jnp.exp(cumulative)[:, :, None]
    )
    mixed = inside + carried + skip_gain[None, :, None] * values
    gated = mixed.reshape(tokens, channels) * jax.nn.silu(gate_input.astype(jnp.float32))
    tp_index = lax.axis_index("tp")
    core, chip = (tp_index % 2, tp_index // 2)
    scaled = (gated * mixer_gain[None, :]).astype(jnp.bfloat16)
    direct = context_count == EXPERTS
    ctx_index = lax.axis_index("ctx")
    if direct:
        pairs = []
        for plane in range(4):
            block = rotated(scaled, 2 * plane) if plane else scaled
            other = lax.ppermute(block, "ctx", [(c, c ^ 1) for c in range(context_count)])
            pair = jnp.concatenate([block, other], axis=0)
            pairs.append(jnp.dot(pair, out_weight, preferred_element_type=jnp.float32))
        products = jnp.stack(pairs)

        def projected(quarter):
            place = (ctx_index // 2 - quarter) % 4
            return lax.dynamic_index_in_dim(products, place, 0, keepdims=False)

    else:
        everyone = lax.all_gather(scaled, "ctx", axis=0, tiled=True)
        span = everyone.shape[0] // tensor_count

        def projected(quarter):
            rows = lax.dynamic_slice_in_dim(everyone, quarter * span, span, 0)
            return jnp.dot(rows, out_weight, preferred_element_type=jnp.float32)

    square_sum = tensor_total(jnp.sum(gated * gated, axis=1))
    scale = lax.rsqrt(square_sum / (channels * tensor_count) + EPSILON)
    own, beside = (chip * 2 + core, chip * 2 + 1 - core)
    across, diagonal = ((1 - chip) * 2 + core, (1 - chip) * 2 + 1 - core)
    far = swapped(projected(diagonal).astype(jnp.bfloat16), 1)
    far = swapped((projected(across) + far.astype(jnp.float32)).astype(jnp.bfloat16), 2)
    near = swapped(projected(beside).astype(jnp.bfloat16), 1)
    reduced = projected(own) + near.astype(jnp.float32) + far.astype(jnp.float32)
    blocks = context_count // tensor_count
    reduced = reduced.astype(jnp.bfloat16).reshape(blocks, tokens, -1)
    pieces = []
    for j in range(blocks):
        moves = [
            (c * tensor_count + p, (p * blocks + (c + j) % blocks) * tensor_count + c // blocks)
            for c in range(context_count)
            for p in range(tensor_count)
        ]
        if direct:
            block = reduced[j]
        else:
            block = lax.dynamic_index_in_dim(reduced, (ctx_index + j) % blocks, 0, keepdims=False)
        pieces.append(lax.ppermute(block, ("ctx", "tp"), moves))
    stacked = jnp.stack(pieces)
    order = (ctx_index - jnp.arange(blocks)) % blocks
    if blocks == 2:
        first = ctx_index % 2 == 0
        mixer_out = jnp.concatenate(
            [jnp.where(first, pieces[0], pieces[1]), jnp.where(first, pieces[1], pieces[0])], axis=1
        )
    else:
        mixer_out = jnp.take(stacked, order, axis=0).transpose(1, 0, 2).reshape(tokens, -1)
    mixer_out = mixer_out.astype(jnp.float32) * scale[:, None]
    hidden_state = (residual.astype(jnp.float32) + mixer_out).astype(jnp.bfloat16)
    state_float = lax.optimization_barrier(hidden_state).astype(jnp.float32)
    width_total = hidden_state.shape[1] * tensor_count
    feed_sum = tensor_total(jnp.sum(state_float * state_float, axis=1))
    feed_scale = lax.rsqrt(feed_sum / width_total + EPSILON)
    expert_input = (state_float * feed_scale[:, None] * feed_gain[None, :]).astype(jnp.bfloat16)
    if direct:
        return experts_direct(
            expert_input, hidden_state, expert_ids, expert_weights, expert_gate, expert_up, expert_down
        )
    group = context_count // EXPERTS
    width_local = expert_input.shape[1]
    flat_experts = expert_ids.reshape(-1)
    matches = (flat_experts[:, None] == jnp.arange(EXPERTS)[None, :]).astype(jnp.int32)
    slots = jnp.sum((jnp.cumsum(matches, axis=0) - matches) * matches, axis=1)
    places = (flat_experts - ctx_index) % EXPERTS if direct else flat_experts
    targets = (places * CAP + slots).reshape(tokens, -1)
    picker = jnp.any(targets[None, :, :] == jnp.arange(EXPERTS * CAP)[:, None, None], axis=2)
    buffer = jnp.dot(
        picker.astype(jnp.bfloat16), expert_input, preferred_element_type=jnp.float32
    ).astype(jnp.bfloat16)
    outgoing = jnp.broadcast_to(
        buffer.reshape(EXPERTS, 1, CAP, width_local), (EXPERTS, group, CAP, width_local)
    )
    outgoing = outgoing.reshape(EXPERTS * group, CAP, width_local)
    gate_local = expert_gate[0]
    up_local = expert_up[0]
    down_local = expert_down[0]
    sources, items, depth = outgoing.shape
    if direct:
        flattened = jnp.concatenate(
            [outgoing[r] if r == 0 else rotated(outgoing[r], r) for r in range(sources)], axis=0
        )
    else:
        arrived = lax.all_to_all(outgoing, "ctx", split_axis=0, concat_axis=0, tiled=True)
        flattened = arrived.reshape(sources * items, depth)
    hidden = gate_local.shape[1] // tensor_count

    def product(source, weight, quarter):
        columns = lax.dynamic_slice_in_dim(weight, quarter * hidden, hidden, 1)
        return jnp.dot(source, columns, preferred_element_type=jnp.float32)

    fars, nears, rows = ([], [], flattened)
    for weight in (gate_local, up_local):
        far = product(rows, weight, diagonal).astype(jnp.bfloat16)
        far = swapped(far, 1)
        nears.append(swapped(product(rows, weight, beside).astype(jnp.bfloat16), 1))
        far = (product(rows, weight, across) + far.astype(jnp.float32)).astype(jnp.bfloat16)
        far, rows = lax.optimization_barrier((far, rows))
        fars.append(swapped(far, 2))
    gate_share, up_share = (
        product(rows, weight, own).astype(jnp.bfloat16).astype(jnp.float32)
        + near.astype(jnp.float32)
        + far.astype(jnp.float32)
        for weight, near, far in zip((gate_local, up_local), nears, fars)
    )
    share = (jax.nn.silu(gate_share) * up_share).astype(jnp.bfloat16)
    share_across = swapped(share, 2)
    share_beside = swapped(share, 1)

    def lowered(part, quarter):
        rows = lax.dynamic_slice_in_dim(down_local, quarter * hidden, hidden, 0)
        return jnp.dot(part, rows, preferred_element_type=jnp.float32)

    local = lowered(share, own) + lowered(share_beside, beside)
    local, share_across = lax.optimization_barrier((local, share_across))
    share_diagonal = swapped(share_across, 1)
    answer = (
        local
        + lowered(share_across, across)
        + lowered(share_diagonal, diagonal)
    ).astype(jnp.bfloat16)
    answer = answer.reshape(sources, items, depth)
    if direct:
        answers = jnp.stack(
            [answer[r] if r == 0 else rotated(answer[r], -r) for r in range(sources)]
        )
    else:
        answers = lax.all_to_all(answer, "ctx", split_axis=0, concat_axis=0, tiled=True)
    summed = jnp.sum(answers.reshape(EXPERTS, group, CAP, width_local), axis=1, dtype=jnp.float32)
    summed = summed.reshape(EXPERTS * CAP, width_local)
    chosen = jnp.take(summed, targets, axis=0)
    routed = jnp.sum(expert_weights[:, :, None] * chosen, axis=1)
    return (state_float + routed).astype(jnp.bfloat16)


def solution(mesh):
    placed = (
        P("ctx", "tp"),
        P("ctx", "tp"),
        P("ctx", "tp"),
        P("ctx", None),
        P("ctx", "tp"),
        P(None, "tp"),
        P(),
        P("tp"),
        P("tp"),
        P("tp"),
        P("tp"),
        P("tp", "ctx"),
        P("tp"),
        P("ctx", "tp", None),
        P("ctx", "tp", None),
        P("ctx", None, "tp"),
        P("ctx", None),
        P("ctx", None),
    )

    return jax.shard_map(
        body, mesh=mesh, in_specs=placed, out_specs=P("ctx", "tp"), check_vma=False
    )
```

```python
import functools

import jax
import jax.numpy as jnp
from jax import lax
from jax.experimental import pallas as pl
from jax.experimental.pallas import tpu as pltpu
from jax.sharding import PartitionSpec as P


EXPERTS = 8
CAP = 36


EPSILON = 1e-05


def passed_along(value, axis, steps):
    count = lax.axis_size(axis)
    first, last = (max(0, -steps), min(count, count - steps))
    return lax.ppermute(value, axis, [(source, source + steps) for source in range(first, last)])


def swapped(value, distance):
    return lax.ppermute(value, "tp", [(p, p ^ distance) for p in range(lax.axis_size("tp"))])


def rotated(value, steps):
    count = lax.axis_size("ctx")
    return lax.ppermute(value, "ctx", [(c, (c + steps) % count) for c in range(count)])


def tensor_total(value):
    return (value + swapped(value, 1)) + (swapped(value, 2) + swapped(value, 3))


def entering(decay, fresh, axis):
    peers, position = (lax.axis_size(axis), lax.axis_index(axis))
    packed = jnp.concatenate([fresh, decay[None, :]], axis=0).astype(jnp.bfloat16)
    if peers == EXPERTS:
        total, carry = (jnp.zeros_like(fresh), jnp.ones_like(decay)[None, :])
        for distance in range(1, peers):
            part = passed_along(packed, axis, distance).astype(jnp.float32)
            total = total + carry * part[:-1]
            carry = carry * part[-1:]
        return total
    everything = lax.all_gather(packed, axis).astype(jnp.float32)

    def step(k, before):
        part = everything[k]
        return jnp.where(k < position, part[-1:] * before + part[:-1], before)

    return lax.fori_loop(0, peers, step, jnp.zeros_like(fresh))


def causal_filter(previous, current, kernel):
    joined = jnp.concatenate([previous, current], axis=0)
    length = current.shape[0]
    total = jnp.zeros(current.shape, jnp.float32)
    for offset in range(kernel.shape[0]):
        total = total + kernel[offset][None, :] * joined[offset : offset + length]
    return jax.nn.silu(total)


def local_terms(values, writer, reader, step_size, log_decay):
    length = values.shape[0]
    cumulative = jnp.cumsum(log_decay, axis=0)
    scores = jnp.dot(reader, writer.T, precision=lax.Precision.HIGHEST)
    order = jnp.arange(length)
    causal = (order[:, None] >= order[None, :])[:, :, None]
    spans = cumulative[:, None, :] - cumulative[None, :, :]
    factor = jnp.where(causal, jnp.exp(jnp.where(causal, spans, 0.0)), 0.0)
    factor = factor * step_size[None, :, :] * scores[:, :, None]
    inside = jnp.einsum("tsh,shp->thp", factor, values, precision=lax.Precision.HIGHEST)
    tail = cumulative[length - 1]
    ending = jnp.exp(tail[None, :] - cumulative) * step_size
    weighted = (ending[:, :, None] * values).reshape(length, -1)
    fresh = jnp.dot(writer.T, weighted, precision=lax.Precision.HIGHEST)
    return (inside, cumulative, fresh, tail)


SUB = 16
CHUNK = 256
MESH = pl.DeviceIdType.MESH


def remote(source, target, send, receive, device):
    return pltpu.make_async_remote_copy(
        src_ref=source,
        dst_ref=target,
        send_sem=send,
        recv_sem=receive,
        device_id=device,
        device_id_type=MESH,
    )


def unfold(count, extra, fold, part):
    j = lax.broadcasted_iota(jnp.int32, (count * extra, count * SUB), 0)
    i = lax.broadcasted_iota(jnp.int32, (count * extra, count * SUB), 1)
    return (i == j * fold + part).astype(jnp.bfloat16)


def refold(count, extra, fold, part):
    j = lax.broadcasted_iota(jnp.int32, (count * SUB, count * extra), 1)
    i = lax.broadcasted_iota(jnp.int32, (count * SUB, count * extra), 0)
    return (i == j * fold + part).astype(jnp.bfloat16)


def block_kernel(
    peers,
    gated,
    mixer_gain,
    residual,
    feed_gain,
    picker,
    weights_high,
    weights_low,
    weight_own,
    weight_beyond,
    gate,
    up,
    down,
    out,
    hidden,
    expert_input,
    stats,
    stats_in,
    gate_tiles,
    up_tiles,
    down_tiles,
    packed,
    packed_extra,
    rows,
    rows_extra,
    answers,
    answers_extra,
    first,
    first_in,
    far,
    far_in,
    near_in,
    active,
    active_beside,
    active_across,
    active_diagonal,
    total,
    tile_sem,
    weight_sem,
    line_send,
    line_receive,
    merge_send,
    merge_receive,
    final_receive,
    stats_send,
    stats_receive,
    home_send,
    home_receive,
    pair_send,
    pair_receive,
):
    ctx, tp = lax.axis_index("ctx"), lax.axis_index("tp")
    beside = tp + 1 - 2 * (tp % 2)
    across = (tp + 2) % 4
    diagonal = 3 - tp
    width = rows.shape[1]
    chunks = first.shape[1]
    hidden_width = chunks * CHUNK
    main = packed.shape[0] // peers
    extra = (rows.shape[0] - peers * main) // peers
    fold = SUB // extra
    piece = width // fold

    places = ((diagonal, across, beside, tp), (diagonal, across, beside, tp), (tp, beside, across, diagonal))

    def tile(kind, place, j):
        span = pl.ds(pl.multiple_of(places[kind][place] * hidden_width + j * CHUNK, CHUNK), CHUNK)
        source = (gate, up, down)[kind]
        source = source.at[0, span, :] if kind == 2 else source.at[0, :, span]
        target = (gate_tiles, up_tiles, down_tiles)[kind].at[place, j]
        return pltpu.make_async_copy(source, target, tile_sem.at[4 * kind + place, j])

    def start_group(chosen):
        def body(j, carry):
            for kind, place in chosen:
                tile(kind, place, j).start()
            return carry

        lax.fori_loop(0, chunks, body, 0)

    z, x = ctx // 2, ctx % 2
    core, side = tp % 2, tp // 2
    line = peers // 2
    tokens = residual.shape[0]
    half = tokens // 2
    held = down_tiles.at[3]

    def weight_copy(n):
        source = (weight_own, weight_beyond)[n // 2].at[:, pl.ds(n % 2 * CHUNK, CHUNK)]
        place = 2 * (x if n < 2 else 1 - x) + n % 2
        return pltpu.make_async_copy(source, gate_tiles.at[3, place], weight_sem.at[n])

    for n in range(4):
        weight_copy(n).start()
    start_group([(kind, place) for place in (0, 1) for kind in (0, 1)])
    start_group([(0, 2), (1, 2), (1, 3)])
    start_group([(2, place) for place in range(3)])

    barrier = pltpu.get_barrier_semaphore()
    for distance in range(1, peers):
        pl.semaphore_signal(
            barrier, inc=1, device_id={"ctx": (ctx + distance) % peers}, device_id_type=MESH
        )
    for other in (beside, across, diagonal):
        pl.semaphore_signal(barrier, inc=1, device_id={"tp": other}, device_id_type=MESH)

    @pl.when(z != tp)
    def _():
        pl.semaphore_signal(
            barrier, inc=1, device_id={"ctx": tp * 2 + x, "tp": beside}, device_id_type=MESH
        )

    def piece_of(b, h):
        return held.at[b // 2, pl.ds(pl.multiple_of(b % 2 * tokens + h * half, half), half), :]

    def slab(kind, b):
        return held.at[line // 2 + kind, pl.ds(pl.multiple_of(b * half, half), half), :]

    def as_row(column):
        return jnp.broadcast_to(column, (tokens, tokens)).T[:8]

    def as_column(row):
        return jnp.broadcast_to(row[:1], (tokens, tokens)).T[:, :1]

    def stats_copy(kind, n):
        other = (beside, across, diagonal)[n]
        return remote(
            stats.at[kind], stats_in.at[kind, n], stats_send.at[kind, n], stats_receive.at[kind, n], {"tp": other}
        )

    def stats_total(kind):
        for n in range(3):
            stats_copy(kind, n).wait_recv()
        row = (stats[kind] + stats_in[kind, 0]) + (stats_in[kind, 1] + stats_in[kind, 2])
        return lax.rsqrt(as_column(row) / (width * 4) + EPSILON)

    value = gated[...]
    held[z // 2, pl.ds(pl.multiple_of(z % 2 * tokens, tokens), tokens), :] = (
        value * mixer_gain[...]
    ).astype(jnp.bfloat16)
    stats[0] = as_row(jnp.sum(value * value, axis=1, keepdims=True))
    pl.semaphore_wait(barrier, peers - 1 + 3 + jnp.where(z == beside, line - 1, 0))

    def line_copy(direction, b, h):
        return remote(
            piece_of(b, h),
            piece_of(b, h),
            line_send.at[direction, b, h],
            line_receive.at[b, h],
            {"ctx": (ctx + 2 - 4 * direction + peers) % peers},
        )

    for h in range(2):

        @pl.when(z < line - 1)
        def _():
            line_copy(0, z, h).start()

        @pl.when(z > 0)
        def _():
            line_copy(1, z, h).start()

    for n in range(3):
        stats_copy(0, n).start()
    for n in range(4):
        weight_copy(n).wait()

    def give_copy(b):
        return remote(slab(0, b), slab(1, b), merge_send.at[0, b], merge_receive.at[0, b], {"tp": beside})

    def cross_copy(b):
        return remote(slab(2, b), slab(3, b), merge_send.at[1, b], merge_receive.at[1, b], {"tp": across})

    def final_copy(b):
        return remote(
            slab(2, b),
            slab(4, core),
            merge_send.at[1, b],
            final_receive.at[core],
            {"ctx": b * 2 + x, "tp": z},
        )

    def mine(slot):
        return pl.ds(pl.multiple_of(slot * tokens + core * half, half), half)

    def store(kind, b, data):
        held[line // 2 + kind, pl.ds(pl.multiple_of(b * half, half), half), :] = data

    def forward(b, direction):
        for h in range(2):
            line_copy(direction, b, h).wait_recv()

            @pl.when((z < line - 1) if direction == 0 else (z > 0))
            def _():
                line_copy(direction, b, h).start()

    def multiply(b, slot):
        block = held[b // 2, pl.ds(pl.multiple_of(b % 2 * tokens, tokens), tokens), :]
        for n in range(4):
            total[slot * tokens : (slot + 1) * tokens, n * CHUNK : (n + 1) * CHUNK] = jnp.dot(
                block, gate_tiles[3, n], preferred_element_type=jnp.float32
            )
        theirs = pl.ds(pl.multiple_of(slot * tokens + (1 - core) * half, half), half)
        store(0, b, total[theirs, :].astype(jnp.bfloat16))
        give_copy(b).start()

    def merge(b, slot):
        give_copy(b).wait_recv()
        joint = total[mine(slot), :] + slab(1, b)[...].astype(jnp.float32)

        @pl.when(side != z // 2)
        def _():
            store(2, b, joint.astype(jnp.bfloat16))
            cross_copy(b).start()

        @pl.when(side == z // 2)
        def _():
            total[mine(slot), :] = joint

    def deliver(b, slot):
        @pl.when(side == z // 2)
        def _():
            cross_copy(b).wait_recv()
            joint = (total[mine(slot), :] + slab(3, b)[...].astype(jnp.float32)).astype(jnp.bfloat16)
            stays = jnp.logical_and(b == z, tp == z)

            @pl.when(stays)
            def _():
                store(4, core, joint)

            @pl.when(jnp.logical_not(stays))
            def _():
                store(2, b, joint)
                final_copy(b).start()

    def each(step, action):
        if step == 0:
            action(z, 0)
            return

        @pl.when(z - step >= 0)
        def _():
            action(z - step, 0)

        @pl.when(z + step < line)
        def _():
            action(z + step, 1)

    for step in range(line):
        if step > 0:
            each(step, forward)
            each(step - 1, deliver)
        each(step, multiply)
        each(step, merge)
    each(line - 1, deliver)

    scale = stats_total(0)
    for h in range(2):

        @pl.when(jnp.logical_not(jnp.logical_and(z == tp, core == h)))
        def _():
            remote(
                slab(4, h), slab(4, h), merge_send.at[1, 0], final_receive.at[h], {"tp": beside}
            ).wait_recv()

    mixer_out = held[line // 2 + 4, :tokens, :].astype(jnp.float32) * scale
    hidden[...] = (residual[...].astype(jnp.float32) + mixer_out).astype(jnp.bfloat16)
    state = hidden[...].astype(jnp.float32)
    stats[1] = as_row(jnp.sum(state * state, axis=1, keepdims=True))
    for n in range(3):
        stats_copy(1, n).start()
    feed_scale = stats_total(1)
    expert_input[...] = (state * feed_scale * feed_gain[...]).astype(jnp.bfloat16)

    picked = jnp.dot(picker[...], expert_input[...], preferred_element_type=jnp.float32)
    packed[...] = picked[: peers * main].astype(jnp.bfloat16)
    tail = picked[peers * main :].astype(jnp.bfloat16)
    folded = jnp.zeros((peers * SUB, piece), jnp.float32)
    for part in range(fold):
        folded = folded + jnp.dot(
            refold(peers, extra, fold, part),
            tail[:, part * piece : (part + 1) * piece],
            preferred_element_type=jnp.float32,
        )
    packed_extra[...] = folded.astype(jnp.bfloat16)

    def travel(sources, targets, sign, base):
        copies = []
        for kind, (source, target) in enumerate(zip(sources, targets)):
            size = (main, SUB)[kind]
            for distance in range(1, peers):
                block = pl.ds(distance * size, size)
                copies.append(
                    remote(
                        source.at[block],
                        target.at[block],
                        home_send.at[base + kind, distance],
                        home_receive.at[base + kind, distance],
                        {"ctx": (ctx + sign * distance + peers) % peers},
                    )
                )
        return copies

    outward = travel((packed, packed_extra), (rows, rows_extra), 1, 0)
    for copy in outward:
        copy.start()
    rows[:main] = packed[:main]
    rows_extra[:SUB] = packed_extra[:SUB]
    for kind in range(2):
        for n in range(3):
            stats_copy(kind, n).wait_send()
    for b in range(line):

        @pl.when(jnp.logical_and(z < line - 1, b <= z))
        def _():
            for h in range(2):
                line_copy(0, b, h).wait_send()

        @pl.when(jnp.logical_and(z > 0, b >= z))
        def _():
            for h in range(2):
                line_copy(1, b, h).wait_send()

        give_copy(b).wait_send()

        @pl.when(side != z // 2)
        def _():
            cross_copy(b).wait_send()

        @pl.when(
            jnp.logical_and(side == z // 2, jnp.logical_not(jnp.logical_and(z == b, tp == z)))
        )
        def _():
            final_copy(b).wait_send()

    start_group([(0, 3), (2, 3)])
    for copy in outward:
        copy.wait_recv()
    landed = rows_extra[...]
    for part in range(fold):
        rows[peers * main :, part * piece : (part + 1) * piece] = jnp.dot(
            unfold(peers, extra, fold, part), landed, preferred_element_type=jnp.float32
        ).astype(jnp.bfloat16)

    def pair(kind, j, source, target, other):
        return remote(source, target, pair_send.at[kind, j], pair_receive.at[kind, j], {"tp": other})

    both = (gate_tiles, up_tiles)

    def product(which, place, j):
        tile(which, place, j).wait()
        return jnp.dot(rows[...], both[which][place, j], preferred_element_type=jnp.float32)

    def first_copy(which, j):
        return pair(which, j, first.at[which, j], first_in.at[which, j], beside)

    def far_copy(which, j):
        return pair(2 + which, j, far.at[which, j], far_in.at[which, j], across)

    def near_copy(which, j):
        return pair(4 + which, j, first.at[which, j], near_in.at[which, j], beside)

    def beside_copy(j):
        return pair(6, j, active.at[j], active_beside.at[j], beside)

    def across_copy(j):
        return pair(7, j, active.at[j], active_across.at[j], across)

    def diagonal_copy(j):
        return pair(8, j, active_across.at[j], active_diagonal.at[j], beside)

    def far_step(j, carry):
        for which in range(2):
            first[which, j] = product(which, 0, j).astype(jnp.bfloat16)
            first_copy(which, j).start()
        for which in range(2):
            mine = product(which, 1, j)
            first_copy(which, j).wait_recv()
            far[which, j] = (mine + first_in[which, j].astype(jnp.float32)).astype(jnp.bfloat16)
            far_copy(which, j).start()
        return carry

    lax.fori_loop(0, chunks, far_step, 0)

    def near_step(j, carry):
        for which in range(2):
            mine = product(which, 2, j).astype(jnp.bfloat16)
            first_copy(which, j).wait_send()
            first[which, j] = mine
            near_copy(which, j).start()
        return carry

    lax.fori_loop(0, chunks, near_step, 0)
    total[...] = jnp.zeros_like(total)

    def lowered(source, place, j):
        tile(2, place, j).wait()
        total[...] += jnp.dot(source[j], down_tiles[place, j], preferred_element_type=jnp.float32)

    def own_step(j, carry):
        sums = []
        for which in range(2):
            mine = product(which, 3, j).astype(jnp.bfloat16).astype(jnp.float32)
            near_copy(which, j).wait_recv()
            mine = mine + near_in[which, j].astype(jnp.float32)
            far_copy(which, j).wait_recv()
            sums.append(mine + far_in[which, j].astype(jnp.float32))
        active[j] = (jax.nn.silu(sums[0]) * sums[1]).astype(jnp.bfloat16)
        across_copy(j).start()
        beside_copy(j).start()
        lowered(active, 0, j)
        beside_copy(j).wait_recv()
        lowered(active_beside, 1, j)
        return carry

    lax.fori_loop(0, chunks, own_step, 0)

    def last_step(j, carry):
        across_copy(j).wait_recv()
        diagonal_copy(j).start()
        lowered(active_across, 2, j)
        diagonal_copy(j).wait_recv()
        lowered(active_diagonal, 3, j)
        return carry

    lax.fori_loop(0, chunks, last_step, 0)

    for copy in outward:
        copy.wait_send()
    packed[...] = total[: peers * main].astype(jnp.bfloat16)
    tail = total[peers * main :].astype(jnp.bfloat16)
    folded = jnp.zeros((peers * SUB, piece), jnp.float32)
    for part in range(fold):
        folded = folded + jnp.dot(
            refold(peers, extra, fold, part),
            tail[:, part * piece : (part + 1) * piece],
            preferred_element_type=jnp.float32,
        )
    packed_extra[...] = folded.astype(jnp.bfloat16)
    homeward = travel((packed, packed_extra), (answers, answers_extra), -1, 2)
    for copy in homeward:
        copy.start()
    answers[:main] = packed[:main]
    answers_extra[:SUB] = packed_extra[:SUB]

    def drain(j, carry):
        for which in range(2):
            far_copy(which, j).wait_send()
            near_copy(which, j).wait_send()
        beside_copy(j).wait_send()
        across_copy(j).wait_send()
        diagonal_copy(j).wait_send()
        return carry

    lax.fori_loop(0, chunks, drain, 0)
    for copy in homeward:
        copy.wait_recv()
    landed = answers_extra[...]
    for part in range(fold):
        answers[peers * main :, part * piece : (part + 1) * piece] = jnp.dot(
            unfold(peers, extra, fold, part), landed, preferred_element_type=jnp.float32
        ).astype(jnp.bfloat16)
    routed = jnp.dot(weights_high[...], answers[...], preferred_element_type=jnp.float32)
    routed = routed + jnp.dot(weights_low[...], answers[...], preferred_element_type=jnp.float32)
    out[...] = (hidden[...].astype(jnp.float32) + routed).astype(jnp.bfloat16)
    for copy in homeward:
        copy.wait_send()


def block_direct(
    gated, mixer_gain, residual, feed_gain, weights_out, expert_ids, expert_weights, gate, up, down
):
    peers = lax.axis_size("ctx")
    ctx = lax.axis_index("ctx")
    tokens, width = residual.shape
    hidden_width = gate.shape[2] // 4
    chunks = hidden_width // CHUNK
    main = CAP // SUB * SUB
    extra = CAP - main
    count = peers * CAP
    flat = expert_ids.reshape(-1)
    matches = (flat[:, None] == jnp.arange(EXPERTS)[None, :]).astype(jnp.int32)
    slots = jnp.sum((jnp.cumsum(matches, axis=0) - matches) * matches, axis=1)
    places = (flat - ctx) % EXPERTS
    targets = jnp.where(
        slots < main, places * main + slots, peers * main + places * extra + slots - main
    ).reshape(tokens, -1)
    chosen = targets[:, :, None] == jnp.arange(count)[None, None, :]
    weights = jnp.sum(jnp.where(chosen, expert_weights[:, :, None], 0.0), axis=1)
    weights_high = weights.astype(jnp.bfloat16)
    weights_low = (weights - weights_high.astype(jnp.float32)).astype(jnp.bfloat16)
    picker = jnp.any(
        targets[None, :, :] == jnp.arange(count)[:, None, None], axis=2
    ).astype(jnp.bfloat16)
    vmem = pl.BlockSpec(memory_space=pltpu.VMEM)
    anywhere = pl.BlockSpec(memory_space=pl.ANY)
    block = (chunks, count, CHUNK)
    low = jnp.bfloat16
    return pl.pallas_call(
        functools.partial(block_kernel, peers),
        out_shape=jax.ShapeDtypeStruct((tokens, width), low),
        in_specs=[vmem] * 7 + [anywhere] * 5,
        out_specs=vmem,
        scratch_shapes=[
            pltpu.VMEM((tokens, width), low),
            pltpu.VMEM((tokens, width), low),
            pltpu.VMEM((2, 8, tokens), jnp.float32),
            pltpu.VMEM((2, 3, 8, tokens), jnp.float32),
            pltpu.VMEM((4, chunks, width, CHUNK), low),
            pltpu.VMEM((4, chunks, width, CHUNK), low),
            pltpu.VMEM((4, chunks, CHUNK, width), low),
            pltpu.VMEM((peers * main, width), low),
            pltpu.VMEM((peers * SUB, width * extra // SUB), low),
            pltpu.VMEM((count, width), low),
            pltpu.VMEM((peers * SUB, width * extra // SUB), low),
            pltpu.VMEM((count, width), low),
            pltpu.VMEM((peers * SUB, width * extra // SUB), low),
            pltpu.VMEM((2,) + block, low),
            pltpu.VMEM((2,) + block, low),
            pltpu.VMEM((2,) + block, low),
            pltpu.VMEM((2,) + block, low),
            pltpu.VMEM((2,) + block, low),
            pltpu.VMEM(block, low),
            pltpu.VMEM(block, low),
            pltpu.VMEM(block, low),
            pltpu.VMEM(block, low),
            pltpu.VMEM((count, width), jnp.float32),
            pltpu.SemaphoreType.DMA((12, chunks)),
            pltpu.SemaphoreType.DMA((4,)),
            pltpu.SemaphoreType.DMA((2, peers // 2, 2)),
            pltpu.SemaphoreType.DMA((peers // 2, 2)),
            pltpu.SemaphoreType.DMA((2, peers // 2)),
            pltpu.SemaphoreType.DMA((2, peers // 2)),
            pltpu.SemaphoreType.DMA((2,)),
            pltpu.SemaphoreType.DMA((2, 3)),
            pltpu.SemaphoreType.DMA((2, 3)),
            pltpu.SemaphoreType.DMA((4, peers)),
            pltpu.SemaphoreType.DMA((4, peers)),
            pltpu.SemaphoreType.DMA((9, chunks)),
            pltpu.SemaphoreType.DMA((9, chunks)),
        ],
        compiler_params=pltpu.CompilerParams(
            collective_id=0, has_side_effects=True, vmem_limit_bytes=66_000_000
        ),
        name="block",
    )(
        gated,
        mixer_gain[None, :],
        residual,
        feed_gain[None, :],
        picker,
        weights_high,
        weights_low,
        weights_out[0],
        weights_out[1],
        gate,
        up,
        down,
    )


def body(
    residual,
    mixer_input,
    gate_input,
    state_proj,
    step_raw,
    conv_weight,
    conv_state_weight,
    step_bias,
    decay_log,
    skip_gain,
    mixer_gain,
    out_weight,
    feed_gain,
    expert_gate,
    expert_up,
    expert_down,
    expert_ids,
    expert_weights,
):
    tensor_count = lax.axis_size("tp")
    context_count = lax.axis_size("ctx")
    tokens = mixer_input.shape[0]
    channels = mixer_input.shape[1]
    states = state_proj.shape[1] // 2
    heads_local = step_raw.shape[1]
    head_size = channels // heads_local
    taps = conv_weight.shape[0]
    direct = context_count == EXPERTS
    if direct:
        weight_beyond = lax.ppermute(out_weight, "ctx", [(c, c ^ 1) for c in range(context_count)])
    joined = jnp.concatenate([mixer_input, state_proj], axis=1)
    previous = passed_along(joined[tokens - (taps - 1) :], "ctx", 1)
    kernel = jnp.concatenate([conv_weight, conv_state_weight], axis=1)
    filtered = causal_filter(previous.astype(jnp.float32), joined.astype(jnp.float32), kernel)
    values = filtered[:, :channels].reshape(tokens, heads_local, head_size)
    writer = filtered[:, channels : channels + states]
    reader = filtered[:, channels + states :]
    step_size = jax.nn.softplus(step_raw + step_bias[None, :])
    log_decay = -step_size * jnp.exp(decay_log)[None, :]
    inside, cumulative, fresh, tail = local_terms(values, writer, reader, step_size, log_decay)

    incoming = entering(jnp.repeat(jnp.exp(tail), head_size), fresh, "ctx")
    carried = (
        jnp.dot(reader, incoming, precision=lax.Precision.HIGHEST).reshape(values.shape)
        * jnp.exp(cumulative)[:, :, None]
    )
    mixed = inside + carried + skip_gain[None, :, None] * values
    gated = mixed.reshape(tokens, channels) * jax.nn.silu(gate_input.astype(jnp.float32))
    if direct:
        return block_direct(
            gated,
            mixer_gain,
            residual,
            feed_gain,
            (out_weight, weight_beyond),
            expert_ids,
            expert_weights,
            expert_gate,
            expert_up,
            expert_down,
        )
    tp_index = lax.axis_index("tp")
    core, chip = (tp_index % 2, tp_index // 2)
    scaled = (gated * mixer_gain[None, :]).astype(jnp.bfloat16)
    ctx_index = lax.axis_index("ctx")
    if direct:
        pairs = []
        for plane in range(4):
            block = rotated(scaled, 2 * plane) if plane else scaled
            other = lax.ppermute(block, "ctx", [(c, c ^ 1) for c in range(context_count)])
            pair = jnp.concatenate([block, other], axis=0)
            pairs.append(jnp.dot(pair, out_weight, preferred_element_type=jnp.float32))
        products = jnp.stack(pairs)

        def projected(quarter):
            place = (ctx_index // 2 - quarter) % 4
            return lax.dynamic_index_in_dim(products, place, 0, keepdims=False)

    else:
        everyone = lax.all_gather(scaled, "ctx", axis=0, tiled=True)
        span = everyone.shape[0] // tensor_count

        def projected(quarter):
            rows = lax.dynamic_slice_in_dim(everyone, quarter * span, span, 0)
            return jnp.dot(rows, out_weight, preferred_element_type=jnp.float32)

    square_sum = tensor_total(jnp.sum(gated * gated, axis=1))
    scale = lax.rsqrt(square_sum / (channels * tensor_count) + EPSILON)
    own, beside = (chip * 2 + core, chip * 2 + 1 - core)
    across, diagonal = ((1 - chip) * 2 + core, (1 - chip) * 2 + 1 - core)
    far = swapped(projected(diagonal).astype(jnp.bfloat16), 1)
    far = swapped((projected(across) + far.astype(jnp.float32)).astype(jnp.bfloat16), 2)
    near = swapped(projected(beside).astype(jnp.bfloat16), 1)
    reduced = projected(own) + near.astype(jnp.float32) + far.astype(jnp.float32)
    blocks = context_count // tensor_count
    reduced = reduced.astype(jnp.bfloat16).reshape(blocks, tokens, -1)
    pieces = []
    for j in range(blocks):
        moves = [
            (c * tensor_count + p, (p * blocks + (c + j) % blocks) * tensor_count + c // blocks)
            for c in range(context_count)
            for p in range(tensor_count)
        ]
        if direct:
            block = reduced[j]
        else:
            block = lax.dynamic_index_in_dim(reduced, (ctx_index + j) % blocks, 0, keepdims=False)
        pieces.append(lax.ppermute(block, ("ctx", "tp"), moves))
    stacked = jnp.stack(pieces)
    order = (ctx_index - jnp.arange(blocks)) % blocks
    if blocks == 2:
        first = ctx_index % 2 == 0
        mixer_out = jnp.concatenate(
            [jnp.where(first, pieces[0], pieces[1]), jnp.where(first, pieces[1], pieces[0])], axis=1
        )
    else:
        mixer_out = jnp.take(stacked, order, axis=0).transpose(1, 0, 2).reshape(tokens, -1)
    mixer_out = mixer_out.astype(jnp.float32) * scale[:, None]
    hidden_state = (residual.astype(jnp.float32) + mixer_out).astype(jnp.bfloat16)
    state_float = lax.optimization_barrier(hidden_state).astype(jnp.float32)
    width_total = hidden_state.shape[1] * tensor_count
    feed_sum = tensor_total(jnp.sum(state_float * state_float, axis=1))
    feed_scale = lax.rsqrt(feed_sum / width_total + EPSILON)
    expert_input = (state_float * feed_scale[:, None] * feed_gain[None, :]).astype(jnp.bfloat16)
    group = context_count // EXPERTS
    width_local = expert_input.shape[1]
    flat_experts = expert_ids.reshape(-1)
    matches = (flat_experts[:, None] == jnp.arange(EXPERTS)[None, :]).astype(jnp.int32)
    slots = jnp.sum((jnp.cumsum(matches, axis=0) - matches) * matches, axis=1)
    places = (flat_experts - ctx_index) % EXPERTS if direct else flat_experts
    targets = (places * CAP + slots).reshape(tokens, -1)
    picker = jnp.any(targets[None, :, :] == jnp.arange(EXPERTS * CAP)[:, None, None], axis=2)
    buffer = jnp.dot(
        picker.astype(jnp.bfloat16), expert_input, preferred_element_type=jnp.float32
    ).astype(jnp.bfloat16)
    outgoing = jnp.broadcast_to(
        buffer.reshape(EXPERTS, 1, CAP, width_local), (EXPERTS, group, CAP, width_local)
    )
    outgoing = outgoing.reshape(EXPERTS * group, CAP, width_local)
    gate_local = expert_gate[0]
    up_local = expert_up[0]
    down_local = expert_down[0]
    sources, items, depth = outgoing.shape
    if direct:
        flattened = jnp.concatenate(
            [outgoing[r] if r == 0 else rotated(outgoing[r], r) for r in range(sources)], axis=0
        )
    else:
        arrived = lax.all_to_all(outgoing, "ctx", split_axis=0, concat_axis=0, tiled=True)
        flattened = arrived.reshape(sources * items, depth)
    hidden = gate_local.shape[1] // tensor_count

    def product(source, weight, quarter):
        columns = lax.dynamic_slice_in_dim(weight, quarter * hidden, hidden, 1)
        return jnp.dot(source, columns, preferred_element_type=jnp.float32)

    fars, nears, rows = ([], [], flattened)
    for weight in (gate_local, up_local):
        far = product(rows, weight, diagonal).astype(jnp.bfloat16)
        far = swapped(far, 1)
        nears.append(swapped(product(rows, weight, beside).astype(jnp.bfloat16), 1))
        far = (product(rows, weight, across) + far.astype(jnp.float32)).astype(jnp.bfloat16)
        far, rows = lax.optimization_barrier((far, rows))
        fars.append(swapped(far, 2))
    gate_share, up_share = (
        product(rows, weight, own).astype(jnp.bfloat16).astype(jnp.float32)
        + near.astype(jnp.float32)
        + far.astype(jnp.float32)
        for weight, near, far in zip((gate_local, up_local), nears, fars)
    )
    share = (jax.nn.silu(gate_share) * up_share).astype(jnp.bfloat16)
    share_across = swapped(share, 2)
    share_beside = swapped(share, 1)

    def lowered(part, quarter):
        rows = lax.dynamic_slice_in_dim(down_local, quarter * hidden, hidden, 0)
        return jnp.dot(part, rows, preferred_element_type=jnp.float32)

    local = lowered(share, own) + lowered(share_beside, beside)
    local, share_across = lax.optimization_barrier((local, share_across))
    share_diagonal = swapped(share_across, 1)
    answer = (
        local
        + lowered(share_across, across)
        + lowered(share_diagonal, diagonal)
    ).astype(jnp.bfloat16)
    answer = answer.reshape(sources, items, depth)
    if direct:
        answers = jnp.stack(
            [answer[r] if r == 0 else rotated(answer[r], -r) for r in range(sources)]
        )
    else:
        answers = lax.all_to_all(answer, "ctx", split_axis=0, concat_axis=0, tiled=True)
    summed = jnp.sum(answers.reshape(EXPERTS, group, CAP, width_local), axis=1, dtype=jnp.float32)
    summed = summed.reshape(EXPERTS * CAP, width_local)
    chosen = jnp.take(summed, targets, axis=0)
    routed = jnp.sum(expert_weights[:, :, None] * chosen, axis=1)
    return (state_float + routed).astype(jnp.bfloat16)


def solution(mesh):
    placed = (
        P("ctx", "tp"),
        P("ctx", "tp"),
        P("ctx", "tp"),
        P("ctx", None),
        P("ctx", "tp"),
        P(None, "tp"),
        P(),
        P("tp"),
        P("tp"),
        P("tp"),
        P("tp"),
        P("tp", "ctx"),
        P("tp"),
        P("ctx", "tp", None),
        P("ctx", "tp", None),
        P("ctx", None, "tp"),
        P("ctx", None),
        P("ctx", None),
    )

    return jax.shard_map(
        body, mesh=mesh, in_specs=placed, out_specs=P("ctx", "tp"), check_vma=False
    )
```

```python
import functools

import jax
import jax.numpy as jnp
from jax import lax
from jax.experimental import pallas as pl
from jax.experimental.pallas import tpu as pltpu
from jax.sharding import PartitionSpec as P


EXPERTS = 8
CAP = 36


EPSILON = 1e-05


def passed_along(value, axis, steps):
    count = lax.axis_size(axis)
    first, last = (max(0, -steps), min(count, count - steps))
    return lax.ppermute(value, axis, [(source, source + steps) for source in range(first, last)])


def swapped(value, distance):
    return lax.ppermute(value, "tp", [(p, p ^ distance) for p in range(lax.axis_size("tp"))])


def rotated(value, steps):
    count = lax.axis_size("ctx")
    return lax.ppermute(value, "ctx", [(c, (c + steps) % count) for c in range(count)])


def tensor_total(value):
    return (value + swapped(value, 1)) + (swapped(value, 2) + swapped(value, 3))


def entering(decay, fresh, axis):
    peers, position = (lax.axis_size(axis), lax.axis_index(axis))
    packed = jnp.concatenate([fresh, decay[None, :]], axis=0).astype(jnp.bfloat16)
    if peers == EXPERTS:
        total, carry = (jnp.zeros_like(fresh), jnp.ones_like(decay)[None, :])
        for distance in range(1, peers):
            part = passed_along(packed, axis, distance).astype(jnp.float32)
            total = total + carry * part[:-1]
            carry = carry * part[-1:]
        return total
    everything = lax.all_gather(packed, axis).astype(jnp.float32)

    def step(k, before):
        part = everything[k]
        return jnp.where(k < position, part[-1:] * before + part[:-1], before)

    return lax.fori_loop(0, peers, step, jnp.zeros_like(fresh))


def causal_filter(previous, current, kernel):
    joined = jnp.concatenate([previous, current], axis=0)
    length = current.shape[0]
    total = jnp.zeros(current.shape, jnp.float32)
    for offset in range(kernel.shape[0]):
        total = total + kernel[offset][None, :] * joined[offset : offset + length]
    return jax.nn.silu(total)


def local_terms(values, writer, reader, step_size, log_decay):
    length = values.shape[0]
    cumulative = jnp.cumsum(log_decay, axis=0)
    scores = jnp.dot(reader, writer.T, precision=lax.Precision.HIGHEST)
    order = jnp.arange(length)
    causal = (order[:, None] >= order[None, :])[:, :, None]
    spans = cumulative[:, None, :] - cumulative[None, :, :]
    factor = jnp.where(causal, jnp.exp(jnp.where(causal, spans, 0.0)), 0.0)
    factor = factor * step_size[None, :, :] * scores[:, :, None]
    inside = jnp.einsum("tsh,shp->thp", factor, values, precision=lax.Precision.HIGHEST)
    tail = cumulative[length - 1]
    ending = jnp.exp(tail[None, :] - cumulative) * step_size
    weighted = (ending[:, :, None] * values).reshape(length, -1)
    fresh = jnp.dot(writer.T, weighted, precision=lax.Precision.HIGHEST)
    return (inside, cumulative, fresh, tail)


SUB = 16
CHUNK = 256
MESH = pl.DeviceIdType.MESH


def remote(source, target, send, receive, device):
    return pltpu.make_async_remote_copy(
        src_ref=source,
        dst_ref=target,
        send_sem=send,
        recv_sem=receive,
        device_id=device,
        device_id_type=MESH,
    )


def unfold(count, extra, fold, part):
    j = lax.broadcasted_iota(jnp.int32, (count * extra, count * SUB), 0)
    i = lax.broadcasted_iota(jnp.int32, (count * extra, count * SUB), 1)
    return (i == j * fold + part).astype(jnp.bfloat16)


def refold(count, extra, fold, part):
    j = lax.broadcasted_iota(jnp.int32, (count * SUB, count * extra), 1)
    i = lax.broadcasted_iota(jnp.int32, (count * SUB, count * extra), 0)
    return (i == j * fold + part).astype(jnp.bfloat16)


def block_kernel(
    peers,
    mixer_input,
    gate_input,
    state_proj,
    step_raw,
    conv_weight,
    conv_state_weight,
    step_bias,
    decay_log,
    skip_gain,
    mixer_gain,
    residual,
    feed_gain,
    expert_ids,
    expert_weights,
    weight_own,
    gate,
    up,
    down,
    out,
    hidden,
    expert_input,
    stats,
    stats_in,
    picker,
    weights_high,
    weights_low,
    edge_in,
    edge_state,
    edge_state_in,
    states_long,
    wide_state,
    wide_sums,
    wide_step,
    state_out,
    state_in,
    tail_out,
    tail_in,
    entering_state,
    logs,
    gate_tiles,
    up_tiles,
    down_tiles,
    packed,
    packed_extra,
    rows,
    rows_extra,
    answers,
    answers_extra,
    first,
    first_in,
    far,
    far_in,
    near_in,
    active,
    active_beside,
    active_across,
    active_diagonal,
    total,
    tile_sem,
    weight_sem,
    weight_send,
    weight_receive,
    edge_send,
    edge_receive,
    state_send,
    state_receive,
    line_send,
    line_receive,
    merge_send,
    merge_receive,
    final_receive,
    stats_send,
    stats_receive,
    home_send,
    home_receive,
    pair_send,
    pair_receive,
):
    ctx, tp = lax.axis_index("ctx"), lax.axis_index("tp")
    beside = tp + 1 - 2 * (tp % 2)
    across = (tp + 2) % 4
    diagonal = 3 - tp
    width = rows.shape[1]
    chunks = first.shape[1]
    hidden_width = chunks * CHUNK
    main = packed.shape[0] // peers
    extra = (rows.shape[0] - peers * main) // peers
    fold = SUB // extra
    piece = width // fold

    places = ((diagonal, across, beside, tp), (diagonal, across, beside, tp), (tp, beside, across, diagonal))

    def tile(kind, place, j):
        span = pl.ds(pl.multiple_of(places[kind][place] * hidden_width + j * CHUNK, CHUNK), CHUNK)
        source = (gate, up, down)[kind]
        source = source.at[0, span, :] if kind == 2 else source.at[0, :, span]
        target = (gate_tiles, up_tiles, down_tiles)[kind].at[place, j]
        return pltpu.make_async_copy(source, target, tile_sem.at[4 * kind + place, j])

    def start_group(chosen):
        def body(j, carry):
            for kind, place in chosen:
                tile(kind, place, j).start()
            return carry

        lax.fori_loop(0, chunks, body, 0)

    z, x = ctx // 2, ctx % 2
    core, side = tp % 2, tp // 2
    line = peers // 2
    tokens = residual.shape[0]
    half = tokens // 2
    held = down_tiles.at[3]

    def weight_copy(n):
        source = weight_own.at[:, pl.ds(n * CHUNK, CHUNK)]
        return pltpu.make_async_copy(source, gate_tiles.at[3, 2 * x + n], weight_sem.at[n])

    def weight_across(n):
        span = pl.ds(n // 2 * CHUNK, CHUNK)
        return remote(
            weight_own.at[span, pl.ds(n % 2 * CHUNK, CHUNK)],
            gate_tiles.at[3, 2 * x + n % 2, span, :],
            weight_send.at[n],
            weight_receive.at[n],
            {"ctx": ctx + 1 - 2 * x},
        )

    pieces = 2 * width // CHUNK
    for distance in range(peers):
        state_in[distance] = jnp.zeros(state_in.shape[1:], state_in.dtype)
        tail_in[distance] = jnp.zeros(tail_in.shape[1:], tail_in.dtype)
    edge_state[...] = jnp.zeros_like(edge_state)
    edge_state[:, : state_proj.shape[1]] = state_proj[tokens - SUB :, :]
    for n in range(2):
        weight_copy(n).start()
    start_group([(kind, place) for place in (0, 1) for kind in (0, 1)])
    start_group([(0, 2), (1, 2), (1, 3)])
    start_group([(2, place) for place in range(3)])

    barrier = pltpu.get_barrier_semaphore()
    for distance in range(1, peers):
        pl.semaphore_signal(
            barrier, inc=1, device_id={"ctx": (ctx + distance) % peers}, device_id_type=MESH
        )
    for other in (beside, across, diagonal):
        pl.semaphore_signal(barrier, inc=1, device_id={"tp": other}, device_id_type=MESH)

    @pl.when(z != tp)
    def _():
        pl.semaphore_signal(
            barrier, inc=1, device_id={"ctx": tp * 2 + x, "tp": beside}, device_id_type=MESH
        )

    def piece_of(b, h):
        return held.at[b // 2, pl.ds(pl.multiple_of(b % 2 * tokens + h * half, half), half), :]

    def slab(kind, b):
        return held.at[line // 2 + kind, pl.ds(pl.multiple_of(b * half, half), half), :]

    def as_row(column):
        return jnp.broadcast_to(column, (tokens, tokens)).T[:8]

    def as_column(row):
        return jnp.broadcast_to(row[:1], (tokens, tokens)).T[:, :1]

    def stats_copy(kind, n):
        other = (beside, across, diagonal)[n]
        return remote(
            stats.at[kind], stats_in.at[kind, n], stats_send.at[kind, n], stats_receive.at[kind, n], {"tp": other}
        )

    def stats_total(kind):
        for n in range(3):
            stats_copy(kind, n).wait_recv()
        row = (stats[kind] + stats_in[kind, 0]) + (stats_in[kind, 1] + stats_in[kind, 2])
        return lax.rsqrt(as_column(row) / (width * 4) + EPSILON)

    lanes = tokens
    states = state_proj.shape[1] // 2
    heads = step_raw.shape[1]
    slabs = width // lanes
    values = total.at[pl.ds(tokens + SUB, tokens)]
    exact = lax.Precision.HIGHEST
    total[8 : 8 + tokens, :] = mixer_input[...].astype(jnp.float32)
    states_long[8 : 8 + tokens, :] = state_proj[...].astype(jnp.float32)
    step_size = jax.nn.softplus(step_raw[...] + step_bias[...])
    log_decay = -step_size * jnp.exp(decay_log[...])
    row_index = lax.broadcasted_iota(jnp.int32, (tokens, tokens), 0)
    column_index = lax.broadcasted_iota(jnp.int32, (tokens, tokens), 1)
    causal = row_index >= column_index
    cumulative = jnp.dot(
        causal.astype(jnp.float32), log_decay, precision=exact, preferred_element_type=jnp.float32
    )
    wide_sums[...] = jnp.zeros_like(wide_sums)
    wide_step[...] = jnp.zeros_like(wide_step)
    wide_state[...] = jnp.zeros_like(wide_state)
    wide_sums[:, :heads] = cumulative
    wide_step[:, :heads] = step_size
    sums_row, step_row = wide_sums[...].T, wide_step[...].T
    tail_out[...] = jnp.broadcast_to(wide_sums[tokens - 1 :, :], tail_out.shape)

    kinds = lax.broadcasted_iota(jnp.int32, (tokens, EXPERTS), 1)
    named = [(expert_ids[:, k : k + 1] == kinds).astype(jnp.float32) for k in range(2)]
    before = jnp.dot(
        (row_index > column_index).astype(jnp.bfloat16),
        (named[0] + named[1]).astype(jnp.bfloat16),
        preferred_element_type=jnp.float32,
    )
    relative = ((kinds - ctx + peers) % peers).astype(jnp.float32)
    spots = jnp.where(
        before < main, relative * main + before, peers * main + relative * extra + before - main
    )
    targets = [jnp.sum(named[k] * spots, axis=1, keepdims=True) for k in range(2)]
    slot_row = lax.broadcasted_iota(jnp.int32, picker.shape, 0).astype(jnp.float32)
    slot_column = lax.broadcasted_iota(jnp.int32, weights_high.shape, 1).astype(jnp.float32)
    picked_rows = [as_row(target)[:1] for target in targets]
    picker[...] = (
        jnp.where(slot_row == picked_rows[0], 1.0, 0.0) + jnp.where(slot_row == picked_rows[1], 1.0, 0.0)
    ).astype(jnp.bfloat16)
    weights = jnp.where(slot_column == targets[0], expert_weights[:, 0:1], 0.0)
    weights = weights + jnp.where(slot_column == targets[1], expert_weights[:, 1:2], 0.0)
    high = weights.astype(jnp.bfloat16)
    weights_high[...] = high
    weights_low[...] = (weights - high.astype(jnp.float32)).astype(jnp.bfloat16)

    pl.semaphore_wait(barrier, peers - 1 + 3 + jnp.where(z == beside, line - 1, 0))

    def edge_copies():
        device = {"ctx": (ctx + 1) % peers}
        return (
            remote(
                mixer_input.at[pl.ds(tokens - SUB, SUB), :], edge_in, edge_send.at[0], edge_receive.at[0], device
            ),
            remote(edge_state, edge_state_in, edge_send.at[1], edge_receive.at[1], device),
        )

    @pl.when(ctx < peers - 1)
    def _():
        for copy in edge_copies():
            copy.start()

    for n in range(2):
        weight_across(n).start()

    @pl.when(ctx > 0)
    def _():
        for copy in edge_copies():
            copy.wait_recv()
        total[:8, :] = edge_in[...].astype(jnp.float32)[8:]
        states_long[:8, :] = edge_state_in[...].astype(jnp.float32)[8:, : 2 * states]

    @pl.when(ctx == 0)
    def _():
        total[:8, :] = jnp.zeros((8, width), jnp.float32)
        states_long[:8, :] = jnp.zeros((8, 2 * states), jnp.float32)

    taps = conv_weight.shape[0]
    base = 8 - (taps - 1)
    filtered = jnp.zeros((tokens, 2 * states), jnp.float32)
    for tap in range(taps):
        filtered = filtered + conv_state_weight[tap : tap + 1, :] * states_long[base + tap : base + tap + tokens, :]
    wide_state[:, : 2 * states] = jax.nn.silu(filtered)
    state_rows = wide_state[...].T
    writer_rows = state_rows[:states]
    ending = jnp.exp(wide_sums[tokens - 1 :, :] - wide_sums[...]) * wide_step[...]
    left = lax.broadcasted_iota(jnp.int32, (tokens, lanes), 1) < lanes // 2

    def widened(narrow, i):
        return jnp.where(left, narrow[:, 2 * i : 2 * i + 1], narrow[:, 2 * i + 1 : 2 * i + 2])

    for i in range(slabs):
        slab_of = slice(i * lanes, (i + 1) * lanes)
        value = jnp.zeros((tokens, lanes), jnp.float32)
        for tap in range(taps):
            value = value + conv_weight[tap : tap + 1, slab_of] * total[base + tap : base + tap + tokens, slab_of]
        value = jax.nn.silu(value)
        values[:, slab_of] = value
        state_out[:, slab_of] = jnp.dot(
            writer_rows, widened(ending, i) * value, precision=exact, preferred_element_type=jnp.float32
        ).astype(jnp.bfloat16)

    def state_copies(distance):
        device = {"ctx": (ctx + distance) % peers}
        return (
            remote(
                state_out, state_in.at[distance], state_send.at[0, distance], state_receive.at[0, distance], device
            ),
            remote(
                tail_out, tail_in.at[distance], state_send.at[1, distance], state_receive.at[1, distance], device
            ),
        )

    for distance in range(peers - 1, 0, -1):

        @pl.when(ctx + distance < peers)
        def _():
            for copy in state_copies(distance):
                copy.start()

    for n in range(2, pieces):
        weight_across(n).start()
    scores = jnp.dot(
        wide_state[:, states : 2 * states], writer_rows, precision=exact, preferred_element_type=jnp.float32
    )
    for i in range(slabs):
        slab_of = slice(i * lanes, (i + 1) * lanes)
        factors = []
        for head in (2 * i, 2 * i + 1):
            spans = wide_sums[:, head : head + 1] - sums_row[head : head + 1, :]
            factors.append(
                jnp.exp(jnp.where(causal, spans, -1e30)) * (step_row[head : head + 1, :] * scores)
            )
        value = values[:, slab_of]
        halves = jnp.concatenate([jnp.where(left, value, 0.0), jnp.where(left, 0.0, value)], axis=0)
        inside = jnp.dot(
            jnp.concatenate(factors, axis=1).astype(jnp.bfloat16),
            halves.astype(jnp.bfloat16),
            preferred_element_type=jnp.float32,
        )
        total[:tokens, slab_of] = inside + widened(skip_gain, i) * value

    for distance in range(1, peers):

        @pl.when(ctx - distance >= 0)
        def _():
            for copy in state_copies(distance):
                copy.wait_recv()

    logs[...] = jnp.zeros_like(logs)
    running = jnp.zeros((1, tokens), jnp.float32)
    for distance in range(1, peers):
        logs[distance - 1 : distance, :] = running
        running = running + tail_in[distance][:1]
    spread = (
        lax.broadcasted_iota(jnp.int32, (lanes, width), 1) // (width // heads)
        == lax.broadcasted_iota(jnp.int32, (lanes, width), 0)
    ).astype(jnp.float32)
    carries = jnp.dot(jnp.exp(logs[...]), spread, precision=exact, preferred_element_type=jnp.float32)
    arrived = jnp.zeros((states, width), jnp.float32)
    for distance in range(1, peers):
        arrived = arrived + carries[distance - 1 : distance, :] * state_in[distance].astype(jnp.float32)
    entering_state[:states, :] = jnp.zeros((states, width), jnp.float32)
    entering_state[states:, :] = arrived
    growth = jnp.exp(wide_sums[...])
    squares = jnp.zeros((tokens, lanes), jnp.float32)
    for i in range(slabs):
        slab_of = slice(i * lanes, (i + 1) * lanes)
        carried = jnp.dot(
            wide_state[:, : 2 * states],
            entering_state[:, slab_of],
            precision=exact,
            preferred_element_type=jnp.float32,
        )
        mixed = total[:tokens, slab_of] + carried * widened(growth, i)
        value = mixed * jax.nn.silu(gate_input[:, slab_of].astype(jnp.float32))
        squares = squares + value * value
        held[z // 2, pl.ds(pl.multiple_of(z % 2 * tokens, tokens), tokens), slab_of] = (
            value * mixer_gain[:, slab_of]
        ).astype(jnp.bfloat16)
    stats[0] = as_row(jnp.sum(squares, axis=1, keepdims=True))

    def line_copy(direction, b, h):
        return remote(
            piece_of(b, h),
            piece_of(b, h),
            line_send.at[direction, b, h],
            line_receive.at[b, h],
            {"ctx": (ctx + 2 - 4 * direction + peers) % peers},
        )

    for h in range(2):

        @pl.when(z < line - 1)
        def _():
            line_copy(0, z, h).start()

        @pl.when(z > 0)
        def _():
            line_copy(1, z, h).start()

    for n in range(3):
        stats_copy(0, n).start()
    for n in range(2):
        weight_copy(n).wait()
    for n in range(pieces):
        weight_across(n).wait_recv()

    def give_copy(b):
        return remote(slab(0, b), slab(1, b), merge_send.at[0, b], merge_receive.at[0, b], {"tp": beside})

    def cross_copy(b):
        return remote(slab(2, b), slab(3, b), merge_send.at[1, b], merge_receive.at[1, b], {"tp": across})

    def final_copy(b):
        return remote(
            slab(2, b),
            slab(4, core),
            merge_send.at[1, b],
            final_receive.at[core],
            {"ctx": b * 2 + x, "tp": z},
        )

    def mine(slot):
        return pl.ds(pl.multiple_of(slot * tokens + core * half, half), half)

    def store(kind, b, data):
        held[line // 2 + kind, pl.ds(pl.multiple_of(b * half, half), half), :] = data

    def forward(b, direction):
        for h in range(2):
            line_copy(direction, b, h).wait_recv()

            @pl.when((z < line - 1) if direction == 0 else (z > 0))
            def _():
                line_copy(direction, b, h).start()

    def multiply(b, slot):
        block = held[b // 2, pl.ds(pl.multiple_of(b % 2 * tokens, tokens), tokens), :]
        for n in range(4):
            total[slot * tokens : (slot + 1) * tokens, n * CHUNK : (n + 1) * CHUNK] = jnp.dot(
                block, gate_tiles[3, n], preferred_element_type=jnp.float32
            )
        theirs = pl.ds(pl.multiple_of(slot * tokens + (1 - core) * half, half), half)
        store(0, b, total[theirs, :].astype(jnp.bfloat16))
        give_copy(b).start()

    def merge(b, slot):
        give_copy(b).wait_recv()
        joint = total[mine(slot), :] + slab(1, b)[...].astype(jnp.float32)

        @pl.when(side != z // 2)
        def _():
            store(2, b, joint.astype(jnp.bfloat16))
            cross_copy(b).start()

        @pl.when(side == z // 2)
        def _():
            total[mine(slot), :] = joint

    def deliver(b, slot):
        @pl.when(side == z // 2)
        def _():
            cross_copy(b).wait_recv()
            joint = (total[mine(slot), :] + slab(3, b)[...].astype(jnp.float32)).astype(jnp.bfloat16)
            stays = jnp.logical_and(b == z, tp == z)

            @pl.when(stays)
            def _():
                store(4, core, joint)

            @pl.when(jnp.logical_not(stays))
            def _():
                store(2, b, joint)
                final_copy(b).start()

    def each(step, action):
        if step == 0:
            action(z, 0)
            return

        @pl.when(z - step >= 0)
        def _():
            action(z - step, 0)

        @pl.when(z + step < line)
        def _():
            action(z + step, 1)

    for step in range(line):
        if step > 0:
            each(step, forward)
            each(step - 1, deliver)
        each(step, multiply)
        each(step, merge)
    each(line - 1, deliver)

    scale = stats_total(0)
    for h in range(2):

        @pl.when(jnp.logical_not(jnp.logical_and(z == tp, core == h)))
        def _():
            remote(
                slab(4, h), slab(4, h), merge_send.at[1, 0], final_receive.at[h], {"tp": beside}
            ).wait_recv()

    mixer_out = held[line // 2 + 4, :tokens, :].astype(jnp.float32) * scale
    hidden[...] = (residual[...].astype(jnp.float32) + mixer_out).astype(jnp.bfloat16)
    state = hidden[...].astype(jnp.float32)
    stats[1] = as_row(jnp.sum(state * state, axis=1, keepdims=True))
    for n in range(3):
        stats_copy(1, n).start()
    feed_scale = stats_total(1)
    expert_input[...] = (state * feed_scale * feed_gain[...]).astype(jnp.bfloat16)

    picked = jnp.dot(picker[...], expert_input[...], preferred_element_type=jnp.float32)
    packed[...] = picked[: peers * main].astype(jnp.bfloat16)
    tail = picked[peers * main :].astype(jnp.bfloat16)
    folded = jnp.zeros((peers * SUB, piece), jnp.float32)
    for part in range(fold):
        folded = folded + jnp.dot(
            refold(peers, extra, fold, part),
            tail[:, part * piece : (part + 1) * piece],
            preferred_element_type=jnp.float32,
        )
    packed_extra[...] = folded.astype(jnp.bfloat16)

    def travel(sources, targets, sign, base):
        copies = []
        for kind, (source, target) in enumerate(zip(sources, targets)):
            size = (main, SUB)[kind]
            for distance in range(1, peers):
                block = pl.ds(distance * size, size)
                copies.append(
                    remote(
                        source.at[block],
                        target.at[block],
                        home_send.at[base + kind, distance],
                        home_receive.at[base + kind, distance],
                        {"ctx": (ctx + sign * distance + peers) % peers},
                    )
                )
        return copies

    outward = travel((packed, packed_extra), (rows, rows_extra), 1, 0)
    for copy in outward:
        copy.start()
    rows[:main] = packed[:main]
    rows_extra[:SUB] = packed_extra[:SUB]
    for kind in range(2):
        for n in range(3):
            stats_copy(kind, n).wait_send()
    for n in range(pieces):
        weight_across(n).wait_send()

    @pl.when(ctx < peers - 1)
    def _():
        for copy in edge_copies():
            copy.wait_send()

    for distance in range(1, peers):

        @pl.when(ctx + distance < peers)
        def _():
            for copy in state_copies(distance):
                copy.wait_send()

    for b in range(line):

        @pl.when(jnp.logical_and(z < line - 1, b <= z))
        def _():
            for h in range(2):
                line_copy(0, b, h).wait_send()

        @pl.when(jnp.logical_and(z > 0, b >= z))
        def _():
            for h in range(2):
                line_copy(1, b, h).wait_send()

        give_copy(b).wait_send()

        @pl.when(side != z // 2)
        def _():
            cross_copy(b).wait_send()

        @pl.when(
            jnp.logical_and(side == z // 2, jnp.logical_not(jnp.logical_and(z == b, tp == z)))
        )
        def _():
            final_copy(b).wait_send()

    start_group([(0, 3), (2, 3)])
    for copy in outward:
        copy.wait_recv()
    landed = rows_extra[...]
    for part in range(fold):
        rows[peers * main :, part * piece : (part + 1) * piece] = jnp.dot(
            unfold(peers, extra, fold, part), landed, preferred_element_type=jnp.float32
        ).astype(jnp.bfloat16)

    def pair(kind, j, source, target, other):
        return remote(source, target, pair_send.at[kind, j], pair_receive.at[kind, j], {"tp": other})

    both = (gate_tiles, up_tiles)

    def product(which, place, j):
        tile(which, place, j).wait()
        return jnp.dot(rows[...], both[which][place, j], preferred_element_type=jnp.float32)

    def first_copy(which, j):
        return pair(which, j, first.at[which, j], first_in.at[which, j], beside)

    def far_copy(which, j):
        return pair(2 + which, j, far.at[which, j], far_in.at[which, j], across)

    def near_copy(which, j):
        return pair(4 + which, j, first.at[which, j], near_in.at[which, j], beside)

    def beside_copy(j):
        return pair(6, j, active.at[j], active_beside.at[j], beside)

    def across_copy(j):
        return pair(7, j, active.at[j], active_across.at[j], across)

    def diagonal_copy(j):
        return pair(8, j, active_across.at[j], active_diagonal.at[j], beside)

    def far_step(j, carry):
        for which in range(2):
            first[which, j] = product(which, 0, j).astype(jnp.bfloat16)
            first_copy(which, j).start()
        for which in range(2):
            mine = product(which, 1, j)
            first_copy(which, j).wait_recv()
            far[which, j] = (mine + first_in[which, j].astype(jnp.float32)).astype(jnp.bfloat16)
            far_copy(which, j).start()
        return carry

    lax.fori_loop(0, chunks, far_step, 0)

    def near_step(j, carry):
        for which in range(2):
            mine = product(which, 2, j).astype(jnp.bfloat16)
            first_copy(which, j).wait_send()
            first[which, j] = mine
            near_copy(which, j).start()
        return carry

    lax.fori_loop(0, chunks, near_step, 0)
    total[...] = jnp.zeros_like(total)

    def lowered(source, place, j):
        tile(2, place, j).wait()
        total[...] += jnp.dot(source[j], down_tiles[place, j], preferred_element_type=jnp.float32)

    def own_step(j, carry):
        sums = []
        for which in range(2):
            mine = product(which, 3, j).astype(jnp.bfloat16).astype(jnp.float32)
            near_copy(which, j).wait_recv()
            mine = mine + near_in[which, j].astype(jnp.float32)
            far_copy(which, j).wait_recv()
            sums.append(mine + far_in[which, j].astype(jnp.float32))
        active[j] = (jax.nn.silu(sums[0]) * sums[1]).astype(jnp.bfloat16)
        across_copy(j).start()
        beside_copy(j).start()
        lowered(active, 0, j)
        beside_copy(j).wait_recv()
        lowered(active_beside, 1, j)
        return carry

    lax.fori_loop(0, chunks, own_step, 0)

    def last_step(j, carry):
        across_copy(j).wait_recv()
        diagonal_copy(j).start()
        lowered(active_across, 2, j)
        diagonal_copy(j).wait_recv()
        lowered(active_diagonal, 3, j)
        return carry

    lax.fori_loop(0, chunks, last_step, 0)

    for copy in outward:
        copy.wait_send()
    packed[...] = total[: peers * main].astype(jnp.bfloat16)
    tail = total[peers * main :].astype(jnp.bfloat16)
    folded = jnp.zeros((peers * SUB, piece), jnp.float32)
    for part in range(fold):
        folded = folded + jnp.dot(
            refold(peers, extra, fold, part),
            tail[:, part * piece : (part + 1) * piece],
            preferred_element_type=jnp.float32,
        )
    packed_extra[...] = folded.astype(jnp.bfloat16)
    homeward = travel((packed, packed_extra), (answers, answers_extra), -1, 2)
    for copy in homeward:
        copy.start()
    answers[:main] = packed[:main]
    answers_extra[:SUB] = packed_extra[:SUB]

    def drain(j, carry):
        for which in range(2):
            far_copy(which, j).wait_send()
            near_copy(which, j).wait_send()
        beside_copy(j).wait_send()
        across_copy(j).wait_send()
        diagonal_copy(j).wait_send()
        return carry

    lax.fori_loop(0, chunks, drain, 0)
    for copy in homeward:
        copy.wait_recv()
    landed = answers_extra[...]
    for part in range(fold):
        answers[peers * main :, part * piece : (part + 1) * piece] = jnp.dot(
            unfold(peers, extra, fold, part), landed, preferred_element_type=jnp.float32
        ).astype(jnp.bfloat16)
    routed = jnp.dot(weights_high[...], answers[...], preferred_element_type=jnp.float32)
    routed = routed + jnp.dot(weights_low[...], answers[...], preferred_element_type=jnp.float32)
    out[...] = (hidden[...].astype(jnp.float32) + routed).astype(jnp.bfloat16)
    for copy in homeward:
        copy.wait_send()


def block_direct(
    residual,
    mixer_input,
    gate_input,
    state_proj,
    step_raw,
    conv_weight,
    conv_state_weight,
    step_bias,
    decay_log,
    skip_gain,
    mixer_gain,
    out_weight,
    feed_gain,
    gate,
    up,
    down,
    expert_ids,
    expert_weights,
):
    peers = lax.axis_size("ctx")
    tokens, width = residual.shape
    states = state_proj.shape[1] // 2
    chunks = gate.shape[2] // 4 // CHUNK
    extra = CAP - CAP // SUB * SUB
    main = CAP - extra
    count = peers * CAP
    vmem = pl.BlockSpec(memory_space=pltpu.VMEM)
    anywhere = pl.BlockSpec(memory_space=pl.ANY)
    block = (chunks, count, CHUNK)
    low = jnp.bfloat16
    return pl.pallas_call(
        functools.partial(block_kernel, peers),
        out_shape=jax.ShapeDtypeStruct((tokens, width), low),
        in_specs=[vmem] * 14 + [anywhere] * 4,
        out_specs=vmem,
        scratch_shapes=[
            pltpu.VMEM((tokens, width), low),
            pltpu.VMEM((tokens, width), low),
            pltpu.VMEM((2, 8, tokens), jnp.float32),
            pltpu.VMEM((2, 3, 8, tokens), jnp.float32),
            pltpu.VMEM((count, tokens), low),
            pltpu.VMEM((tokens, count), low),
            pltpu.VMEM((tokens, count), low),
            pltpu.VMEM((SUB, width), low),
            pltpu.VMEM((SUB, tokens), low),
            pltpu.VMEM((SUB, tokens), low),
            pltpu.VMEM((8 + tokens, 2 * states), jnp.float32),
            pltpu.VMEM((tokens, tokens), jnp.float32),
            pltpu.VMEM((tokens, tokens), jnp.float32),
            pltpu.VMEM((tokens, tokens), jnp.float32),
            pltpu.VMEM((states, width), low),
            pltpu.VMEM((peers, states, width), low),
            pltpu.VMEM((8, tokens), jnp.float32),
            pltpu.VMEM((peers, 8, tokens), jnp.float32),
            pltpu.VMEM((2 * states, width), jnp.float32),
            pltpu.VMEM((8, tokens), jnp.float32),
            pltpu.VMEM((4, chunks, width, CHUNK), low),
            pltpu.VMEM((4, chunks, width, CHUNK), low),
            pltpu.VMEM((4, chunks, CHUNK, width), low),
            pltpu.VMEM((peers * main, width), low),
            pltpu.VMEM((peers * SUB, width * extra // SUB), low),
            pltpu.VMEM((count, width), low),
            pltpu.VMEM((peers * SUB, width * extra // SUB), low),
            pltpu.VMEM((count, width), low),
            pltpu.VMEM((peers * SUB, width * extra // SUB), low),
            pltpu.VMEM((2,) + block, low),
            pltpu.VMEM((2,) + block, low),
            pltpu.VMEM((2,) + block, low),
            pltpu.VMEM((2,) + block, low),
            pltpu.VMEM((2,) + block, low),
            pltpu.VMEM(block, low),
            pltpu.VMEM(block, low),
            pltpu.VMEM(block, low),
            pltpu.VMEM(block, low),
            pltpu.VMEM((count, width), jnp.float32),
            pltpu.SemaphoreType.DMA((12, chunks)),
            pltpu.SemaphoreType.DMA((2,)),
            pltpu.SemaphoreType.DMA((2 * width // CHUNK,)),
            pltpu.SemaphoreType.DMA((2 * width // CHUNK,)),
            pltpu.SemaphoreType.DMA((2,)),
            pltpu.SemaphoreType.DMA((2,)),
            pltpu.SemaphoreType.DMA((2, peers)),
            pltpu.SemaphoreType.DMA((2, peers)),
            pltpu.SemaphoreType.DMA((2, peers // 2, 2)),
            pltpu.SemaphoreType.DMA((peers // 2, 2)),
            pltpu.SemaphoreType.DMA((2, peers // 2)),
            pltpu.SemaphoreType.DMA((2, peers // 2)),
            pltpu.SemaphoreType.DMA((2,)),
            pltpu.SemaphoreType.DMA((2, 3)),
            pltpu.SemaphoreType.DMA((2, 3)),
            pltpu.SemaphoreType.DMA((4, peers)),
            pltpu.SemaphoreType.DMA((4, peers)),
            pltpu.SemaphoreType.DMA((9, chunks)),
            pltpu.SemaphoreType.DMA((9, chunks)),
        ],
        compiler_params=pltpu.CompilerParams(
            collective_id=0, has_side_effects=True, vmem_limit_bytes=66_000_000
        ),
        name="block",
    )(
        mixer_input,
        gate_input,
        state_proj,
        step_raw,
        conv_weight,
        conv_state_weight,
        step_bias[None, :],
        decay_log[None, :],
        skip_gain[None, :],
        mixer_gain[None, :],
        residual,
        feed_gain[None, :],
        expert_ids,
        expert_weights,
        out_weight,
        gate,
        up,
        down,
    )


def body(
    residual,
    mixer_input,
    gate_input,
    state_proj,
    step_raw,
    conv_weight,
    conv_state_weight,
    step_bias,
    decay_log,
    skip_gain,
    mixer_gain,
    out_weight,
    feed_gain,
    expert_gate,
    expert_up,
    expert_down,
    expert_ids,
    expert_weights,
):
    tensor_count = lax.axis_size("tp")
    context_count = lax.axis_size("ctx")
    tokens = mixer_input.shape[0]
    channels = mixer_input.shape[1]
    states = state_proj.shape[1] // 2
    heads_local = step_raw.shape[1]
    head_size = channels // heads_local
    taps = conv_weight.shape[0]
    direct = context_count == EXPERTS
    joined = jnp.concatenate([mixer_input, state_proj], axis=1)
    previous = passed_along(joined[tokens - (taps - 1) :], "ctx", 1)
    kernel = jnp.concatenate([conv_weight, conv_state_weight], axis=1)
    filtered = causal_filter(previous.astype(jnp.float32), joined.astype(jnp.float32), kernel)
    values = filtered[:, :channels].reshape(tokens, heads_local, head_size)
    writer = filtered[:, channels : channels + states]
    reader = filtered[:, channels + states :]
    step_size = jax.nn.softplus(step_raw + step_bias[None, :])
    log_decay = -step_size * jnp.exp(decay_log)[None, :]
    inside, cumulative, fresh, tail = local_terms(values, writer, reader, step_size, log_decay)

    incoming = entering(jnp.repeat(jnp.exp(tail), head_size), fresh, "ctx")
    carried = (
        jnp.dot(reader, incoming, precision=lax.Precision.HIGHEST).reshape(values.shape)
        * jnp.exp(cumulative)[:, :, None]
    )
    mixed = inside + carried + skip_gain[None, :, None] * values
    gated = mixed.reshape(tokens, channels) * jax.nn.silu(gate_input.astype(jnp.float32))
    tp_index = lax.axis_index("tp")
    core, chip = (tp_index % 2, tp_index // 2)
    scaled = (gated * mixer_gain[None, :]).astype(jnp.bfloat16)
    ctx_index = lax.axis_index("ctx")
    if direct:
        pairs = []
        for plane in range(4):
            block = rotated(scaled, 2 * plane) if plane else scaled
            other = lax.ppermute(block, "ctx", [(c, c ^ 1) for c in range(context_count)])
            pair = jnp.concatenate([block, other], axis=0)
            pairs.append(jnp.dot(pair, out_weight, preferred_element_type=jnp.float32))
        products = jnp.stack(pairs)

        def projected(quarter):
            place = (ctx_index // 2 - quarter) % 4
            return lax.dynamic_index_in_dim(products, place, 0, keepdims=False)

    else:
        everyone = lax.all_gather(scaled, "ctx", axis=0, tiled=True)
        span = everyone.shape[0] // tensor_count

        def projected(quarter):
            rows = lax.dynamic_slice_in_dim(everyone, quarter * span, span, 0)
            return jnp.dot(rows, out_weight, preferred_element_type=jnp.float32)

    square_sum = tensor_total(jnp.sum(gated * gated, axis=1))
    scale = lax.rsqrt(square_sum / (channels * tensor_count) + EPSILON)
    own, beside = (chip * 2 + core, chip * 2 + 1 - core)
    across, diagonal = ((1 - chip) * 2 + core, (1 - chip) * 2 + 1 - core)
    far = swapped(projected(diagonal).astype(jnp.bfloat16), 1)
    far = swapped((projected(across) + far.astype(jnp.float32)).astype(jnp.bfloat16), 2)
    near = swapped(projected(beside).astype(jnp.bfloat16), 1)
    reduced = projected(own) + near.astype(jnp.float32) + far.astype(jnp.float32)
    blocks = context_count // tensor_count
    reduced = reduced.astype(jnp.bfloat16).reshape(blocks, tokens, -1)
    pieces = []
    for j in range(blocks):
        moves = [
            (c * tensor_count + p, (p * blocks + (c + j) % blocks) * tensor_count + c // blocks)
            for c in range(context_count)
            for p in range(tensor_count)
        ]
        if direct:
            block = reduced[j]
        else:
            block = lax.dynamic_index_in_dim(reduced, (ctx_index + j) % blocks, 0, keepdims=False)
        pieces.append(lax.ppermute(block, ("ctx", "tp"), moves))
    stacked = jnp.stack(pieces)
    order = (ctx_index - jnp.arange(blocks)) % blocks
    if blocks == 2:
        first = ctx_index % 2 == 0
        mixer_out = jnp.concatenate(
            [jnp.where(first, pieces[0], pieces[1]), jnp.where(first, pieces[1], pieces[0])], axis=1
        )
    else:
        mixer_out = jnp.take(stacked, order, axis=0).transpose(1, 0, 2).reshape(tokens, -1)
    mixer_out = mixer_out.astype(jnp.float32) * scale[:, None]
    hidden_state = (residual.astype(jnp.float32) + mixer_out).astype(jnp.bfloat16)
    state_float = lax.optimization_barrier(hidden_state).astype(jnp.float32)
    width_total = hidden_state.shape[1] * tensor_count
    feed_sum = tensor_total(jnp.sum(state_float * state_float, axis=1))
    feed_scale = lax.rsqrt(feed_sum / width_total + EPSILON)
    expert_input = (state_float * feed_scale[:, None] * feed_gain[None, :]).astype(jnp.bfloat16)
    group = context_count // EXPERTS
    width_local = expert_input.shape[1]
    flat_experts = expert_ids.reshape(-1)
    matches = (flat_experts[:, None] == jnp.arange(EXPERTS)[None, :]).astype(jnp.int32)
    slots = jnp.sum((jnp.cumsum(matches, axis=0) - matches) * matches, axis=1)
    places = (flat_experts - ctx_index) % EXPERTS if direct else flat_experts
    targets = (places * CAP + slots).reshape(tokens, -1)
    picker = jnp.any(targets[None, :, :] == jnp.arange(EXPERTS * CAP)[:, None, None], axis=2)
    buffer = jnp.dot(
        picker.astype(jnp.bfloat16), expert_input, preferred_element_type=jnp.float32
    ).astype(jnp.bfloat16)
    outgoing = jnp.broadcast_to(
        buffer.reshape(EXPERTS, 1, CAP, width_local), (EXPERTS, group, CAP, width_local)
    )
    outgoing = outgoing.reshape(EXPERTS * group, CAP, width_local)
    gate_local = expert_gate[0]
    up_local = expert_up[0]
    down_local = expert_down[0]
    sources, items, depth = outgoing.shape
    if direct:
        flattened = jnp.concatenate(
            [outgoing[r] if r == 0 else rotated(outgoing[r], r) for r in range(sources)], axis=0
        )
    else:
        arrived = lax.all_to_all(outgoing, "ctx", split_axis=0, concat_axis=0, tiled=True)
        flattened = arrived.reshape(sources * items, depth)
    hidden = gate_local.shape[1] // tensor_count

    def product(source, weight, quarter):
        columns = lax.dynamic_slice_in_dim(weight, quarter * hidden, hidden, 1)
        return jnp.dot(source, columns, preferred_element_type=jnp.float32)

    fars, nears, rows = ([], [], flattened)
    for weight in (gate_local, up_local):
        far = product(rows, weight, diagonal).astype(jnp.bfloat16)
        far = swapped(far, 1)
        nears.append(swapped(product(rows, weight, beside).astype(jnp.bfloat16), 1))
        far = (product(rows, weight, across) + far.astype(jnp.float32)).astype(jnp.bfloat16)
        far, rows = lax.optimization_barrier((far, rows))
        fars.append(swapped(far, 2))
    gate_share, up_share = (
        product(rows, weight, own).astype(jnp.bfloat16).astype(jnp.float32)
        + near.astype(jnp.float32)
        + far.astype(jnp.float32)
        for weight, near, far in zip((gate_local, up_local), nears, fars)
    )
    share = (jax.nn.silu(gate_share) * up_share).astype(jnp.bfloat16)
    share_across = swapped(share, 2)
    share_beside = swapped(share, 1)

    def lowered(part, quarter):
        rows = lax.dynamic_slice_in_dim(down_local, quarter * hidden, hidden, 0)
        return jnp.dot(part, rows, preferred_element_type=jnp.float32)

    local = lowered(share, own) + lowered(share_beside, beside)
    local, share_across = lax.optimization_barrier((local, share_across))
    share_diagonal = swapped(share_across, 1)
    answer = (
        local
        + lowered(share_across, across)
        + lowered(share_diagonal, diagonal)
    ).astype(jnp.bfloat16)
    answer = answer.reshape(sources, items, depth)
    if direct:
        answers = jnp.stack(
            [answer[r] if r == 0 else rotated(answer[r], -r) for r in range(sources)]
        )
    else:
        answers = lax.all_to_all(answer, "ctx", split_axis=0, concat_axis=0, tiled=True)
    summed = jnp.sum(answers.reshape(EXPERTS, group, CAP, width_local), axis=1, dtype=jnp.float32)
    summed = summed.reshape(EXPERTS * CAP, width_local)
    chosen = jnp.take(summed, targets, axis=0)
    routed = jnp.sum(expert_weights[:, :, None] * chosen, axis=1)
    return (state_float + routed).astype(jnp.bfloat16)


def solution(mesh):
    placed = (
        P("ctx", "tp"),
        P("ctx", "tp"),
        P("ctx", "tp"),
        P("ctx", None),
        P("ctx", "tp"),
        P(None, "tp"),
        P(),
        P("tp"),
        P("tp"),
        P("tp"),
        P("tp"),
        P("tp", "ctx"),
        P("tp"),
        P("ctx", "tp", None),
        P("ctx", "tp", None),
        P("ctx", None, "tp"),
        P("ctx", None),
        P("ctx", None),
    )

    direct = mesh.shape["ctx"] == EXPERTS and mesh.shape["tp"] == 4

    def layer(*args):
        return (block_direct if direct else body)(*args)

    return jax.shard_map(
        layer, mesh=mesh, in_specs=placed, out_specs=P("ctx", "tp"), check_vma=False
    )
```

```python
import functools

import jax
import jax.numpy as jnp
from jax import lax
from jax.experimental import pallas as pl
from jax.experimental.pallas import tpu as pltpu
from jax.sharding import PartitionSpec as P


EXPERTS = 8
CAP = 36


EPSILON = 1e-05


def passed_along(value, axis, steps):
    count = lax.axis_size(axis)
    first, last = (max(0, -steps), min(count, count - steps))
    return lax.ppermute(value, axis, [(source, source + steps) for source in range(first, last)])


def swapped(value, distance):
    return lax.ppermute(value, "tp", [(p, p ^ distance) for p in range(lax.axis_size("tp"))])


def rotated(value, steps):
    count = lax.axis_size("ctx")
    return lax.ppermute(value, "ctx", [(c, (c + steps) % count) for c in range(count)])


def tensor_total(value):
    return (value + swapped(value, 1)) + (swapped(value, 2) + swapped(value, 3))


def entering(decay, fresh, axis):
    peers, position = (lax.axis_size(axis), lax.axis_index(axis))
    packed = jnp.concatenate([fresh, decay[None, :]], axis=0).astype(jnp.bfloat16)
    if peers == EXPERTS:
        total, carry = (jnp.zeros_like(fresh), jnp.ones_like(decay)[None, :])
        for distance in range(1, peers):
            part = passed_along(packed, axis, distance).astype(jnp.float32)
            total = total + carry * part[:-1]
            carry = carry * part[-1:]
        return total
    everything = lax.all_gather(packed, axis).astype(jnp.float32)

    def step(k, before):
        part = everything[k]
        return jnp.where(k < position, part[-1:] * before + part[:-1], before)

    return lax.fori_loop(0, peers, step, jnp.zeros_like(fresh))


def causal_filter(previous, current, kernel):
    joined = jnp.concatenate([previous, current], axis=0)
    length = current.shape[0]
    total = jnp.zeros(current.shape, jnp.float32)
    for offset in range(kernel.shape[0]):
        total = total + kernel[offset][None, :] * joined[offset : offset + length]
    return jax.nn.silu(total)


def local_terms(values, writer, reader, step_size, log_decay):
    length = values.shape[0]
    cumulative = jnp.cumsum(log_decay, axis=0)
    scores = jnp.dot(reader, writer.T, precision=lax.Precision.HIGHEST)
    order = jnp.arange(length)
    causal = (order[:, None] >= order[None, :])[:, :, None]
    spans = cumulative[:, None, :] - cumulative[None, :, :]
    factor = jnp.where(causal, jnp.exp(jnp.where(causal, spans, 0.0)), 0.0)
    factor = factor * step_size[None, :, :] * scores[:, :, None]
    inside = jnp.einsum("tsh,shp->thp", factor, values, precision=lax.Precision.HIGHEST)
    tail = cumulative[length - 1]
    ending = jnp.exp(tail[None, :] - cumulative) * step_size
    weighted = (ending[:, :, None] * values).reshape(length, -1)
    fresh = jnp.dot(writer.T, weighted, precision=lax.Precision.HIGHEST)
    return (inside, cumulative, fresh, tail)


SUB = 16
CHUNK = 256
MESH = pl.DeviceIdType.MESH


def remote(source, target, send, receive, device):
    return pltpu.make_async_remote_copy(
        src_ref=source,
        dst_ref=target,
        send_sem=send,
        recv_sem=receive,
        device_id=device,
        device_id_type=MESH,
    )


def unfold(count, extra, fold, part):
    j = lax.broadcasted_iota(jnp.int32, (count * extra, count * SUB), 0)
    i = lax.broadcasted_iota(jnp.int32, (count * extra, count * SUB), 1)
    return (i == j * fold + part).astype(jnp.bfloat16)


def refold(count, extra, fold, part):
    j = lax.broadcasted_iota(jnp.int32, (count * SUB, count * extra), 1)
    i = lax.broadcasted_iota(jnp.int32, (count * SUB, count * extra), 0)
    return (i == j * fold + part).astype(jnp.bfloat16)


def block_kernel(
    peers,
    mixer_input,
    gate_input,
    state_proj,
    step_raw,
    conv_weight,
    conv_state_weight,
    step_bias,
    decay_log,
    skip_gain,
    mixer_gain,
    residual,
    feed_gain,
    expert_ids,
    expert_weights,
    weight_own,
    gate,
    up,
    down,
    out,
    hidden,
    expert_input,
    stats,
    stats_in,
    picker,
    weights_high,
    weights_low,
    edge_in,
    edge_state,
    edge_state_in,
    states_long,
    wide_state,
    wide_sums,
    wide_step,
    state_out,
    state_in,
    tail_out,
    tail_in,
    entering_state,
    logs,
    gate_tiles,
    up_tiles,
    down_tiles,
    packed,
    packed_extra,
    rows,
    rows_extra,
    answers,
    answers_extra,
    first,
    first_in,
    far,
    far_in,
    near_in,
    active,
    active_beside,
    active_across,
    active_diagonal,
    total,
    tile_sem,
    weight_sem,
    weight_send,
    weight_receive,
    edge_send,
    edge_receive,
    state_send,
    state_receive,
    line_send,
    line_receive,
    merge_send,
    merge_receive,
    final_receive,
    stats_send,
    stats_receive,
    home_send,
    home_receive,
    pair_send,
    pair_receive,
):
    ctx, tp = lax.axis_index("ctx"), lax.axis_index("tp")
    beside = tp + 1 - 2 * (tp % 2)
    across = (tp + 2) % 4
    diagonal = 3 - tp
    width = rows.shape[1]
    chunks = first.shape[2]
    hidden_width = chunks * CHUNK
    main = packed.shape[0] // peers
    extra = (rows.shape[0] - peers * main) // peers
    near = peers // 2
    group = near * (main + extra)
    fold = SUB // extra
    piece = width // fold

    places = ((diagonal, across, beside, tp), (diagonal, across, beside, tp), (tp, beside, across, diagonal))

    def tile(kind, place, j):
        span = pl.ds(pl.multiple_of(places[kind][place] * hidden_width + j * CHUNK, CHUNK), CHUNK)
        source = (gate, up, down)[kind]
        source = source.at[0, span, :] if kind == 2 else source.at[0, :, span]
        target = (gate_tiles, up_tiles, down_tiles)[kind].at[place, j]
        return pltpu.make_async_copy(source, target, tile_sem.at[4 * kind + place, j])

    def start_group(chosen):
        def body(j, carry):
            for kind, place in chosen:
                tile(kind, place, j).start()
            return carry

        lax.fori_loop(0, chunks, body, 0)

    z, x = ctx // 2, ctx % 2
    core, side = tp % 2, tp // 2
    line = peers // 2
    tokens = residual.shape[0]
    half = tokens // 2
    held = down_tiles.at[3]

    def weight_copy(n):
        source = weight_own.at[:, pl.ds(n * CHUNK, CHUNK)]
        return pltpu.make_async_copy(source, gate_tiles.at[3, 2 * x + n], weight_sem.at[n])

    def weight_across(n):
        span = pl.ds(n // 2 * CHUNK, CHUNK)
        return remote(
            weight_own.at[span, pl.ds(n % 2 * CHUNK, CHUNK)],
            gate_tiles.at[3, 2 * x + n % 2, span, :],
            weight_send.at[n],
            weight_receive.at[n],
            {"ctx": ctx + 1 - 2 * x},
        )

    pieces = 2 * width // CHUNK
    for distance in range(peers):
        state_in[distance] = jnp.zeros(state_in.shape[1:], state_in.dtype)
        tail_in[distance] = jnp.zeros(tail_in.shape[1:], tail_in.dtype)
    states = state_proj.shape[0] // 2
    heads = step_raw.shape[0]
    wide_state[...] = jnp.zeros_like(wide_state)
    wide_state[: 2 * states, :] = state_proj[...].astype(jnp.float32)
    state_columns = wide_state[...].T
    edge_state[...] = state_columns[tokens - SUB :].astype(jnp.bfloat16)
    for n in range(2):
        weight_copy(n).start()
    start_group([(kind, place) for place in (0, 1) for kind in (0, 1)])
    start_group([(0, 2), (1, 2), (1, 3)])
    start_group([(2, place) for place in range(3)])

    barrier = pltpu.get_barrier_semaphore()
    for distance in range(1, peers):
        pl.semaphore_signal(
            barrier, inc=1, device_id={"ctx": (ctx + distance) % peers}, device_id_type=MESH
        )
    for other in (beside, across, diagonal):
        pl.semaphore_signal(barrier, inc=1, device_id={"tp": other}, device_id_type=MESH)

    @pl.when(z != tp)
    def _():
        pl.semaphore_signal(
            barrier, inc=1, device_id={"ctx": tp * 2 + x, "tp": beside}, device_id_type=MESH
        )

    def piece_of(b, h):
        return held.at[b // 2, pl.ds(pl.multiple_of(b % 2 * tokens + h * half, half), half), :]

    def slab(kind, b):
        return held.at[line // 2 + kind, pl.ds(pl.multiple_of(b * half, half), half), :]

    def as_row(column):
        return jnp.broadcast_to(column, (tokens, tokens)).T[:8]

    def as_column(row):
        return jnp.broadcast_to(row[:1], (tokens, tokens)).T[:, :1]

    def stats_copy(kind, n):
        other = (beside, across, diagonal)[n]
        return remote(
            stats.at[kind], stats_in.at[kind, n], stats_send.at[kind, n], stats_receive.at[kind, n], {"tp": other}
        )

    def stats_total(kind):
        for n in range(3):
            stats_copy(kind, n).wait_recv()
        row = (stats[kind] + stats_in[kind, 0]) + (stats_in[kind, 1] + stats_in[kind, 2])
        return lax.rsqrt(as_column(row) / (width * 4) + EPSILON)

    lanes = tokens
    slabs = width // lanes
    values = total.at[pl.ds(tokens + SUB, tokens)]
    exact = lax.Precision.HIGHEST
    total[8 : 8 + tokens, :] = mixer_input[...].astype(jnp.float32)
    states_long[8 : 8 + tokens, :] = state_columns[:, : 2 * states]
    wide_step[...] = jnp.zeros_like(wide_step)
    wide_step[:heads, :] = step_raw[...]
    step_size = jax.nn.softplus(wide_step[...].T[:, :heads] + step_bias[...])
    wide_sums[...] = jnp.zeros_like(wide_sums)
    wide_sums[:2, :] = expert_ids[...].astype(jnp.float32)
    wide_sums[2:4, :] = expert_weights[...]
    route = wide_sums[...].T
    log_decay = -step_size * jnp.exp(decay_log[...])
    row_index = lax.broadcasted_iota(jnp.int32, (tokens, tokens), 0)
    column_index = lax.broadcasted_iota(jnp.int32, (tokens, tokens), 1)
    causal = row_index >= column_index
    cumulative = jnp.dot(
        causal.astype(jnp.float32), log_decay, precision=exact, preferred_element_type=jnp.float32
    )
    wide_sums[...] = jnp.zeros_like(wide_sums)
    wide_step[...] = jnp.zeros_like(wide_step)
    wide_state[...] = jnp.zeros_like(wide_state)
    wide_sums[:, :heads] = cumulative
    wide_step[:, :heads] = step_size
    sums_row, step_row = wide_sums[...].T, wide_step[...].T
    tail_out[...] = jnp.broadcast_to(wide_sums[tokens - 1 :, :], tail_out.shape)

    kinds = lax.broadcasted_iota(jnp.int32, (tokens, EXPERTS), 1)
    named = [(route[:, k : k + 1] == kinds.astype(jnp.float32)).astype(jnp.float32) for k in range(2)]
    before = jnp.dot(
        (row_index > column_index).astype(jnp.bfloat16),
        (named[0] + named[1]).astype(jnp.bfloat16),
        preferred_element_type=jnp.float32,
    )
    relative = kinds ^ ctx
    start = (relative // near * group).astype(jnp.float32)
    inner = (relative % near).astype(jnp.float32)
    spots = start + jnp.where(
        before < main, inner * main + before, near * main + inner * extra + before - main
    )
    targets = [jnp.sum(named[k] * spots, axis=1, keepdims=True) for k in range(2)]
    slot_row = lax.broadcasted_iota(jnp.int32, picker.shape, 0).astype(jnp.float32)
    slot_column = lax.broadcasted_iota(jnp.int32, weights_high.shape, 1).astype(jnp.float32)
    picked_rows = [as_row(target)[:1] for target in targets]
    picker[...] = (
        jnp.where(slot_row == picked_rows[0], 1.0, 0.0) + jnp.where(slot_row == picked_rows[1], 1.0, 0.0)
    ).astype(jnp.bfloat16)
    weights = jnp.where(slot_column == targets[0], route[:, 2:3], 0.0)
    weights = weights + jnp.where(slot_column == targets[1], route[:, 3:4], 0.0)
    high = weights.astype(jnp.bfloat16)
    weights_high[...] = high
    weights_low[...] = (weights - high.astype(jnp.float32)).astype(jnp.bfloat16)

    pl.semaphore_wait(barrier, peers - 1 + 3 + jnp.where(z == beside, line - 1, 0))

    def edge_copies():
        device = {"ctx": (ctx + 1) % peers}
        return (
            remote(
                mixer_input.at[pl.ds(tokens - SUB, SUB), :], edge_in, edge_send.at[0], edge_receive.at[0], device
            ),
            remote(edge_state, edge_state_in, edge_send.at[1], edge_receive.at[1], device),
        )

    @pl.when(ctx < peers - 1)
    def _():
        for copy in edge_copies():
            copy.start()

    for n in range(2):
        weight_across(n).start()

    @pl.when(ctx > 0)
    def _():
        for copy in edge_copies():
            copy.wait_recv()
        total[:8, :] = edge_in[...].astype(jnp.float32)[8:]
        states_long[:8, :] = edge_state_in[...].astype(jnp.float32)[8:, : 2 * states]

    @pl.when(ctx == 0)
    def _():
        total[:8, :] = jnp.zeros((8, width), jnp.float32)
        states_long[:8, :] = jnp.zeros((8, 2 * states), jnp.float32)

    taps = conv_weight.shape[0]
    base = 8 - (taps - 1)
    filtered = jnp.zeros((tokens, 2 * states), jnp.float32)
    for tap in range(taps):
        filtered = filtered + conv_state_weight[tap : tap + 1, :] * states_long[base + tap : base + tap + tokens, :]
    wide_state[:, : 2 * states] = jax.nn.silu(filtered)
    state_rows = wide_state[...].T
    writer_rows = state_rows[:states]
    ending = jnp.exp(wide_sums[tokens - 1 :, :] - wide_sums[...]) * wide_step[...]
    left = lax.broadcasted_iota(jnp.int32, (tokens, lanes), 1) < lanes // 2

    def widened(narrow, i):
        return jnp.where(left, narrow[:, 2 * i : 2 * i + 1], narrow[:, 2 * i + 1 : 2 * i + 2])

    for i in range(slabs):
        slab_of = slice(i * lanes, (i + 1) * lanes)
        value = jnp.zeros((tokens, lanes), jnp.float32)
        for tap in range(taps):
            value = value + conv_weight[tap : tap + 1, slab_of] * total[base + tap : base + tap + tokens, slab_of]
        value = jax.nn.silu(value)
        values[:, slab_of] = value
        state_out[:, slab_of] = jnp.dot(
            writer_rows, widened(ending, i) * value, precision=exact, preferred_element_type=jnp.float32
        ).astype(jnp.bfloat16)

    def state_copies(distance):
        device = {"ctx": (ctx + distance) % peers}
        return (
            remote(
                state_out, state_in.at[distance], state_send.at[0, distance], state_receive.at[0, distance], device
            ),
            remote(
                tail_out, tail_in.at[distance], state_send.at[1, distance], state_receive.at[1, distance], device
            ),
        )

    for distance in range(peers - 1, 0, -1):

        @pl.when(ctx + distance < peers)
        def _():
            for copy in state_copies(distance):
                copy.start()

    for n in range(2, pieces):
        weight_across(n).start()
    scores = jnp.dot(
        wide_state[:, states : 2 * states], writer_rows, precision=exact, preferred_element_type=jnp.float32
    )
    for i in range(slabs):
        slab_of = slice(i * lanes, (i + 1) * lanes)
        factors = []
        for head in (2 * i, 2 * i + 1):
            spans = wide_sums[:, head : head + 1] - sums_row[head : head + 1, :]
            factors.append(
                jnp.exp(jnp.where(causal, spans, -1e30)) * (step_row[head : head + 1, :] * scores)
            )
        value = values[:, slab_of]
        halves = jnp.concatenate([jnp.where(left, value, 0.0), jnp.where(left, 0.0, value)], axis=0)
        inside = jnp.dot(
            jnp.concatenate(factors, axis=1).astype(jnp.bfloat16),
            halves.astype(jnp.bfloat16),
            preferred_element_type=jnp.float32,
        )
        total[:tokens, slab_of] = inside + widened(skip_gain, i) * value

    for distance in range(1, peers):

        @pl.when(ctx - distance >= 0)
        def _():
            for copy in state_copies(distance):
                copy.wait_recv()

    logs[...] = jnp.zeros_like(logs)
    running = jnp.zeros((1, tokens), jnp.float32)
    for distance in range(1, peers):
        logs[distance - 1 : distance, :] = running
        running = running + tail_in[distance][:1]
    spread = (
        lax.broadcasted_iota(jnp.int32, (lanes, width), 1) // (width // heads)
        == lax.broadcasted_iota(jnp.int32, (lanes, width), 0)
    ).astype(jnp.float32)
    carries = jnp.dot(jnp.exp(logs[...]), spread, precision=exact, preferred_element_type=jnp.float32)
    arrived = jnp.zeros((states, width), jnp.float32)
    for distance in range(1, peers):
        arrived = arrived + carries[distance - 1 : distance, :] * state_in[distance].astype(jnp.float32)
    entering_state[:states, :] = jnp.zeros((states, width), jnp.float32)
    entering_state[states:, :] = arrived
    growth = jnp.exp(wide_sums[...])
    squares = jnp.zeros((tokens, lanes), jnp.float32)
    for i in range(slabs):
        slab_of = slice(i * lanes, (i + 1) * lanes)
        carried = jnp.dot(
            wide_state[:, : 2 * states],
            entering_state[:, slab_of],
            precision=exact,
            preferred_element_type=jnp.float32,
        )
        mixed = total[:tokens, slab_of] + carried * widened(growth, i)
        value = mixed * jax.nn.silu(gate_input[:, slab_of].astype(jnp.float32))
        squares = squares + value * value
        held[z // 2, pl.ds(pl.multiple_of(z % 2 * tokens, tokens), tokens), slab_of] = (
            value * mixer_gain[:, slab_of]
        ).astype(jnp.bfloat16)
    stats[0] = as_row(jnp.sum(squares, axis=1, keepdims=True))

    def line_copy(direction, b, h):
        return remote(
            piece_of(b, h),
            piece_of(b, h),
            line_send.at[direction, b, h],
            line_receive.at[b, h],
            {"ctx": (ctx + 2 - 4 * direction + peers) % peers},
        )

    for h in range(2):

        @pl.when(z < line - 1)
        def _():
            line_copy(0, z, h).start()

        @pl.when(z > 0)
        def _():
            line_copy(1, z, h).start()

    for n in range(3):
        stats_copy(0, n).start()
    for n in range(2):
        weight_copy(n).wait()
    for n in range(pieces):
        weight_across(n).wait_recv()

    def give_copy(b):
        return remote(slab(0, b), slab(1, b), merge_send.at[0, b], merge_receive.at[0, b], {"tp": beside})

    def cross_copy(b):
        return remote(slab(2, b), slab(3, b), merge_send.at[1, b], merge_receive.at[1, b], {"tp": across})

    def final_copy(b):
        return remote(
            slab(2, b),
            slab(4, core),
            merge_send.at[1, b],
            final_receive.at[core],
            {"ctx": b * 2 + x, "tp": z},
        )

    def mine(slot):
        return pl.ds(pl.multiple_of(slot * tokens + core * half, half), half)

    def store(kind, b, data):
        held[line // 2 + kind, pl.ds(pl.multiple_of(b * half, half), half), :] = data

    def forward(b, direction):
        for h in range(2):
            line_copy(direction, b, h).wait_recv()

            @pl.when((z < line - 1) if direction == 0 else (z > 0))
            def _():
                line_copy(direction, b, h).start()

    def multiply(b, slot):
        block = held[b // 2, pl.ds(pl.multiple_of(b % 2 * tokens, tokens), tokens), :]
        for n in range(4):
            total[slot * tokens : (slot + 1) * tokens, n * CHUNK : (n + 1) * CHUNK] = jnp.dot(
                block, gate_tiles[3, n], preferred_element_type=jnp.float32
            )
        theirs = pl.ds(pl.multiple_of(slot * tokens + (1 - core) * half, half), half)
        store(0, b, total[theirs, :].astype(jnp.bfloat16))
        give_copy(b).start()

    def merge(b, slot):
        give_copy(b).wait_recv()
        joint = total[mine(slot), :] + slab(1, b)[...].astype(jnp.float32)

        @pl.when(side != z // 2)
        def _():
            store(2, b, joint.astype(jnp.bfloat16))
            cross_copy(b).start()

        @pl.when(side == z // 2)
        def _():
            total[mine(slot), :] = joint

    def deliver(b, slot):
        @pl.when(side == z // 2)
        def _():
            cross_copy(b).wait_recv()
            joint = (total[mine(slot), :] + slab(3, b)[...].astype(jnp.float32)).astype(jnp.bfloat16)
            stays = jnp.logical_and(b == z, tp == z)

            @pl.when(stays)
            def _():
                store(4, core, joint)

            @pl.when(jnp.logical_not(stays))
            def _():
                store(2, b, joint)
                final_copy(b).start()

    def each(step, action):
        if step == 0:
            action(z, 0)
            return

        @pl.when(z - step >= 0)
        def _():
            action(z - step, 0)

        @pl.when(z + step < line)
        def _():
            action(z + step, 1)

    for step in range(line):
        if step > 0:
            each(step, forward)
            each(step - 1, deliver)
        each(step, multiply)
        each(step, merge)
    each(line - 1, deliver)

    scale = stats_total(0)
    for h in range(2):

        @pl.when(jnp.logical_not(jnp.logical_and(z == tp, core == h)))
        def _():
            remote(
                slab(4, h), slab(4, h), merge_send.at[1, 0], final_receive.at[h], {"tp": beside}
            ).wait_recv()

    mixer_out = held[line // 2 + 4, :tokens, :].astype(jnp.float32) * scale
    hidden[...] = (residual[...].astype(jnp.float32) + mixer_out).astype(jnp.bfloat16)
    state = hidden[...].astype(jnp.float32)
    stats[1] = as_row(jnp.sum(state * state, axis=1, keepdims=True))
    for n in range(3):
        stats_copy(1, n).start()
    feed_scale = stats_total(1)
    expert_input[...] = (state * feed_scale * feed_gain[...]).astype(jnp.bfloat16)

    def pack(g, block):
        packed[g * near * main : (g + 1) * near * main, :] = block[: near * main].astype(jnp.bfloat16)
        tail = block[near * main :].astype(jnp.bfloat16)
        folded = jnp.zeros((near * SUB, piece), jnp.float32)
        for part in range(fold):
            folded = folded + jnp.dot(
                refold(near, extra, fold, part),
                tail[:, part * piece : (part + 1) * piece],
                preferred_element_type=jnp.float32,
            )
        packed_extra[g * near * SUB : (g + 1) * near * SUB, :] = folded.astype(jnp.bfloat16)

    def unpack(g, target, landed):
        block = landed[g * near * SUB : (g + 1) * near * SUB, :]
        for part in range(fold):
            target[g * group + near * main : (g + 1) * group, part * piece : (part + 1) * piece] = jnp.dot(
                unfold(near, extra, fold, part), block, preferred_element_type=jnp.float32
            ).astype(jnp.bfloat16)

    def partner(r):
        high = (ctx // 4 + r // 4) % 2
        middle = (ctx // 2 % 2 + r // 2 % 2) % 2
        return {"ctx": 4 * high + 2 * middle + (ctx % 2 + r % 2) % 2}

    def travel(g, target, target_extra, kind):
        copies = []
        for r in range(max(1, g * near), (g + 1) * near):
            spot = pl.ds(g * group + r % near * main, main)
            tile_rows = pl.ds(r * SUB, SUB)
            copies.append(
                remote(
                    packed.at[pl.ds(r * main, main)],
                    target.at[spot],
                    home_send.at[kind, r],
                    home_receive.at[kind, r],
                    partner(r),
                )
            )
            copies.append(
                remote(
                    packed_extra.at[tile_rows],
                    target_extra.at[tile_rows],
                    home_send.at[kind + 1, r],
                    home_receive.at[kind + 1, r],
                    partner(r),
                )
            )
        return copies

    for g in range(2):
        pack(
            g,
            jnp.dot(
                picker[g * group : (g + 1) * group, :], expert_input[...], preferred_element_type=jnp.float32
            ),
        )
        for copy in travel(g, rows, rows_extra, 0):
            copy.start()
    rows[:main] = packed[:main]
    rows_extra[:SUB] = packed_extra[:SUB]
    for kind in range(2):
        for n in range(3):
            stats_copy(kind, n).wait_send()
    for n in range(pieces):
        weight_across(n).wait_send()

    @pl.when(ctx < peers - 1)
    def _():
        for copy in edge_copies():
            copy.wait_send()

    for distance in range(1, peers):

        @pl.when(ctx + distance < peers)
        def _():
            for copy in state_copies(distance):
                copy.wait_send()

    for b in range(line):

        @pl.when(jnp.logical_and(z < line - 1, b <= z))
        def _():
            for h in range(2):
                line_copy(0, b, h).wait_send()

        @pl.when(jnp.logical_and(z > 0, b >= z))
        def _():
            for h in range(2):
                line_copy(1, b, h).wait_send()

        give_copy(b).wait_send()

        @pl.when(side != z // 2)
        def _():
            cross_copy(b).wait_send()

        @pl.when(
            jnp.logical_and(side == z // 2, jnp.logical_not(jnp.logical_and(z == b, tp == z)))
        )
        def _():
            final_copy(b).wait_send()

    start_group([(0, 3), (2, 3)])

    def pair(g, kind, j, source, target, other):
        return remote(source, target, pair_send.at[g, kind, j], pair_receive.at[g, kind, j], {"tp": other})

    both = (gate_tiles, up_tiles)

    def product(g, which, place, j, fresh):
        if fresh:
            tile(which, place, j).wait()
        return jnp.dot(
            rows[g * group : (g + 1) * group, :], both[which][place, j], preferred_element_type=jnp.float32
        )

    def first_copy(g, which, j):
        return pair(g, which, j, first.at[g, which, j], first_in.at[g, which, j], beside)

    def far_copy(g, which, j):
        return pair(g, 2 + which, j, far.at[g, which, j], far_in.at[g, which, j], across)

    def near_copy(g, which, j):
        return pair(g, 4 + which, j, first.at[g, which, j], near_in.at[g, which, j], beside)

    def beside_copy(g, j):
        return pair(g, 6, j, active.at[g, j], active_beside.at[g, j], beside)

    def across_copy(g, j):
        return pair(g, 7, j, active.at[g, j], active_across.at[g, j], across)

    def diagonal_copy(g, j):
        return pair(g, 8, j, active_across.at[g, j], active_diagonal.at[g, j], beside)

    def loop(step):
        def run(j, carry):
            step(j)
            return carry

        lax.fori_loop(0, chunks, run, 0)

    def receive_rows(g):
        for copy in travel(g, rows, rows_extra, 0):
            copy.wait_recv()
        unpack(g, rows, rows_extra)

    def far_step(g, fresh, j):
        for which in range(2):
            first[g, which, j] = product(g, which, 0, j, fresh).astype(jnp.bfloat16)
            first_copy(g, which, j).start()
        for which in range(2):
            mine = product(g, which, 1, j, fresh)
            first_copy(g, which, j).wait_recv()
            far[g, which, j] = (mine + first_in[g, which, j].astype(jnp.float32)).astype(jnp.bfloat16)
            far_copy(g, which, j).start()

    def near_step(g, fresh, j):
        for which in range(2):
            mine = product(g, which, 2, j, fresh).astype(jnp.bfloat16)
            first_copy(g, which, j).wait_send()
            first[g, which, j] = mine
            near_copy(g, which, j).start()

    def lowered(g, source, place, j, fresh):
        if fresh:
            tile(2, place, j).wait()
        total[g * group : (g + 1) * group, :] += jnp.dot(
            source[g, j], down_tiles[place, j], preferred_element_type=jnp.float32
        )

    def active_step(g, fresh, j):
        sums = []
        for which in range(2):
            mine = product(g, which, 3, j, fresh).astype(jnp.bfloat16).astype(jnp.float32)
            near_copy(g, which, j).wait_recv()
            mine = mine + near_in[g, which, j].astype(jnp.float32)
            far_copy(g, which, j).wait_recv()
            sums.append(mine + far_in[g, which, j].astype(jnp.float32))
        active[g, j] = (jax.nn.silu(sums[0]) * sums[1]).astype(jnp.bfloat16)
        across_copy(g, j).start()
        beside_copy(g, j).start()

    def lower_step(g, fresh, j):
        lowered(g, active, 0, j, fresh)
        beside_copy(g, j).wait_recv()
        lowered(g, active_beside, 1, j, fresh)

    def last_step(g, fresh, j):
        across_copy(g, j).wait_recv()
        diagonal_copy(g, j).start()
        lowered(g, active_across, 2, j, fresh)
        diagonal_copy(g, j).wait_recv()
        lowered(g, active_diagonal, 3, j, fresh)

    def send_home(g):
        pack(g, total[g * group : (g + 1) * group, :])
        for copy in travel(g, answers, answers_extra, 2):
            copy.start()

    receive_rows(0)
    loop(functools.partial(far_step, 0, True))
    receive_rows(1)
    loop(functools.partial(far_step, 1, False))
    total[...] = jnp.zeros_like(total)
    loop(functools.partial(near_step, 0, True))
    loop(functools.partial(near_step, 1, False))

    def far_group(j):
        active_step(1, True, j)
        lower_step(1, True, j)

    loop(far_group)
    loop(functools.partial(active_step, 0, False))
    for g in range(2):
        for copy in travel(g, rows, rows_extra, 0):
            copy.wait_send()
    loop(functools.partial(last_step, 1, True))
    send_home(1)
    loop(functools.partial(lower_step, 0, False))
    loop(functools.partial(last_step, 0, False))
    send_home(0)
    answers[:main] = packed[:main]
    answers_extra[:SUB] = packed_extra[:SUB]

    def drain(j):
        for g in range(2):
            for which in range(2):
                far_copy(g, which, j).wait_send()
                near_copy(g, which, j).wait_send()
            beside_copy(g, j).wait_send()
            across_copy(g, j).wait_send()
            diagonal_copy(g, j).wait_send()

    loop(drain)
    for g in (1, 0):
        for copy in travel(g, answers, answers_extra, 2):
            copy.wait_recv()
        unpack(g, answers, answers_extra)
    routed = jnp.dot(weights_high[...], answers[...], preferred_element_type=jnp.float32)
    routed = routed + jnp.dot(weights_low[...], answers[...], preferred_element_type=jnp.float32)
    out[...] = (hidden[...].astype(jnp.float32) + routed).astype(jnp.bfloat16)
    for g in range(2):
        for copy in travel(g, answers, answers_extra, 2):
            copy.wait_send()


def block_direct(
    residual,
    mixer_input,
    gate_input,
    state_proj,
    step_raw,
    conv_weight,
    conv_state_weight,
    step_bias,
    decay_log,
    skip_gain,
    mixer_gain,
    out_weight,
    feed_gain,
    gate,
    up,
    down,
    expert_ids,
    expert_weights,
):
    peers = lax.axis_size("ctx")
    tokens, width = residual.shape
    states = state_proj.shape[1] // 2
    chunks = gate.shape[2] // 4 // CHUNK
    extra = CAP - CAP // SUB * SUB
    main = CAP - extra
    count = peers * CAP
    vmem = pl.BlockSpec(memory_space=pltpu.VMEM)
    anywhere = pl.BlockSpec(memory_space=pl.ANY)
    block = (chunks, count // 2, CHUNK)
    low = jnp.bfloat16
    return pl.pallas_call(
        functools.partial(block_kernel, peers),
        out_shape=jax.ShapeDtypeStruct((tokens, width), low),
        in_specs=[vmem] * 14 + [anywhere] * 4,
        out_specs=vmem,
        scratch_shapes=[
            pltpu.VMEM((tokens, width), low),
            pltpu.VMEM((tokens, width), low),
            pltpu.VMEM((2, 8, tokens), jnp.float32),
            pltpu.VMEM((2, 3, 8, tokens), jnp.float32),
            pltpu.VMEM((count, tokens), low),
            pltpu.VMEM((tokens, count), low),
            pltpu.VMEM((tokens, count), low),
            pltpu.VMEM((SUB, width), low),
            pltpu.VMEM((SUB, tokens), low),
            pltpu.VMEM((SUB, tokens), low),
            pltpu.VMEM((8 + tokens, 2 * states), jnp.float32),
            pltpu.VMEM((tokens, tokens), jnp.float32),
            pltpu.VMEM((tokens, tokens), jnp.float32),
            pltpu.VMEM((tokens, tokens), jnp.float32),
            pltpu.VMEM((states, width), low),
            pltpu.VMEM((peers, states, width), low),
            pltpu.VMEM((8, tokens), jnp.float32),
            pltpu.VMEM((peers, 8, tokens), jnp.float32),
            pltpu.VMEM((2 * states, width), jnp.float32),
            pltpu.VMEM((8, tokens), jnp.float32),
            pltpu.VMEM((4, chunks, width, CHUNK), low),
            pltpu.VMEM((4, chunks, width, CHUNK), low),
            pltpu.VMEM((4, chunks, CHUNK, width), low),
            pltpu.VMEM((peers * main, width), low),
            pltpu.VMEM((peers * SUB, width * extra // SUB), low),
            pltpu.VMEM((count, width), low),
            pltpu.VMEM((peers * SUB, width * extra // SUB), low),
            pltpu.VMEM((count, width), low),
            pltpu.VMEM((peers * SUB, width * extra // SUB), low),
            pltpu.VMEM((2, 2) + block, low),
            pltpu.VMEM((2, 2) + block, low),
            pltpu.VMEM((2, 2) + block, low),
            pltpu.VMEM((2, 2) + block, low),
            pltpu.VMEM((2, 2) + block, low),
            pltpu.VMEM((2,) + block, low),
            pltpu.VMEM((2,) + block, low),
            pltpu.VMEM((2,) + block, low),
            pltpu.VMEM((2,) + block, low),
            pltpu.VMEM((count, width), jnp.float32),
            pltpu.SemaphoreType.DMA((12, chunks)),
            pltpu.SemaphoreType.DMA((2,)),
            pltpu.SemaphoreType.DMA((2 * width // CHUNK,)),
            pltpu.SemaphoreType.DMA((2 * width // CHUNK,)),
            pltpu.SemaphoreType.DMA((2,)),
            pltpu.SemaphoreType.DMA((2,)),
            pltpu.SemaphoreType.DMA((2, peers)),
            pltpu.SemaphoreType.DMA((2, peers)),
            pltpu.SemaphoreType.DMA((2, peers // 2, 2)),
            pltpu.SemaphoreType.DMA((peers // 2, 2)),
            pltpu.SemaphoreType.DMA((2, peers // 2)),
            pltpu.SemaphoreType.DMA((2, peers // 2)),
            pltpu.SemaphoreType.DMA((2,)),
            pltpu.SemaphoreType.DMA((2, 3)),
            pltpu.SemaphoreType.DMA((2, 3)),
            pltpu.SemaphoreType.DMA((4, peers)),
            pltpu.SemaphoreType.DMA((4, peers)),
            pltpu.SemaphoreType.DMA((2, 9, chunks)),
            pltpu.SemaphoreType.DMA((2, 9, chunks)),
        ],
        compiler_params=pltpu.CompilerParams(
            collective_id=0, has_side_effects=True, vmem_limit_bytes=66_000_000
        ),
        name="block",
    )(
        mixer_input,
        gate_input,
        state_proj.T,
        step_raw.T,
        conv_weight,
        conv_state_weight,
        step_bias[None, :],
        decay_log[None, :],
        skip_gain[None, :],
        mixer_gain[None, :],
        residual,
        feed_gain[None, :],
        expert_ids.T,
        expert_weights.T,
        out_weight,
        gate,
        up,
        down,
    )


def body(
    residual,
    mixer_input,
    gate_input,
    state_proj,
    step_raw,
    conv_weight,
    conv_state_weight,
    step_bias,
    decay_log,
    skip_gain,
    mixer_gain,
    out_weight,
    feed_gain,
    expert_gate,
    expert_up,
    expert_down,
    expert_ids,
    expert_weights,
):
    tensor_count = lax.axis_size("tp")
    context_count = lax.axis_size("ctx")
    tokens = mixer_input.shape[0]
    channels = mixer_input.shape[1]
    states = state_proj.shape[1] // 2
    heads_local = step_raw.shape[1]
    head_size = channels // heads_local
    taps = conv_weight.shape[0]
    direct = context_count == EXPERTS
    joined = jnp.concatenate([mixer_input, state_proj], axis=1)
    previous = passed_along(joined[tokens - (taps - 1) :], "ctx", 1)
    kernel = jnp.concatenate([conv_weight, conv_state_weight], axis=1)
    filtered = causal_filter(previous.astype(jnp.float32), joined.astype(jnp.float32), kernel)
    values = filtered[:, :channels].reshape(tokens, heads_local, head_size)
    writer = filtered[:, channels : channels + states]
    reader = filtered[:, channels + states :]
    step_size = jax.nn.softplus(step_raw + step_bias[None, :])
    log_decay = -step_size * jnp.exp(decay_log)[None, :]
    inside, cumulative, fresh, tail = local_terms(values, writer, reader, step_size, log_decay)

    incoming = entering(jnp.repeat(jnp.exp(tail), head_size), fresh, "ctx")
    carried = (
        jnp.dot(reader, incoming, precision=lax.Precision.HIGHEST).reshape(values.shape)
        * jnp.exp(cumulative)[:, :, None]
    )
    mixed = inside + carried + skip_gain[None, :, None] * values
    gated = mixed.reshape(tokens, channels) * jax.nn.silu(gate_input.astype(jnp.float32))
    tp_index = lax.axis_index("tp")
    core, chip = (tp_index % 2, tp_index // 2)
    scaled = (gated * mixer_gain[None, :]).astype(jnp.bfloat16)
    ctx_index = lax.axis_index("ctx")
    if direct:
        pairs = []
        for plane in range(4):
            block = rotated(scaled, 2 * plane) if plane else scaled
            other = lax.ppermute(block, "ctx", [(c, c ^ 1) for c in range(context_count)])
            pair = jnp.concatenate([block, other], axis=0)
            pairs.append(jnp.dot(pair, out_weight, preferred_element_type=jnp.float32))
        products = jnp.stack(pairs)

        def projected(quarter):
            place = (ctx_index // 2 - quarter) % 4
            return lax.dynamic_index_in_dim(products, place, 0, keepdims=False)

    else:
        everyone = lax.all_gather(scaled, "ctx", axis=0, tiled=True)
        span = everyone.shape[0] // tensor_count

        def projected(quarter):
            rows = lax.dynamic_slice_in_dim(everyone, quarter * span, span, 0)
            return jnp.dot(rows, out_weight, preferred_element_type=jnp.float32)

    square_sum = tensor_total(jnp.sum(gated * gated, axis=1))
    scale = lax.rsqrt(square_sum / (channels * tensor_count) + EPSILON)
    own, beside = (chip * 2 + core, chip * 2 + 1 - core)
    across, diagonal = ((1 - chip) * 2 + core, (1 - chip) * 2 + 1 - core)
    far = swapped(projected(diagonal).astype(jnp.bfloat16), 1)
    far = swapped((projected(across) + far.astype(jnp.float32)).astype(jnp.bfloat16), 2)
    near = swapped(projected(beside).astype(jnp.bfloat16), 1)
    reduced = projected(own) + near.astype(jnp.float32) + far.astype(jnp.float32)
    blocks = context_count // tensor_count
    reduced = reduced.astype(jnp.bfloat16).reshape(blocks, tokens, -1)
    pieces = []
    for j in range(blocks):
        moves = [
            (c * tensor_count + p, (p * blocks + (c + j) % blocks) * tensor_count + c // blocks)
            for c in range(context_count)
            for p in range(tensor_count)
        ]
        if direct:
            block = reduced[j]
        else:
            block = lax.dynamic_index_in_dim(reduced, (ctx_index + j) % blocks, 0, keepdims=False)
        pieces.append(lax.ppermute(block, ("ctx", "tp"), moves))
    stacked = jnp.stack(pieces)
    order = (ctx_index - jnp.arange(blocks)) % blocks
    if blocks == 2:
        first = ctx_index % 2 == 0
        mixer_out = jnp.concatenate(
            [jnp.where(first, pieces[0], pieces[1]), jnp.where(first, pieces[1], pieces[0])], axis=1
        )
    else:
        mixer_out = jnp.take(stacked, order, axis=0).transpose(1, 0, 2).reshape(tokens, -1)
    mixer_out = mixer_out.astype(jnp.float32) * scale[:, None]
    hidden_state = (residual.astype(jnp.float32) + mixer_out).astype(jnp.bfloat16)
    state_float = lax.optimization_barrier(hidden_state).astype(jnp.float32)
    width_total = hidden_state.shape[1] * tensor_count
    feed_sum = tensor_total(jnp.sum(state_float * state_float, axis=1))
    feed_scale = lax.rsqrt(feed_sum / width_total + EPSILON)
    expert_input = (state_float * feed_scale[:, None] * feed_gain[None, :]).astype(jnp.bfloat16)
    group = context_count // EXPERTS
    width_local = expert_input.shape[1]
    flat_experts = expert_ids.reshape(-1)
    matches = (flat_experts[:, None] == jnp.arange(EXPERTS)[None, :]).astype(jnp.int32)
    slots = jnp.sum((jnp.cumsum(matches, axis=0) - matches) * matches, axis=1)
    places = (flat_experts - ctx_index) % EXPERTS if direct else flat_experts
    targets = (places * CAP + slots).reshape(tokens, -1)
    picker = jnp.any(targets[None, :, :] == jnp.arange(EXPERTS * CAP)[:, None, None], axis=2)
    buffer = jnp.dot(
        picker.astype(jnp.bfloat16), expert_input, preferred_element_type=jnp.float32
    ).astype(jnp.bfloat16)
    outgoing = jnp.broadcast_to(
        buffer.reshape(EXPERTS, 1, CAP, width_local), (EXPERTS, group, CAP, width_local)
    )
    outgoing = outgoing.reshape(EXPERTS * group, CAP, width_local)
    gate_local = expert_gate[0]
    up_local = expert_up[0]
    down_local = expert_down[0]
    sources, items, depth = outgoing.shape
    if direct:
        flattened = jnp.concatenate(
            [outgoing[r] if r == 0 else rotated(outgoing[r], r) for r in range(sources)], axis=0
        )
    else:
        arrived = lax.all_to_all(outgoing, "ctx", split_axis=0, concat_axis=0, tiled=True)
        flattened = arrived.reshape(sources * items, depth)
    hidden = gate_local.shape[1] // tensor_count

    def product(source, weight, quarter):
        columns = lax.dynamic_slice_in_dim(weight, quarter * hidden, hidden, 1)
        return jnp.dot(source, columns, preferred_element_type=jnp.float32)

    fars, nears, rows = ([], [], flattened)
    for weight in (gate_local, up_local):
        far = product(rows, weight, diagonal).astype(jnp.bfloat16)
        far = swapped(far, 1)
        nears.append(swapped(product(rows, weight, beside).astype(jnp.bfloat16), 1))
        far = (product(rows, weight, across) + far.astype(jnp.float32)).astype(jnp.bfloat16)
        far, rows = lax.optimization_barrier((far, rows))
        fars.append(swapped(far, 2))
    gate_share, up_share = (
        product(rows, weight, own).astype(jnp.bfloat16).astype(jnp.float32)
        + near.astype(jnp.float32)
        + far.astype(jnp.float32)
        for weight, near, far in zip((gate_local, up_local), nears, fars)
    )
    share = (jax.nn.silu(gate_share) * up_share).astype(jnp.bfloat16)
    share_across = swapped(share, 2)
    share_beside = swapped(share, 1)

    def lowered(part, quarter):
        rows = lax.dynamic_slice_in_dim(down_local, quarter * hidden, hidden, 0)
        return jnp.dot(part, rows, preferred_element_type=jnp.float32)

    local = lowered(share, own) + lowered(share_beside, beside)
    local, share_across = lax.optimization_barrier((local, share_across))
    share_diagonal = swapped(share_across, 1)
    answer = (
        local
        + lowered(share_across, across)
        + lowered(share_diagonal, diagonal)
    ).astype(jnp.bfloat16)
    answer = answer.reshape(sources, items, depth)
    if direct:
        answers = jnp.stack(
            [answer[r] if r == 0 else rotated(answer[r], -r) for r in range(sources)]
        )
    else:
        answers = lax.all_to_all(answer, "ctx", split_axis=0, concat_axis=0, tiled=True)
    summed = jnp.sum(answers.reshape(EXPERTS, group, CAP, width_local), axis=1, dtype=jnp.float32)
    summed = summed.reshape(EXPERTS * CAP, width_local)
    chosen = jnp.take(summed, targets, axis=0)
    routed = jnp.sum(expert_weights[:, :, None] * chosen, axis=1)
    return (state_float + routed).astype(jnp.bfloat16)


def solution(mesh):
    placed = (
        P("ctx", "tp"),
        P("ctx", "tp"),
        P("ctx", "tp"),
        P("ctx", None),
        P("ctx", "tp"),
        P(None, "tp"),
        P(),
        P("tp"),
        P("tp"),
        P("tp"),
        P("tp"),
        P("tp", "ctx"),
        P("tp"),
        P("ctx", "tp", None),
        P("ctx", "tp", None),
        P("ctx", None, "tp"),
        P("ctx", None),
        P("ctx", None),
    )

    direct = mesh.shape["ctx"] == EXPERTS and mesh.shape["tp"] == 4

    def layer(*args):
        return (block_direct if direct else body)(*args)

    return jax.shard_map(
        layer, mesh=mesh, in_specs=placed, out_specs=P("ctx", "tp"), check_vma=False
    )
```

```python
import functools

import jax
import jax.numpy as jnp
from jax import lax
from jax.experimental import pallas as pl
from jax.experimental.pallas import tpu as pltpu
from jax.sharding import PartitionSpec as P


EXPERTS = 8
CAP = 36


EPSILON = 1e-05


def passed_along(value, axis, steps):
    count = lax.axis_size(axis)
    first, last = (max(0, -steps), min(count, count - steps))
    return lax.ppermute(value, axis, [(source, source + steps) for source in range(first, last)])


def swapped(value, distance):
    return lax.ppermute(value, "tp", [(p, p ^ distance) for p in range(lax.axis_size("tp"))])


def rotated(value, steps):
    count = lax.axis_size("ctx")
    return lax.ppermute(value, "ctx", [(c, (c + steps) % count) for c in range(count)])


def tensor_total(value):
    return (value + swapped(value, 1)) + (swapped(value, 2) + swapped(value, 3))


def entering(decay, fresh, axis):
    peers, position = (lax.axis_size(axis), lax.axis_index(axis))
    packed = jnp.concatenate([fresh, decay[None, :]], axis=0).astype(jnp.bfloat16)
    if peers == EXPERTS:
        total, carry = (jnp.zeros_like(fresh), jnp.ones_like(decay)[None, :])
        for distance in range(1, peers):
            part = passed_along(packed, axis, distance).astype(jnp.float32)
            total = total + carry * part[:-1]
            carry = carry * part[-1:]
        return total
    everything = lax.all_gather(packed, axis).astype(jnp.float32)

    def step(k, before):
        part = everything[k]
        return jnp.where(k < position, part[-1:] * before + part[:-1], before)

    return lax.fori_loop(0, peers, step, jnp.zeros_like(fresh))


def causal_filter(previous, current, kernel):
    joined = jnp.concatenate([previous, current], axis=0)
    length = current.shape[0]
    total = jnp.zeros(current.shape, jnp.float32)
    for offset in range(kernel.shape[0]):
        total = total + kernel[offset][None, :] * joined[offset : offset + length]
    return jax.nn.silu(total)


def local_terms(values, writer, reader, step_size, log_decay):
    length = values.shape[0]
    cumulative = jnp.cumsum(log_decay, axis=0)
    scores = jnp.dot(reader, writer.T, precision=lax.Precision.HIGHEST)
    order = jnp.arange(length)
    causal = (order[:, None] >= order[None, :])[:, :, None]
    spans = cumulative[:, None, :] - cumulative[None, :, :]
    factor = jnp.where(causal, jnp.exp(jnp.where(causal, spans, 0.0)), 0.0)
    factor = factor * step_size[None, :, :] * scores[:, :, None]
    inside = jnp.einsum("tsh,shp->thp", factor, values, precision=lax.Precision.HIGHEST)
    tail = cumulative[length - 1]
    ending = jnp.exp(tail[None, :] - cumulative) * step_size
    weighted = (ending[:, :, None] * values).reshape(length, -1)
    fresh = jnp.dot(writer.T, weighted, precision=lax.Precision.HIGHEST)
    return (inside, cumulative, fresh, tail)


SUB = 16
CHUNK = 256
MESH = pl.DeviceIdType.MESH


def remote(source, target, send, receive, device):
    return pltpu.make_async_remote_copy(
        src_ref=source,
        dst_ref=target,
        send_sem=send,
        recv_sem=receive,
        device_id=device,
        device_id_type=MESH,
    )


def unfold(count, extra, fold, part):
    j = lax.broadcasted_iota(jnp.int32, (count * extra, count * SUB), 0)
    i = lax.broadcasted_iota(jnp.int32, (count * extra, count * SUB), 1)
    return (i == j * fold + part).astype(jnp.bfloat16)


def refold(count, extra, fold, part):
    j = lax.broadcasted_iota(jnp.int32, (count * SUB, count * extra), 1)
    i = lax.broadcasted_iota(jnp.int32, (count * SUB, count * extra), 0)
    return (i == j * fold + part).astype(jnp.bfloat16)


def block_kernel(
    peers,
    mixer_input,
    gate_input,
    state_proj,
    step_raw,
    conv_weight,
    conv_state_weight,
    step_bias,
    decay_log,
    skip_gain,
    mixer_gain,
    residual,
    feed_gain,
    expert_ids,
    expert_weights,
    weight_own,
    gate,
    up,
    down,
    out,
    hidden,
    expert_input,
    stats,
    stats_in,
    picker,
    weights_high,
    weights_low,
    edge_in,
    edge_state,
    edge_state_in,
    states_long,
    wide_state,
    wide_sums,
    wide_step,
    state_out,
    state_in,
    tail_out,
    tail_in,
    entering_state,
    logs,
    kept,
    gate_tiles,
    up_tiles,
    down_tiles,
    packed,
    packed_extra,
    rows,
    rows_extra,
    answers,
    answers_extra,
    first,
    first_in,
    far,
    far_in,
    near_in,
    active,
    active_beside,
    active_across,
    active_diagonal,
    total,
    tile_sem,
    weight_sem,
    weight_send,
    weight_receive,
    edge_send,
    edge_receive,
    state_send,
    state_receive,
    line_send,
    line_receive,
    merge_send,
    merge_receive,
    final_receive,
    stats_send,
    stats_receive,
    home_send,
    home_receive,
    pair_send,
    pair_receive,
):
    ctx, tp = lax.axis_index("ctx"), lax.axis_index("tp")
    beside = tp + 1 - 2 * (tp % 2)
    across = (tp + 2) % 4
    diagonal = 3 - tp
    width = rows.shape[1]
    chunks = first.shape[2]
    hidden_width = chunks * CHUNK
    main = packed.shape[0] // peers
    extra = (rows.shape[0] - peers * main) // peers
    near = peers // 2
    group = near * (main + extra)
    fold = SUB // extra
    piece = width // fold

    places = ((diagonal, across, beside, tp), (diagonal, across, beside, tp), (tp, beside, across, diagonal))

    def tile(kind, place, j):
        span = pl.ds(pl.multiple_of(places[kind][place] * hidden_width + j * CHUNK, CHUNK), CHUNK)
        source = (gate, up, down)[kind]
        source = source.at[0, span, :] if kind == 2 else source.at[0, :, span]
        target = (gate_tiles, up_tiles, down_tiles)[kind].at[place, j]
        return pltpu.make_async_copy(source, target, tile_sem.at[4 * kind + place, j])

    def start_group(chosen):
        def body(j, carry):
            for kind, place in chosen:
                tile(kind, place, j).start()
            return carry

        lax.fori_loop(0, chunks, body, 0)

    z, x = ctx // 2, ctx % 2
    core, side = tp % 2, tp // 2
    line = peers // 2
    tokens = residual.shape[0]
    half = tokens // 2
    held = down_tiles.at[3]

    def weight_copy(n):
        source = weight_own.at[:, pl.ds(n * CHUNK, CHUNK)]
        return pltpu.make_async_copy(source, gate_tiles.at[3, 2 * x + n], weight_sem.at[n])

    def weight_across(n):
        span = pl.ds(n // 2 * CHUNK, CHUNK)
        return remote(
            weight_own.at[span, pl.ds(n % 2 * CHUNK, CHUNK)],
            gate_tiles.at[3, 2 * x + n % 2, span, :],
            weight_send.at[n],
            weight_receive.at[n],
            {"ctx": ctx + 1 - 2 * x},
        )

    pieces = 2 * width // CHUNK
    for distance in range(peers):
        state_in[distance] = jnp.zeros(state_in.shape[1:], state_in.dtype)
        tail_in[distance] = jnp.zeros(tail_in.shape[1:], tail_in.dtype)
    states = state_proj.shape[0] // 2
    heads = step_raw.shape[0]
    wide_state[...] = jnp.zeros_like(wide_state)
    wide_state[: 2 * states, :] = state_proj[...].astype(jnp.float32)
    state_columns = wide_state[...].T
    edge_state[...] = state_columns[tokens - SUB :].astype(jnp.bfloat16)
    for n in range(2):
        weight_copy(n).start()
    start_group([(kind, place) for place in (0, 1) for kind in (0, 1)])
    start_group([(0, 2), (1, 2), (1, 3)])
    start_group([(2, place) for place in range(3)])

    barrier = pltpu.get_barrier_semaphore()
    for distance in range(1, peers):
        pl.semaphore_signal(
            barrier, inc=1, device_id={"ctx": (ctx + distance) % peers}, device_id_type=MESH
        )
    for other in (beside, across, diagonal):
        pl.semaphore_signal(barrier, inc=1, device_id={"tp": other}, device_id_type=MESH)

    @pl.when(z != tp)
    def _():
        pl.semaphore_signal(
            barrier, inc=1, device_id={"ctx": tp * 2 + x, "tp": beside}, device_id_type=MESH
        )

    def piece_of(b, h):
        return held.at[b // 2, pl.ds(pl.multiple_of(b % 2 * tokens + h * half, half), half), :]

    def slab(kind, b):
        return held.at[line // 2 + kind, pl.ds(pl.multiple_of(b * half, half), half), :]

    def as_row(column):
        return jnp.broadcast_to(column, (tokens, tokens)).T[:8]

    def as_column(row):
        return jnp.broadcast_to(row[:1], (tokens, tokens)).T[:, :1]

    def stats_copy(kind, n):
        other = (beside, across, diagonal)[n]
        return remote(
            stats.at[kind], stats_in.at[kind, n], stats_send.at[kind, n], stats_receive.at[kind, n], {"tp": other}
        )

    def stats_total(kind):
        for n in range(3):
            stats_copy(kind, n).wait_recv()
        row = (stats[kind] + stats_in[kind, 0]) + (stats_in[kind, 1] + stats_in[kind, 2])
        return lax.rsqrt(as_column(row) / (width * 4) + EPSILON)

    lanes = tokens
    slabs = width // lanes
    values = total.at[pl.ds(tokens + SUB, tokens)]
    exact = lax.Precision.HIGHEST
    total[8 : 8 + tokens, :] = mixer_input[...].astype(jnp.float32)
    states_long[8 : 8 + tokens, :] = state_columns[:, : 2 * states]
    wide_step[...] = jnp.zeros_like(wide_step)
    wide_step[:heads, :] = step_raw[...]
    step_size = jax.nn.softplus(wide_step[...].T[:, :heads] + step_bias[...])
    wide_sums[...] = jnp.zeros_like(wide_sums)
    wide_sums[:2, :] = expert_ids[...].astype(jnp.float32)
    wide_sums[2:4, :] = expert_weights[...]
    route = wide_sums[...].T
    log_decay = -step_size * jnp.exp(decay_log[...])
    row_index = lax.broadcasted_iota(jnp.int32, (tokens, tokens), 0)
    column_index = lax.broadcasted_iota(jnp.int32, (tokens, tokens), 1)
    causal = row_index >= column_index
    cumulative = jnp.dot(
        causal.astype(jnp.float32), log_decay, precision=exact, preferred_element_type=jnp.float32
    )
    wide_sums[...] = jnp.zeros_like(wide_sums)
    wide_step[...] = jnp.zeros_like(wide_step)
    wide_state[...] = jnp.zeros_like(wide_state)
    wide_sums[:, :heads] = cumulative
    wide_step[:, :heads] = step_size
    sums_row, step_row = wide_sums[...].T, wide_step[...].T
    tail_out[...] = jnp.broadcast_to(wide_sums[tokens - 1 :, :], tail_out.shape)

    kinds = lax.broadcasted_iota(jnp.int32, (tokens, EXPERTS), 1)
    named = [(route[:, k : k + 1] == kinds.astype(jnp.float32)).astype(jnp.float32) for k in range(2)]
    before = jnp.dot(
        (row_index > column_index).astype(jnp.bfloat16),
        (named[0] + named[1]).astype(jnp.bfloat16),
        preferred_element_type=jnp.float32,
    )
    relative = kinds ^ ctx
    start = (relative // near * group).astype(jnp.float32)
    inner = (relative % near).astype(jnp.float32)
    spots = start + jnp.where(
        before < main, inner * main + before, near * main + inner * extra + before - main
    )
    targets = [jnp.sum(named[k] * spots, axis=1, keepdims=True) for k in range(2)]
    slot_row = lax.broadcasted_iota(jnp.int32, picker.shape, 0).astype(jnp.float32)
    slot_column = lax.broadcasted_iota(jnp.int32, weights_high.shape, 1).astype(jnp.float32)
    picked_rows = [as_row(target)[:1] for target in targets]
    picker[...] = (
        jnp.where(slot_row == picked_rows[0], 1.0, 0.0) + jnp.where(slot_row == picked_rows[1], 1.0, 0.0)
    ).astype(jnp.bfloat16)
    weights = jnp.where(slot_column == targets[0], route[:, 2:3], 0.0)
    weights = weights + jnp.where(slot_column == targets[1], route[:, 3:4], 0.0)
    high = weights.astype(jnp.bfloat16)
    weights_high[...] = high
    weights_low[...] = (weights - high.astype(jnp.float32)).astype(jnp.bfloat16)

    pl.semaphore_wait(barrier, peers - 1 + 3 + jnp.where(z == beside, line - 1, 0))

    def edge_copies():
        device = {"ctx": (ctx + 1) % peers}
        return (
            remote(
                mixer_input.at[pl.ds(tokens - SUB, SUB), :], edge_in, edge_send.at[0], edge_receive.at[0], device
            ),
            remote(edge_state, edge_state_in, edge_send.at[1], edge_receive.at[1], device),
        )

    @pl.when(ctx < peers - 1)
    def _():
        for copy in edge_copies():
            copy.start()

    for n in range(2):
        weight_across(n).start()

    @pl.when(ctx > 0)
    def _():
        for copy in edge_copies():
            copy.wait_recv()
        total[:8, :] = edge_in[...].astype(jnp.float32)[8:]
        states_long[:8, :] = edge_state_in[...].astype(jnp.float32)[8:, : 2 * states]

    @pl.when(ctx == 0)
    def _():
        total[:8, :] = jnp.zeros((8, width), jnp.float32)
        states_long[:8, :] = jnp.zeros((8, 2 * states), jnp.float32)

    taps = conv_weight.shape[0]
    base = 8 - (taps - 1)
    filtered = jnp.zeros((tokens, 2 * states), jnp.float32)
    for tap in range(taps):
        filtered = filtered + conv_state_weight[tap : tap + 1, :] * states_long[base + tap : base + tap + tokens, :]
    wide_state[:, : 2 * states] = jax.nn.silu(filtered)
    state_rows = wide_state[...].T
    writer_rows = state_rows[:states]
    ending = jnp.exp(wide_sums[tokens - 1 :, :] - wide_sums[...]) * wide_step[...]
    left = lax.broadcasted_iota(jnp.int32, (tokens, lanes), 1) < lanes // 2

    def widened(narrow, i):
        return jnp.where(left, narrow[:, 2 * i : 2 * i + 1], narrow[:, 2 * i + 1 : 2 * i + 2])

    for i in range(slabs):
        slab_of = slice(i * lanes, (i + 1) * lanes)
        value = jnp.zeros((tokens, lanes), jnp.float32)
        for tap in range(taps):
            value = value + conv_weight[tap : tap + 1, slab_of] * total[base + tap : base + tap + tokens, slab_of]
        value = jax.nn.silu(value)
        values[:, slab_of] = value
        state_out[:, slab_of] = jnp.dot(
            writer_rows, widened(ending, i) * value, precision=exact, preferred_element_type=jnp.float32
        ).astype(jnp.bfloat16)

    def state_copies(distance):
        device = {"ctx": (ctx + distance) % peers}
        return (
            remote(
                state_out, state_in.at[distance], state_send.at[0, distance], state_receive.at[0, distance], device
            ),
            remote(
                tail_out, tail_in.at[distance], state_send.at[1, distance], state_receive.at[1, distance], device
            ),
        )

    for distance in range(peers - 1, 0, -1):

        @pl.when(ctx + distance < peers)
        def _():
            for copy in state_copies(distance):
                copy.start()

    for n in range(2, pieces):
        weight_across(n).start()
    scores = jnp.dot(
        wide_state[:, states : 2 * states], writer_rows, precision=exact, preferred_element_type=jnp.float32
    )
    for i in range(slabs):
        slab_of = slice(i * lanes, (i + 1) * lanes)
        factors = []
        for head in (2 * i, 2 * i + 1):
            spans = wide_sums[:, head : head + 1] - sums_row[head : head + 1, :]
            factors.append(
                jnp.exp(jnp.where(causal, spans, -1e30)) * (step_row[head : head + 1, :] * scores)
            )
        value = values[:, slab_of]
        halves = jnp.concatenate([jnp.where(left, value, 0.0), jnp.where(left, 0.0, value)], axis=0)
        inside = jnp.dot(
            jnp.concatenate(factors, axis=1).astype(jnp.bfloat16),
            halves.astype(jnp.bfloat16),
            preferred_element_type=jnp.float32,
        )
        total[:tokens, slab_of] = inside + widened(skip_gain, i) * value

    for distance in range(1, peers):

        @pl.when(ctx - distance >= 0)
        def _():
            for copy in state_copies(distance):
                copy.wait_recv()

    logs[...] = jnp.zeros_like(logs)
    running = jnp.zeros((1, tokens), jnp.float32)
    for distance in range(1, peers):
        logs[distance - 1 : distance, :] = running
        running = running + tail_in[distance][:1]
    spread = (
        lax.broadcasted_iota(jnp.int32, (lanes, width), 1) // (width // heads)
        == lax.broadcasted_iota(jnp.int32, (lanes, width), 0)
    ).astype(jnp.float32)
    carries = jnp.dot(jnp.exp(logs[...]), spread, precision=exact, preferred_element_type=jnp.float32)
    arrived = jnp.zeros((states, width), jnp.float32)
    for distance in range(1, peers):
        arrived = arrived + carries[distance - 1 : distance, :] * state_in[distance].astype(jnp.float32)
    entering_state[:states, :] = jnp.zeros((states, width), jnp.float32)
    entering_state[states:, :] = arrived
    growth = jnp.exp(wide_sums[...])
    squares = jnp.zeros((tokens, lanes), jnp.float32)
    for i in range(slabs):
        slab_of = slice(i * lanes, (i + 1) * lanes)
        carried = jnp.dot(
            wide_state[:, : 2 * states],
            entering_state[:, slab_of],
            precision=exact,
            preferred_element_type=jnp.float32,
        )
        mixed = total[:tokens, slab_of] + carried * widened(growth, i)
        value = mixed * jax.nn.silu(gate_input[:, slab_of].astype(jnp.float32))
        squares = squares + value * value
        held[z // 2, pl.ds(pl.multiple_of(z % 2 * tokens, tokens), tokens), slab_of] = (
            value * mixer_gain[:, slab_of]
        ).astype(jnp.bfloat16)
    stats[0] = as_row(jnp.sum(squares, axis=1, keepdims=True))

    def line_copy(direction, b, h):
        return remote(
            piece_of(b, h),
            piece_of(b, h),
            line_send.at[direction, b, h],
            line_receive.at[b, h],
            {"ctx": (ctx + 2 - 4 * direction + peers) % peers},
        )

    for h in range(2):

        @pl.when(z < line - 1)
        def _():
            line_copy(0, z, h).start()

        @pl.when(z > 0)
        def _():
            line_copy(1, z, h).start()

    for n in range(3):
        stats_copy(0, n).start()

    def give_copy(b):
        return remote(slab(0, b), slab(1, b), merge_send.at[0, b], merge_receive.at[0, b], {"tp": beside})

    def cross_copy(b):
        return remote(slab(2, b), slab(3, b), merge_send.at[1, b], merge_receive.at[1, b], {"tp": across})

    def final_copy(b):
        return remote(
            slab(2, b),
            slab(4, core),
            merge_send.at[1, b],
            final_receive.at[core],
            {"ctx": b * 2 + x, "tp": z},
        )

    def mine(slot):
        return pl.ds(pl.multiple_of(slot * tokens + core * half, half), half)

    def store(kind, b, data):
        held[line // 2 + kind, pl.ds(pl.multiple_of(b * half, half), half), :] = data

    def forward(h):
        def action(b, direction):
            line_copy(direction, b, h).wait_recv()

            @pl.when((z < line - 1) if direction == 0 else (z > 0))
            def _():
                line_copy(direction, b, h).start()

        return action

    def multiply(b, slot):
        block = held[b // 2, pl.ds(pl.multiple_of(b % 2 * tokens, tokens), tokens), :]
        for n in range(4):
            total[slot * tokens : (slot + 1) * tokens, n * CHUNK : (n + 1) * CHUNK] = jnp.dot(
                block, gate_tiles[3, n], preferred_element_type=jnp.float32
            )
        theirs = pl.ds(pl.multiple_of(slot * tokens + (1 - core) * half, half), half)
        store(0, b, total[theirs, :].astype(jnp.bfloat16))
        give_copy(b).start()

    def merge(b, slot):
        give_copy(b).wait_recv()
        joint = total[mine(slot), :] + slab(1, b)[...].astype(jnp.float32)

        @pl.when(side != z // 2)
        def _():
            store(2, b, joint.astype(jnp.bfloat16))
            cross_copy(b).start()

        @pl.when(side == z // 2)
        def _():
            kept[b] = joint

    def deliver(b, slot):
        @pl.when(side == z // 2)
        def _():
            cross_copy(b).wait_recv()
            joint = (kept[b] + slab(3, b)[...].astype(jnp.float32)).astype(jnp.bfloat16)
            stays = jnp.logical_and(b == z, tp == z)

            @pl.when(stays)
            def _():
                store(4, core, joint)

            @pl.when(jnp.logical_not(stays))
            def _():
                store(2, b, joint)
                final_copy(b).start()

    def each(step, action):
        if step == 0:
            action(z, 0)
            return

        @pl.when(z - step >= 0)
        def _():
            action(z - step, 0)

        @pl.when(z + step < line)
        def _():
            action(z + step, 1)

    def gather(step):
        for h in range(2):
            each(step, forward(h))

    gather(1)
    for n in range(2):
        weight_copy(n).wait()
    for n in range(pieces):
        weight_across(n).wait_recv()
    each(0, multiply)
    each(0, merge)
    for step in range(1, line):
        if step == 1:
            for ahead in range(2, line - 1):
                gather(ahead)
        elif step == line - 1:
            gather(step)
        each(step, multiply)
        each(step, merge)
        each(step - 1, deliver)
    each(line - 1, deliver)

    scale = stats_total(0)
    for h in range(2):

        @pl.when(jnp.logical_not(jnp.logical_and(z == tp, core == h)))
        def _():
            remote(
                slab(4, h), slab(4, h), merge_send.at[1, 0], final_receive.at[h], {"tp": beside}
            ).wait_recv()

    mixer_out = held[line // 2 + 4, :tokens, :].astype(jnp.float32) * scale
    hidden[...] = (residual[...].astype(jnp.float32) + mixer_out).astype(jnp.bfloat16)
    state = hidden[...].astype(jnp.float32)
    stats[1] = as_row(jnp.sum(state * state, axis=1, keepdims=True))
    for n in range(3):
        stats_copy(1, n).start()
    feed_scale = stats_total(1)
    expert_input[...] = (state * feed_scale * feed_gain[...]).astype(jnp.bfloat16)

    def pack(g, block):
        packed[g * near * main : (g + 1) * near * main, :] = block[: near * main].astype(jnp.bfloat16)
        tail = block[near * main :].astype(jnp.bfloat16)
        folded = jnp.zeros((near * SUB, piece), jnp.float32)
        for part in range(fold):
            folded = folded + jnp.dot(
                refold(near, extra, fold, part),
                tail[:, part * piece : (part + 1) * piece],
                preferred_element_type=jnp.float32,
            )
        packed_extra[g * near * SUB : (g + 1) * near * SUB, :] = folded.astype(jnp.bfloat16)

    def unpack(g, target, landed):
        block = landed[g * near * SUB : (g + 1) * near * SUB, :]
        for part in range(fold):
            target[g * group + near * main : (g + 1) * group, part * piece : (part + 1) * piece] = jnp.dot(
                unfold(near, extra, fold, part), block, preferred_element_type=jnp.float32
            ).astype(jnp.bfloat16)

    def partner(r):
        high = (ctx // 4 + r // 4) % 2
        middle = (ctx // 2 % 2 + r // 2 % 2) % 2
        return {"ctx": 4 * high + 2 * middle + (ctx % 2 + r % 2) % 2}

    def travel(g, target, target_extra, kind):
        copies = []
        for r in range(max(1, g * near), (g + 1) * near):
            spot = pl.ds(g * group + r % near * main, main)
            tile_rows = pl.ds(r * SUB, SUB)
            copies.append(
                remote(
                    packed.at[pl.ds(r * main, main)],
                    target.at[spot],
                    home_send.at[kind, r],
                    home_receive.at[kind, r],
                    partner(r),
                )
            )
            copies.append(
                remote(
                    packed_extra.at[tile_rows],
                    target_extra.at[tile_rows],
                    home_send.at[kind + 1, r],
                    home_receive.at[kind + 1, r],
                    partner(r),
                )
            )
        return copies

    for g in range(2):
        pack(
            g,
            jnp.dot(
                picker[g * group : (g + 1) * group, :], expert_input[...], preferred_element_type=jnp.float32
            ),
        )
        for copy in travel(g, rows, rows_extra, 0):
            copy.start()
    rows[:main] = packed[:main]
    rows_extra[:SUB] = packed_extra[:SUB]
    for kind in range(2):
        for n in range(3):
            stats_copy(kind, n).wait_send()
    for n in range(pieces):
        weight_across(n).wait_send()

    @pl.when(ctx < peers - 1)
    def _():
        for copy in edge_copies():
            copy.wait_send()

    for distance in range(1, peers):

        @pl.when(ctx + distance < peers)
        def _():
            for copy in state_copies(distance):
                copy.wait_send()

    for b in range(line):

        @pl.when(jnp.logical_and(z < line - 1, b <= z))
        def _():
            for h in range(2):
                line_copy(0, b, h).wait_send()

        @pl.when(jnp.logical_and(z > 0, b >= z))
        def _():
            for h in range(2):
                line_copy(1, b, h).wait_send()

        give_copy(b).wait_send()

        @pl.when(side != z // 2)
        def _():
            cross_copy(b).wait_send()

        @pl.when(
            jnp.logical_and(side == z // 2, jnp.logical_not(jnp.logical_and(z == b, tp == z)))
        )
        def _():
            final_copy(b).wait_send()

    start_group([(0, 3), (2, 3)])

    def pair(g, kind, j, source, target, other):
        return remote(source, target, pair_send.at[g, kind, j], pair_receive.at[g, kind, j], {"tp": other})

    both = (gate_tiles, up_tiles)

    def product(g, which, place, j, fresh):
        if fresh:
            tile(which, place, j).wait()
        return jnp.dot(
            rows[g * group : (g + 1) * group, :], both[which][place, j], preferred_element_type=jnp.float32
        )

    def first_copy(g, which, j):
        return pair(g, which, j, first.at[g, which, j], first_in.at[g, which, j], beside)

    def far_copy(g, which, j):
        return pair(g, 2 + which, j, far.at[g, which, j], far_in.at[g, which, j], across)

    def near_copy(g, which, j):
        return pair(g, 4 + which, j, first.at[g, which, j], near_in.at[g, which, j], beside)

    def beside_copy(g, j):
        return pair(g, 6, j, active.at[g, j], active_beside.at[g, j], beside)

    def across_copy(g, j):
        return pair(g, 7, j, active.at[g, j], active_across.at[g, j], across)

    def diagonal_copy(g, j):
        return pair(g, 8, j, active_across.at[g, j], active_diagonal.at[g, j], beside)

    def loop(step):
        def run(j, carry):
            step(j)
            return carry

        lax.fori_loop(0, chunks, run, 0)

    def receive_rows(g):
        for copy in travel(g, rows, rows_extra, 0):
            copy.wait_recv()
        unpack(g, rows, rows_extra)

    def far_step(g, fresh, j):
        for which in range(2):
            first[g, which, j] = product(g, which, 0, j, fresh).astype(jnp.bfloat16)
            first_copy(g, which, j).start()
        for which in range(2):
            mine = product(g, which, 1, j, fresh)
            first_copy(g, which, j).wait_recv()
            far[g, which, j] = (mine + first_in[g, which, j].astype(jnp.float32)).astype(jnp.bfloat16)
            far_copy(g, which, j).start()

    def near_step(g, fresh, j):
        for which in range(2):
            mine = product(g, which, 2, j, fresh).astype(jnp.bfloat16)
            first_copy(g, which, j).wait_send()
            first[g, which, j] = mine
            near_copy(g, which, j).start()

    def lowered(g, source, place, j, fresh):
        if fresh:
            tile(2, place, j).wait()
        total[g * group : (g + 1) * group, :] += jnp.dot(
            source[g, j], down_tiles[place, j], preferred_element_type=jnp.float32
        )

    def active_step(g, fresh, j):
        sums = []
        for which in range(2):
            mine = product(g, which, 3, j, fresh).astype(jnp.bfloat16).astype(jnp.float32)
            near_copy(g, which, j).wait_recv()
            mine = mine + near_in[g, which, j].astype(jnp.float32)
            far_copy(g, which, j).wait_recv()
            sums.append(mine + far_in[g, which, j].astype(jnp.float32))
        active[g, j] = (jax.nn.silu(sums[0]) * sums[1]).astype(jnp.bfloat16)
        across_copy(g, j).start()
        beside_copy(g, j).start()

    def lower_step(g, fresh, j):
        lowered(g, active, 0, j, fresh)
        beside_copy(g, j).wait_recv()
        lowered(g, active_beside, 1, j, fresh)

    def across_step(g, fresh, j):
        across_copy(g, j).wait_recv()
        diagonal_copy(g, j).start()
        lowered(g, active_across, 2, j, fresh)

    def diagonal_step(g, fresh, j):
        diagonal_copy(g, j).wait_recv()
        lowered(g, active_diagonal, 3, j, fresh)

    def last_steps(g, fresh):
        across_step(g, fresh, 0)

        def run(j, carry):
            across_step(g, fresh, j)
            diagonal_step(g, fresh, j - 1)
            return carry

        lax.fori_loop(1, chunks, run, 0)
        diagonal_step(g, fresh, chunks - 1)

    def send_home(g):
        pack(g, total[g * group : (g + 1) * group, :])
        for copy in travel(g, answers, answers_extra, 2):
            copy.start()

    receive_rows(0)
    loop(functools.partial(far_step, 0, True))
    receive_rows(1)
    loop(functools.partial(far_step, 1, False))
    total[...] = jnp.zeros_like(total)
    loop(functools.partial(near_step, 0, True))
    loop(functools.partial(near_step, 1, False))

    def far_group(j):
        active_step(1, True, j)
        lower_step(1, True, j)

    loop(far_group)
    loop(functools.partial(active_step, 0, False))
    for g in range(2):
        for copy in travel(g, rows, rows_extra, 0):
            copy.wait_send()
    last_steps(1, True)
    send_home(1)
    loop(functools.partial(lower_step, 0, False))
    last_steps(0, False)
    send_home(0)
    answers[:main] = packed[:main]
    answers_extra[:SUB] = packed_extra[:SUB]

    def drain(j):
        for g in range(2):
            for which in range(2):
                far_copy(g, which, j).wait_send()
                near_copy(g, which, j).wait_send()
            beside_copy(g, j).wait_send()
            across_copy(g, j).wait_send()
            diagonal_copy(g, j).wait_send()

    loop(drain)
    for g in (1, 0):
        for copy in travel(g, answers, answers_extra, 2):
            copy.wait_recv()
        unpack(g, answers, answers_extra)
    routed = jnp.dot(weights_high[...], answers[...], preferred_element_type=jnp.float32)
    routed = routed + jnp.dot(weights_low[...], answers[...], preferred_element_type=jnp.float32)
    out[...] = (hidden[...].astype(jnp.float32) + routed).astype(jnp.bfloat16)
    for g in range(2):
        for copy in travel(g, answers, answers_extra, 2):
            copy.wait_send()


def block_direct(
    residual,
    mixer_input,
    gate_input,
    state_proj,
    step_raw,
    conv_weight,
    conv_state_weight,
    step_bias,
    decay_log,
    skip_gain,
    mixer_gain,
    out_weight,
    feed_gain,
    gate,
    up,
    down,
    expert_ids,
    expert_weights,
):
    peers = lax.axis_size("ctx")
    tokens, width = residual.shape
    states = state_proj.shape[1] // 2
    chunks = gate.shape[2] // 4 // CHUNK
    extra = CAP - CAP // SUB * SUB
    main = CAP - extra
    count = peers * CAP
    vmem = pl.BlockSpec(memory_space=pltpu.VMEM)
    anywhere = pl.BlockSpec(memory_space=pl.ANY)
    block = (chunks, count // 2, CHUNK)
    low = jnp.bfloat16
    return pl.pallas_call(
        functools.partial(block_kernel, peers),
        out_shape=jax.ShapeDtypeStruct((tokens, width), low),
        in_specs=[vmem] * 14 + [anywhere] * 4,
        out_specs=vmem,
        scratch_shapes=[
            pltpu.VMEM((tokens, width), low),
            pltpu.VMEM((tokens, width), low),
            pltpu.VMEM((2, 8, tokens), jnp.float32),
            pltpu.VMEM((2, 3, 8, tokens), jnp.float32),
            pltpu.VMEM((count, tokens), low),
            pltpu.VMEM((tokens, count), low),
            pltpu.VMEM((tokens, count), low),
            pltpu.VMEM((SUB, width), low),
            pltpu.VMEM((SUB, tokens), low),
            pltpu.VMEM((SUB, tokens), low),
            pltpu.VMEM((8 + tokens, 2 * states), jnp.float32),
            pltpu.VMEM((tokens, tokens), jnp.float32),
            pltpu.VMEM((tokens, tokens), jnp.float32),
            pltpu.VMEM((tokens, tokens), jnp.float32),
            pltpu.VMEM((states, width), low),
            pltpu.VMEM((peers, states, width), low),
            pltpu.VMEM((8, tokens), jnp.float32),
            pltpu.VMEM((peers, 8, tokens), jnp.float32),
            pltpu.VMEM((2 * states, width), jnp.float32),
            pltpu.VMEM((8, tokens), jnp.float32),
            pltpu.VMEM((peers // 2, tokens // 2, width), jnp.float32),
            pltpu.VMEM((4, chunks, width, CHUNK), low),
            pltpu.VMEM((4, chunks, width, CHUNK), low),
            pltpu.VMEM((4, chunks, CHUNK, width), low),
            pltpu.VMEM((peers * main, width), low),
            pltpu.VMEM((peers * SUB, width * extra // SUB), low),
            pltpu.VMEM((count, width), low),
            pltpu.VMEM((peers * SUB, width * extra // SUB), low),
            pltpu.VMEM((count, width), low),
            pltpu.VMEM((peers * SUB, width * extra // SUB), low),
            pltpu.VMEM((2, 2) + block, low),
            pltpu.VMEM((2, 2) + block, low),
            pltpu.VMEM((2, 2) + block, low),
            pltpu.VMEM((2, 2) + block, low),
            pltpu.VMEM((2, 2) + block, low),
            pltpu.VMEM((2,) + block, low),
            pltpu.VMEM((2,) + block, low),
            pltpu.VMEM((2,) + block, low),
            pltpu.VMEM((2,) + block, low),
            pltpu.VMEM((count, width), jnp.float32),
            pltpu.SemaphoreType.DMA((12, chunks)),
            pltpu.SemaphoreType.DMA((2,)),
            pltpu.SemaphoreType.DMA((2 * width // CHUNK,)),
            pltpu.SemaphoreType.DMA((2 * width // CHUNK,)),
            pltpu.SemaphoreType.DMA((2,)),
            pltpu.SemaphoreType.DMA((2,)),
            pltpu.SemaphoreType.DMA((2, peers)),
            pltpu.SemaphoreType.DMA((2, peers)),
            pltpu.SemaphoreType.DMA((2, peers // 2, 2)),
            pltpu.SemaphoreType.DMA((peers // 2, 2)),
            pltpu.SemaphoreType.DMA((2, peers // 2)),
            pltpu.SemaphoreType.DMA((2, peers // 2)),
            pltpu.SemaphoreType.DMA((2,)),
            pltpu.SemaphoreType.DMA((2, 3)),
            pltpu.SemaphoreType.DMA((2, 3)),
            pltpu.SemaphoreType.DMA((4, peers)),
            pltpu.SemaphoreType.DMA((4, peers)),
            pltpu.SemaphoreType.DMA((2, 9, chunks)),
            pltpu.SemaphoreType.DMA((2, 9, chunks)),
        ],
        compiler_params=pltpu.CompilerParams(
            collective_id=0, has_side_effects=True, vmem_limit_bytes=67_000_000
        ),
        name="block",
    )(
        mixer_input,
        gate_input,
        state_proj.T,
        step_raw.T,
        conv_weight,
        conv_state_weight,
        step_bias[None, :],
        decay_log[None, :],
        skip_gain[None, :],
        mixer_gain[None, :],
        residual,
        feed_gain[None, :],
        expert_ids.T,
        expert_weights.T,
        out_weight,
        gate,
        up,
        down,
    )


def body(
    residual,
    mixer_input,
    gate_input,
    state_proj,
    step_raw,
    conv_weight,
    conv_state_weight,
    step_bias,
    decay_log,
    skip_gain,
    mixer_gain,
    out_weight,
    feed_gain,
    expert_gate,
    expert_up,
    expert_down,
    expert_ids,
    expert_weights,
):
    tensor_count = lax.axis_size("tp")
    context_count = lax.axis_size("ctx")
    tokens = mixer_input.shape[0]
    channels = mixer_input.shape[1]
    states = state_proj.shape[1] // 2
    heads_local = step_raw.shape[1]
    head_size = channels // heads_local
    taps = conv_weight.shape[0]
    direct = context_count == EXPERTS
    joined = jnp.concatenate([mixer_input, state_proj], axis=1)
    previous = passed_along(joined[tokens - (taps - 1) :], "ctx", 1)
    kernel = jnp.concatenate([conv_weight, conv_state_weight], axis=1)
    filtered = causal_filter(previous.astype(jnp.float32), joined.astype(jnp.float32), kernel)
    values = filtered[:, :channels].reshape(tokens, heads_local, head_size)
    writer = filtered[:, channels : channels + states]
    reader = filtered[:, channels + states :]
    step_size = jax.nn.softplus(step_raw + step_bias[None, :])
    log_decay = -step_size * jnp.exp(decay_log)[None, :]
    inside, cumulative, fresh, tail = local_terms(values, writer, reader, step_size, log_decay)

    incoming = entering(jnp.repeat(jnp.exp(tail), head_size), fresh, "ctx")
    carried = (
        jnp.dot(reader, incoming, precision=lax.Precision.HIGHEST).reshape(values.shape)
        * jnp.exp(cumulative)[:, :, None]
    )
    mixed = inside + carried + skip_gain[None, :, None] * values
    gated = mixed.reshape(tokens, channels) * jax.nn.silu(gate_input.astype(jnp.float32))
    tp_index = lax.axis_index("tp")
    core, chip = (tp_index % 2, tp_index // 2)
    scaled = (gated * mixer_gain[None, :]).astype(jnp.bfloat16)
    ctx_index = lax.axis_index("ctx")
    if direct:
        pairs = []
        for plane in range(4):
            block = rotated(scaled, 2 * plane) if plane else scaled
            other = lax.ppermute(block, "ctx", [(c, c ^ 1) for c in range(context_count)])
            pair = jnp.concatenate([block, other], axis=0)
            pairs.append(jnp.dot(pair, out_weight, preferred_element_type=jnp.float32))
        products = jnp.stack(pairs)

        def projected(quarter):
            place = (ctx_index // 2 - quarter) % 4
            return lax.dynamic_index_in_dim(products, place, 0, keepdims=False)

    else:
        everyone = lax.all_gather(scaled, "ctx", axis=0, tiled=True)
        span = everyone.shape[0] // tensor_count

        def projected(quarter):
            rows = lax.dynamic_slice_in_dim(everyone, quarter * span, span, 0)
            return jnp.dot(rows, out_weight, preferred_element_type=jnp.float32)

    square_sum = tensor_total(jnp.sum(gated * gated, axis=1))
    scale = lax.rsqrt(square_sum / (channels * tensor_count) + EPSILON)
    own, beside = (chip * 2 + core, chip * 2 + 1 - core)
    across, diagonal = ((1 - chip) * 2 + core, (1 - chip) * 2 + 1 - core)
    far = swapped(projected(diagonal).astype(jnp.bfloat16), 1)
    far = swapped((projected(across) + far.astype(jnp.float32)).astype(jnp.bfloat16), 2)
    near = swapped(projected(beside).astype(jnp.bfloat16), 1)
    reduced = projected(own) + near.astype(jnp.float32) + far.astype(jnp.float32)
    blocks = context_count // tensor_count
    reduced = reduced.astype(jnp.bfloat16).reshape(blocks, tokens, -1)
    pieces = []
    for j in range(blocks):
        moves = [
            (c * tensor_count + p, (p * blocks + (c + j) % blocks) * tensor_count + c // blocks)
            for c in range(context_count)
            for p in range(tensor_count)
        ]
        if direct:
            block = reduced[j]
        else:
            block = lax.dynamic_index_in_dim(reduced, (ctx_index + j) % blocks, 0, keepdims=False)
        pieces.append(lax.ppermute(block, ("ctx", "tp"), moves))
    stacked = jnp.stack(pieces)
    order = (ctx_index - jnp.arange(blocks)) % blocks
    if blocks == 2:
        first = ctx_index % 2 == 0
        mixer_out = jnp.concatenate(
            [jnp.where(first, pieces[0], pieces[1]), jnp.where(first, pieces[1], pieces[0])], axis=1
        )
    else:
        mixer_out = jnp.take(stacked, order, axis=0).transpose(1, 0, 2).reshape(tokens, -1)
    mixer_out = mixer_out.astype(jnp.float32) * scale[:, None]
    hidden_state = (residual.astype(jnp.float32) + mixer_out).astype(jnp.bfloat16)
    state_float = lax.optimization_barrier(hidden_state).astype(jnp.float32)
    width_total = hidden_state.shape[1] * tensor_count
    feed_sum = tensor_total(jnp.sum(state_float * state_float, axis=1))
    feed_scale = lax.rsqrt(feed_sum / width_total + EPSILON)
    expert_input = (state_float * feed_scale[:, None] * feed_gain[None, :]).astype(jnp.bfloat16)
    group = context_count // EXPERTS
    width_local = expert_input.shape[1]
    flat_experts = expert_ids.reshape(-1)
    matches = (flat_experts[:, None] == jnp.arange(EXPERTS)[None, :]).astype(jnp.int32)
    slots = jnp.sum((jnp.cumsum(matches, axis=0) - matches) * matches, axis=1)
    places = (flat_experts - ctx_index) % EXPERTS if direct else flat_experts
    targets = (places * CAP + slots).reshape(tokens, -1)
    picker = jnp.any(targets[None, :, :] == jnp.arange(EXPERTS * CAP)[:, None, None], axis=2)
    buffer = jnp.dot(
        picker.astype(jnp.bfloat16), expert_input, preferred_element_type=jnp.float32
    ).astype(jnp.bfloat16)
    outgoing = jnp.broadcast_to(
        buffer.reshape(EXPERTS, 1, CAP, width_local), (EXPERTS, group, CAP, width_local)
    )
    outgoing = outgoing.reshape(EXPERTS * group, CAP, width_local)
    gate_local = expert_gate[0]
    up_local = expert_up[0]
    down_local = expert_down[0]
    sources, items, depth = outgoing.shape
    if direct:
        flattened = jnp.concatenate(
            [outgoing[r] if r == 0 else rotated(outgoing[r], r) for r in range(sources)], axis=0
        )
    else:
        arrived = lax.all_to_all(outgoing, "ctx", split_axis=0, concat_axis=0, tiled=True)
        flattened = arrived.reshape(sources * items, depth)
    hidden = gate_local.shape[1] // tensor_count

    def product(source, weight, quarter):
        columns = lax.dynamic_slice_in_dim(weight, quarter * hidden, hidden, 1)
        return jnp.dot(source, columns, preferred_element_type=jnp.float32)

    fars, nears, rows = ([], [], flattened)
    for weight in (gate_local, up_local):
        far = product(rows, weight, diagonal).astype(jnp.bfloat16)
        far = swapped(far, 1)
        nears.append(swapped(product(rows, weight, beside).astype(jnp.bfloat16), 1))
        far = (product(rows, weight, across) + far.astype(jnp.float32)).astype(jnp.bfloat16)
        far, rows = lax.optimization_barrier((far, rows))
        fars.append(swapped(far, 2))
    gate_share, up_share = (
        product(rows, weight, own).astype(jnp.bfloat16).astype(jnp.float32)
        + near.astype(jnp.float32)
        + far.astype(jnp.float32)
        for weight, near, far in zip((gate_local, up_local), nears, fars)
    )
    share = (jax.nn.silu(gate_share) * up_share).astype(jnp.bfloat16)
    share_across = swapped(share, 2)
    share_beside = swapped(share, 1)

    def lowered(part, quarter):
        rows = lax.dynamic_slice_in_dim(down_local, quarter * hidden, hidden, 0)
        return jnp.dot(part, rows, preferred_element_type=jnp.float32)

    local = lowered(share, own) + lowered(share_beside, beside)
    local, share_across = lax.optimization_barrier((local, share_across))
    share_diagonal = swapped(share_across, 1)
    answer = (
        local
        + lowered(share_across, across)
        + lowered(share_diagonal, diagonal)
    ).astype(jnp.bfloat16)
    answer = answer.reshape(sources, items, depth)
    if direct:
        answers = jnp.stack(
            [answer[r] if r == 0 else rotated(answer[r], -r) for r in range(sources)]
        )
    else:
        answers = lax.all_to_all(answer, "ctx", split_axis=0, concat_axis=0, tiled=True)
    summed = jnp.sum(answers.reshape(EXPERTS, group, CAP, width_local), axis=1, dtype=jnp.float32)
    summed = summed.reshape(EXPERTS * CAP, width_local)
    chosen = jnp.take(summed, targets, axis=0)
    routed = jnp.sum(expert_weights[:, :, None] * chosen, axis=1)
    return (state_float + routed).astype(jnp.bfloat16)


def solution(mesh):
    placed = (
        P("ctx", "tp"),
        P("ctx", "tp"),
        P("ctx", "tp"),
        P("ctx", None),
        P("ctx", "tp"),
        P(None, "tp"),
        P(),
        P("tp"),
        P("tp"),
        P("tp"),
        P("tp"),
        P("tp", "ctx"),
        P("tp"),
        P("ctx", "tp", None),
        P("ctx", "tp", None),
        P("ctx", None, "tp"),
        P("ctx", None),
        P("ctx", None),
    )

    direct = mesh.shape["ctx"] == EXPERTS and mesh.shape["tp"] == 4

    def layer(*args):
        return (block_direct if direct else body)(*args)

    return jax.shard_map(
        layer, mesh=mesh, in_specs=placed, out_specs=P("ctx", "tp"), check_vma=False
    )
```
